256 devices in a mesh: dp: 32 (over y, x, z_hi), tensor: 8 (over z_lo, core).
Axes of the slice: x: 4, y: 4, z: 8 (z_hi: 2, z_lo: 4; z = z_hi * 4 + z_lo), core: 2. Of those that a mesh axis runs over, the one named last changes fastest.
Arguments:
- leaf_tokens: bfloat16 [512, 8, 2048], P(('dp', 'tensor')), may hold values from -40 to 40
- attn_gain: float32 [2048], replicated, may hold values from 0.25 to 2.5
- w_query: bfloat16 [2048, 2048], P(None, 'tensor'), may hold values from -0.125 to 0.125
- w_key: bfloat16 [2048, 2048], P(None, 'tensor'), may hold values from -0.125 to 0.125
- w_value: bfloat16 [2048, 2048], P(None, 'tensor'), may hold values from -0.125 to 0.125
- w_out: bfloat16 [2048, 2048], P('tensor'), may hold values from -0.125 to 0.125
- prefix_kv: bfloat16 [2, 28672, 2048], P(None, 'dp', 'tensor'), may hold values from -104 to 104
- prefix_owner: int32 [512, 3], P('dp'), may hold values from 0 to 31, as said below
- prefix_start: int32 [512, 3], P('dp'), may hold values from 0 to 864, as said below
- prefix_len: int32 [512, 3], P('dp'), may hold values from 1 to 512, as said below
- mlp_gain: float32 [2048], replicated, may hold values from 0.25 to 2.5
- shared_in: bfloat16 [2048, 2, 1408], P(None, None, 'tensor'), may hold values from -0.125 to 0.125
- shared_out: bfloat16 [1408, 2048], P('tensor'), may hold values from -0.15625 to 0.15625
- expert_in: bfloat16 [64, 2048, 2, 1408], P('dp', None, None, 'tensor'), may hold values from -0.125 to 0.125
- expert_out: bfloat16 [64, 1408, 2048], P('dp', 'tensor'), may hold values from -0.15625 to 0.15625
- expert_ids: int32 [512, 8, 6], P('dp'), may hold values from 0 to 63, all different within a row; in each aligned block of 128 rows (0 to 127, 128 to 255, ..., all dimensions but the last counted through in order) at most 16 rows name the same one
- gate_weights: float32 [512, 8, 6], P('dp'), may hold values from 0.05 to 0.4
- request_of: int32 [512], P('dp'), may hold values from 0 to 511, as said below
Outputs:
- layer_out: bfloat16 [512, 8, 2048], P('dp', 'tensor')
The draws below stay inside these ranges and needn't reach their ends.
Inputs may be any that keep to these rules, and one draw needn't show every extreme that they name: `prefix_owner`: each data group owns exactly one first-level node, two second-level nodes and four third-level nodes; a first-level node serves 16 requests, a second-level node half as many, a third-level node a quarter. The 16 requests of one data group name 16 different owners at each level, and together over the three levels they name no owner more than twice. `prefix_start`: the first level starts at 0; the second at 512 or 640; the third at 768 + q * 32 with q from 0 to 3. `prefix_len`: A node has 1 to 512, 128 or 32 keys at the first, second or third level, each of these maxima reached. Requests naming the same owner and start at a level share that node and its length; each node lies under one node of the level above. `expert_ids`: each row names 6 different experts; in the rows of one data group (aligned blocks of 128 rows) no expert is named more than 16 times. `request_of`: A permutation; the 16 dealt requests of one data group go to 16 different data groups.
All inputs are finite; a program needn't handle non-finite values.
Results may differ from the reference program's by a relative error of at most 0.025.
Values may be sent and summed in bfloat16 or wider, within the bound.
A program may use at most 128 MiB of HBM per device.

```python
import math
import jax
import jax.numpy as jnp
import numpy as np
from jax import lax

D = 2048
HEADS = 16
HEAD_DIM = 128
EXPERTS = 64
TOPK = 6
FF = 1408
SHARED = 1
LEAF_LEN = 8
MAX3 = 32
MAX2 = 128
MAX1 = 512
POOL_DEV = 896
POOL = 28672
R_DEV = 16
REQS = 512
CAP_E = 16
N_DP = 32
N_TENSOR = 8


def draw_leaf_tokens(key, part):
    noise_key, row_key, column_key = jax.random.split(jax.random.fold_in(key, 3), 3)
    full_shape = (REQS, LEAF_LEN, D)
    column_scale = jnp.exp(jax.random.uniform(column_key, (1, 1, D), jnp.float32, -1.15, 1.15))
    noise_rows = jax.random.truncated_normal(noise_key, -4.0, 4.0, full_shape, jnp.float32)
    row_scale = jnp.exp(jax.random.uniform(row_key, (REQS, LEAF_LEN, 1), jnp.float32, -1.15, 1.15))
    return (noise_rows * row_scale * column_scale).astype(jnp.bfloat16)


def draw_prefix_kv(key, part):
    key_noise, value_noise = jax.random.split(jax.random.fold_in(key, 5), 2)
    width_all = HEADS * HEAD_DIM
    key_part = jax.random.truncated_normal(key_noise, -4.0, 4.0, (1, POOL, width_all), jnp.float32)
    value_part = 2.0 * jax.random.truncated_normal(value_noise, -4.0, 4.0, (1, POOL, width_all), jnp.float32)
    return jnp.concatenate([key_part, value_part], axis=0).astype(jnp.bfloat16)


def ragged_lengths(one_key, node_count, longest):
    first_key, second_key = jax.random.split(one_key)
    raw_draw = jax.random.randint(first_key, (node_count,), 0, longest)
    lengths = 1 + raw_draw * raw_draw // longest
    forced = jax.random.randint(second_key, (), 0, node_count)
    return lengths.at[forced].set(longest)


def tree_tables(key):
    base_key = jax.random.fold_in(key, 7)
    groups = REQS // R_DEV
    order_key, slots_key, root_key, middle_key, lower_key = jax.random.split(base_key, 5)
    group_order = jax.random.permutation(order_key, groups)
    group_inverse = jnp.argsort(group_order)
    slot_keys = jax.random.split(slots_key, groups)
    local_slot = jax.vmap(lambda one_key: jax.random.permutation(one_key, R_DEV))(slot_keys)
    diagonal = (group_order[:, None] + local_slot) % groups
    half_size = R_DEV // 2
    quarter_size = R_DEV // 4
    half_index = local_slot // half_size
    quarter_index = local_slot // quarter_size
    owner_root = group_inverse[diagonal]
    owner_middle = group_inverse[(diagonal + half_size + half_size * half_index) % groups]
    owner_lower = group_inverse[(diagonal + R_DEV) % groups]
    root_lengths = ragged_lengths(root_key, groups, MAX1)
    middle_lengths = ragged_lengths(middle_key, groups * 2, MAX2).reshape(groups, 2)
    lower_lengths = ragged_lengths(lower_key, groups * 4, MAX3).reshape(groups, 4)
    owners = jnp.stack([owner_root, owner_middle, owner_lower], axis=-1).reshape(REQS, 3)
    starts = jnp.stack([jnp.zeros_like(local_slot), MAX1 + MAX2 * half_index, MAX1 + 2 * MAX2 + MAX3 * quarter_index], axis=-1).reshape(REQS, 3)
    lengths = jnp.stack([root_lengths[diagonal], middle_lengths[diagonal, half_index], lower_lengths[diagonal, quarter_index]], axis=-1).reshape(REQS, 3)
    return (owners.astype(jnp.int32), starts.astype(jnp.int32), lengths.astype(jnp.int32))


def draw_prefix_owner(key, part):
    return tree_tables(key)[0]


def draw_prefix_start(key, part):
    return tree_tables(key)[1]


def draw_prefix_len(key, part):
    return tree_tables(key)[2]


def draw_request_of(key, part):
    base_key = jax.random.fold_in(key, 11)
    groups = REQS // R_DEV
    shift_key, relabel_key, slots_key = jax.random.split(base_key, 3)
    shifts = jax.random.permutation(shift_key, groups)[:R_DEV]
    relabel = jax.random.permutation(relabel_key, groups)
    source_group = jnp.arange(groups)[:, None]
    target = relabel[(source_group + shifts[None, :]) % groups]
    slot_keys = jax.random.split(slots_key, groups)
    arrival = jax.vmap(lambda one_key: jax.random.permutation(one_key, R_DEV))(slot_keys)
    placed = arrival[target, jnp.arange(R_DEV)[None, :]]
    return (target * R_DEV + placed).reshape(REQS).astype(jnp.int32)


def levels(rng, dims, cuts, least, top_value):
    factor_of = 1.0
    for dim, blocks in cuts:
        draws = jax.random.uniform(jax.random.fold_in(jax.random.fold_in(rng, 6), dim), (blocks,), jnp.float32, least / len(cuts), top_value / len(cuts))
        factor_of = factor_of * jnp.repeat(jnp.exp(draws), dims[dim] // blocks).reshape((-1,) + (1,) * (len(dims) - 1 - dim))
    return factor_of


def deal_out(key, own, number, rows, count, top, limit, slope):
    ranking = jax.random.permutation(key, count)
    heavy_load, usual = shares(count, rows * top, limit, slope, True), shares(count, rows * top, limit, slope, False)
    places = jnp.arange(count)

    def named(tallies, turn):
        used = int((tallies > 0).sum())
        fixed = max(1, used // 4)
        moved = fixed + (places - fixed + turn * (used - fixed)) % max(1, count - fixed)
        return jnp.zeros((count,), jnp.int32).at[ranking[jnp.where(places < fixed, places, moved)]].set(jnp.asarray(tallies, jnp.int32))

    tallies = jnp.where(number % 4 == 0, named(heavy_load, number // 4), named(usual, number - number // 4 - 1))
    mixed = jax.random.permutation(jax.random.fold_in(own, 3), count)
    donor, sink = mixed[0:count // 2 * 2:2], mixed[1:count // 2 * 2:2]
    slack = jnp.minimum(tallies[donor] - 1, limit - tallies[sink]) // 2
    slack = jnp.where((donor == ranking[0]) | (sink == ranking[0]) | (tallies[sink] == 0), 0, jnp.maximum(slack, 0))
    moved = jax.random.randint(jax.random.fold_in(own, 4), (count // 2,), 0, 1 << 20) % (slack + 1)
    tallies = tallies.at[donor].add(-moved).at[sink].add(moved)
    labels = jnp.searchsorted(jnp.cumsum(tallies), jnp.arange(rows * top), side="right").astype(jnp.int32)
    listing = labels.reshape(top, rows).T
    listing = listing[jax.random.permutation(jax.random.fold_in(own, 1), rows)]
    turn = jax.random.randint(jax.random.fold_in(own, 2), (rows, 1), 0, top)
    return jnp.take_along_axis(listing, (jnp.arange(top)[None, :] + turn) % top, axis=1)


def shares(amount, total, reach, slope, full):
    weights = [(1 << 20) // math.isqrt(standing ** slope) + 1 for standing in range(1, amount + 1)]
    largest = reach if full else min(reach, max(-(-total // amount), total * weights[0] // sum(weights)))
    least = 1 if total - largest >= amount - 1 else 0
    given, spare = [largest] + [least] * (amount - 1), total - largest - least * (amount - 1)
    while spare > 0:
        movable = [i for i in range(1, amount) if given[i] < largest] or [i for i in range(1, amount) if given[i] < reach]
        whole, remaining = sum([weights[i] for i in movable]), spare
        for i in movable:
            more = min(reach - given[i], max(1, remaining * weights[i] // whole), spare)
            given[i] = given[i] + more
            spare = spare - more
    return np.array(given)


def scatter_about(stream_key, shape, scale, reach, cuts=(), kind=jnp.bfloat16):
    factor_of = levels(stream_key, shape, cuts, -0.22, 0.18) if cuts else 1.0
    entries = jax.random.normal(stream_key, shape, jnp.float32) * scale * factor_of
    return jnp.minimum(jnp.maximum(entries, -reach), reach).astype(kind)


def setup_inputs(seed: int = 0) -> dict:
    splits = jax.random.split(jax.random.key(seed), 19)
    leaf_tokens = draw_leaf_tokens(jax.random.fold_in(splits[18], 71), 0)
    attn_gain = jnp.clip(jnp.exp(jax.random.uniform(splits[1], (D,), jnp.float32, math.log(0.25), math.log(2.5))), 0.25, 2.5)
    w_query = scatter_about(splits[2], (D, HEADS * HEAD_DIM), D ** -0.5, 0.125, ((1, 8),))
    w_key = scatter_about(splits[3], (D, HEADS * HEAD_DIM), D ** -0.5, 0.125, ((1, 8),))
    w_value = scatter_about(splits[4], (D, HEADS * HEAD_DIM), D ** -0.5, 0.125, ((1, 8),))
    w_out = scatter_about(splits[5], (HEADS * HEAD_DIM, D), (HEADS * HEAD_DIM) ** -0.5, 0.125, ((0, 8),))
    prefix_kv = draw_prefix_kv(jax.random.fold_in(splits[18], 71), 0)
    prefix_owner = draw_prefix_owner(jax.random.fold_in(splits[18], 71), 0)
    prefix_start = draw_prefix_start(jax.random.fold_in(splits[18], 71), 0)
    prefix_len = draw_prefix_len(jax.random.fold_in(splits[18], 71), 0)
    mlp_gain = jnp.clip(jnp.exp(jax.random.uniform(splits[10], (D,), jnp.float32, math.log(0.25), math.log(2.5))), 0.25, 2.5)
    shared_in = scatter_about(splits[11], (D, 2, SHARED * FF), D ** -0.5, 0.125, ((2, 8),))
    shared_out = scatter_about(splits[12], (SHARED * FF, D), (SHARED * FF) ** -0.5, 0.15625, ((0, 8),))
    expert_in = scatter_about(splits[13], (EXPERTS, D, 2, FF), D ** -0.5, 0.125, ((0, 32), (3, 8)))
    expert_out = scatter_about(splits[14], (EXPERTS, FF, D), FF ** -0.5, 0.15625, ((0, 32), (1, 8)))
    expert_ids_keys = jax.random.split(jax.random.fold_in(splits[15], 1), REQS * LEAF_LEN // (R_DEV * LEAF_LEN))
    expert_ids_turns = jax.random.permutation(jax.random.fold_in(splits[15], 3), REQS * LEAF_LEN // (R_DEV * LEAF_LEN))
    expert_ids = jax.vmap(lambda own, number: deal_out(jax.random.fold_in(splits[15], 2), own, number, R_DEV * LEAF_LEN, EXPERTS, TOPK, CAP_E, 1))(expert_ids_keys, expert_ids_turns).reshape((REQS, LEAF_LEN, TOPK))
    gate_weights = jnp.clip(0.05 + 0.35 * jax.random.uniform(splits[16], (REQS, LEAF_LEN, TOPK), jnp.float32) ** levels(splits[16], (REQS, LEAF_LEN, TOPK), ((0, 32),), -0.2, 0.2), 0.05, 0.4)
    request_of = draw_request_of(jax.random.fold_in(splits[18], 71), 0)
    return {"leaf_tokens": leaf_tokens, "attn_gain": attn_gain, "w_query": w_query, "w_key": w_key, "w_value": w_value, "w_out": w_out, "prefix_kv": prefix_kv, "prefix_owner": prefix_owner, "prefix_start": prefix_start, "prefix_len": prefix_len, "mlp_gain": mlp_gain, "shared_in": shared_in, "shared_out": shared_out, "expert_in": expert_in, "expert_out": expert_out, "expert_ids": expert_ids, "gate_weights": gate_weights, "request_of": request_of}


EPS = 1e-06
ROPE_BASE = 10000.0

def rms_scaled(values, gain_vector):
    mean_square = lax.optimization_barrier(jnp.mean(values * values, axis=-1, keepdims=True))
    return values * lax.rsqrt(mean_square + EPS) * gain_vector

def rotate_heads(values, positions):
    head_dim = values.shape[-1]
    half_dim = head_dim // 2
    frequency = ROPE_BASE ** (-2.0 * jnp.arange(half_dim, dtype=jnp.float32) / head_dim)
    angles = positions[..., None, None] * frequency
    cosine = jnp.cos(angles)
    sine_part = jnp.sin(angles)
    first_half = values[..., :half_dim]
    second_half = values[..., half_dim:]
    return jnp.concatenate([first_half * cosine - second_half * sine_part, second_half * cosine + first_half * sine_part], axis=-1)

def softmax_parts(scores, visible):
    scores = jnp.where(visible, scores, -jnp.inf)
    highest = lax.optimization_barrier(jnp.max(scores, axis=-1, keepdims=True))
    anchor = jnp.where(jnp.isfinite(highest), highest, 0.0)
    weights = jnp.exp(scores - anchor)
    totals = lax.optimization_barrier(jnp.sum(weights, axis=-1, keepdims=True))
    return (weights, anchor, totals)

def rounded_weights(weights):
    return lax.optimization_barrier(weights.astype(jnp.bfloat16)).astype(jnp.float32)

def merge_parts(outputs, log_totals):
    stacked = jnp.stack(log_totals, axis=0)
    highest = lax.optimization_barrier(jnp.max(stacked, axis=0))
    scales = jnp.exp(stacked - highest)
    weighted = scales[0][..., None] * outputs[0]
    for part_index in range(1, len(outputs)):
        weighted = weighted + scales[part_index][..., None] * outputs[part_index]
    return weighted / lax.optimization_barrier(jnp.sum(scales, axis=0))[..., None]

def reference(leaf_tokens, attn_gain, w_query, w_key, w_value, w_out, prefix_kv, prefix_owner, prefix_start, prefix_len, mlp_gain, shared_in, shared_out, expert_in, expert_out, expert_ids, gate_weights, request_of):
    token_count = REQS * LEAF_LEN
    head_width = HEADS * HEAD_DIM
    score_scale = HEAD_DIM ** (-0.5)
    residual = leaf_tokens.astype(jnp.float32)
    normed_attn = rms_scaled(residual, attn_gain).astype(jnp.bfloat16).reshape(token_count, D)
    positions = lax.optimization_barrier(jnp.sum(prefix_len, axis=1)).astype(jnp.float32)[:, None] + jnp.arange(LEAF_LEN, dtype=jnp.float32)[None, :]

    def project(weight):
        return jnp.dot(normed_attn, weight, preferred_element_type=jnp.float32).reshape(REQS, LEAF_LEN, HEADS, HEAD_DIM)
    queries = rotate_heads(project(w_query), positions).astype(jnp.bfloat16)
    key_rows = rotate_heads(project(w_key), positions).astype(jnp.bfloat16)
    leaf_values = project(w_value).astype(jnp.bfloat16)
    windows = (MAX1, MAX2, MAX3)
    causal = jnp.arange(LEAF_LEN)[:, None] >= jnp.arange(LEAF_LEN)[None, :]

    def attend(request):
        query_rows = queries[request].astype(jnp.float32)
        scores = jnp.einsum('ihd,jhd->hij', query_rows, key_rows[request].astype(jnp.float32)) * score_scale
        weights, anchor, totals = softmax_parts(scores, causal[None])
        mixed_leaf = jnp.einsum('hij,jhd->ihd', rounded_weights(weights), leaf_values[request].astype(jnp.float32))
        outputs = [mixed_leaf / jnp.transpose(totals, (1, 0, 2))]
        log_totals = [jnp.transpose(anchor + jnp.log(totals), (1, 0, 2))[..., 0]]
        zero_index = jnp.zeros((), jnp.int32)
        for tree_level in range(3):
            node_begin = (prefix_owner[request, tree_level] * POOL_DEV + prefix_start[request, tree_level]).astype(jnp.int32)
            node_window = lax.dynamic_slice(prefix_kv, (zero_index, node_begin, zero_index), (2, windows[tree_level], head_width))
            node_window = node_window.astype(jnp.float32).reshape(2, windows[tree_level], HEADS, HEAD_DIM)
            scores = jnp.einsum('ihd,khd->hik', query_rows, node_window[0]) * score_scale
            visible = jnp.arange(windows[tree_level]) < prefix_len[request, tree_level]
            weights, anchor, totals = softmax_parts(scores, visible[None, None, :])
            mixed_level = jnp.einsum('hik,khd->ihd', rounded_weights(weights), node_window[1])
            outputs.append(mixed_level / jnp.transpose(totals, (1, 0, 2)))
            log_totals.append(jnp.transpose(anchor + jnp.log(totals), (1, 0, 2))[..., 0])
        return merge_parts(outputs, log_totals).astype(jnp.bfloat16).reshape(LEAF_LEN, head_width)
    attended = lax.map(attend, jnp.arange(REQS))
    attn_sum = jnp.dot(attended.reshape(token_count, head_width), w_out, preferred_element_type=jnp.float32)
    residual_mid = residual + attn_sum.reshape(REQS, LEAF_LEN, D)
    normed_mlp = rms_scaled(residual_mid, mlp_gain).astype(jnp.bfloat16).reshape(token_count, D)
    shared_width = SHARED * FF
    gate_up = jnp.dot(normed_mlp, shared_in.reshape(D, 2 * shared_width), preferred_element_type=jnp.float32)
    shared_hidden = (jax.nn.silu(gate_up[:, :shared_width]) * gate_up[:, shared_width:]).astype(jnp.bfloat16)
    shared_part = jnp.dot(shared_hidden, shared_out, preferred_element_type=jnp.float32)
    flat_ids = expert_ids.reshape(token_count, TOPK)
    flat_gates = gate_weights.reshape(token_count, TOPK)
    most_rows = N_DP * CAP_E
    slice_width = FF // N_TENSOR

    def add_expert(routed, expert):
        hit_mask = flat_ids == expert
        gate_sum = lax.optimization_barrier(jnp.sum(jnp.where(hit_mask, flat_gates, 0.0), axis=1))
        member = jnp.any(hit_mask, axis=1)
        chosen = jnp.nonzero(member, size=most_rows, fill_value=0)[0]
        present = (jnp.arange(most_rows) < jnp.sum(member.astype(jnp.int32))).astype(jnp.float32)
        inputs = normed_mlp[chosen]
        weight_in = expert_in[expert]
        weight_back = expert_out[expert]
        expert_value = jnp.zeros((most_rows, D), jnp.float32)
        for part_index in range(N_TENSOR):
            first_unit = part_index * slice_width
            gate_part = jnp.dot(inputs, weight_in[:, 0, first_unit:first_unit + slice_width], preferred_element_type=jnp.float32)
            up_part = jnp.dot(inputs, weight_in[:, 1, first_unit:first_unit + slice_width], preferred_element_type=jnp.float32)
            slice_hidden = (jax.nn.silu(gate_part) * up_part).astype(jnp.bfloat16)
            slice_out = jnp.dot(slice_hidden, weight_back[first_unit:first_unit + slice_width], preferred_element_type=jnp.float32).astype(jnp.bfloat16)
            expert_value = expert_value + lax.optimization_barrier(slice_out).astype(jnp.float32)
        routed = routed.at[chosen].add(expert_value * (gate_sum[chosen] * present)[:, None])
        return (routed, None)
    routed = lax.scan(add_expert, jnp.zeros((token_count, D), jnp.float32), jnp.arange(EXPERTS))[0]
    mixed_rows = (residual_mid.reshape(token_count, D) + shared_part + routed).astype(jnp.bfloat16).reshape(REQS, LEAF_LEN, D)
    return jnp.zeros_like(mixed_rows).at[request_of].set(mixed_rows)
```

```python
import jax
import jax.numpy as jnp
from jax import lax
from jax.experimental import pallas as pl
from jax.experimental.pallas import tpu as pltpu
from jax.sharding import PartitionSpec as P

HEAD_DIM = 128
EPS = 1e-06
ROPE_BASE = 10000.0
MESH = pl.DeviceIdType.MESH
BF = jnp.bfloat16
F32 = jnp.float32
NEG = -1e30


def nt_dot(a, b):
    return lax.dot_general(a, b, (((1,), (1,)), ((), ())), preferred_element_type=F32)


def nn_dot(a, b):
    return jnp.dot(a, b, preferred_element_type=F32)


def rms_rows(values, gain):
    mean_square = jnp.mean(values * values, axis=-1, keepdims=True)
    return (values * lax.rsqrt(mean_square + EPS) * gain).astype(BF)


def iota(shape, dim):
    return lax.broadcasted_iota(jnp.int32, shape, dim)


class Place:
    def __init__(self):
        self.groups = lax.axis_size("dp")
        self.me = lax.axis_index("dp")
        self.t = lax.axis_index("tensor")
        self.chip = self.t // 2
        self.core = lax.rem(self.t, 2)
        self.sib = self.chip * 2 + (1 - self.core)

    def ahead(self, k):
        return lax.rem(self.me + k, self.groups)

    def behind(self, k):
        return lax.rem(self.me + self.groups - k, self.groups)

    def lane(self, k):
        return lax.rem(self.chip + k, 4) * 2 + self.core


def to_group(src, dst, send, recv, group):
    return pltpu.make_async_remote_copy(
        src, dst, send, recv, device_id={"dp": group}, device_id_type=MESH
    )


def to_lane(src, dst, send, recv, lane):
    return pltpu.make_async_remote_copy(
        src, dst, send, recv, device_id={"tensor": lane}, device_id_type=MESH
    )


def announce(p):
    barrier = pltpu.get_barrier_semaphore()

    def signal(k, carry):
        pl.semaphore_signal(barrier, inc=1, device_id={"dp": p.ahead(k)}, device_id_type=MESH)
        return carry

    pl.semaphore_signal(barrier, inc=1, device_id={"tensor": p.sib}, device_id_type=MESH)
    for k in range(1, 4):
        pl.semaphore_signal(barrier, inc=1, device_id={"tensor": p.lane(k)}, device_id_type=MESH)
    lax.fori_loop(1, p.groups, signal, 0)


def await_all(p):
    pl.semaphore_wait(pltpu.get_barrier_semaphore(), p.groups - 1 + 4)


def gather_rows(p, buf, sems, between=None):
    send, recv = sems
    direct = []
    for k in range(1, 4):
        copy = to_lane(buf.at[p.t], buf.at[p.t], send.at[k], recv.at[k], p.lane(k))
        copy.start()
        direct.append(copy)
    passed = [to_lane(buf.at[p.t], buf.at[p.t], send.at[0], recv.at[0], p.sib)]
    passed[0].start()
    if between is not None:
        between()
    for k in range(1, 4):
        direct[k - 1].wait_recv()
        source = p.lane(4 - k)
        copy = to_lane(buf.at[source], buf.at[source], send.at[3 + k], recv.at[3 + k], p.sib)
        copy.start()
        passed.append(copy)
    for copy in direct:
        copy.wait_send()
    for copy in passed:
        copy.wait()


def scatter_sum(p, part, sib_send, sib_recv, rs_send, rs_recv, sems):
    send, recv = sems
    for c in range(4):
        sib_send[c] = part[c * 2 + (1 - p.core)].astype(BF)
    swap = to_lane(sib_send, sib_recv, send.at[0], recv.at[0], p.sib)
    swap.start()
    swap.wait_recv()
    copies = []
    for k in range(1, 4):
        there = lax.rem(p.chip + k, 4)
        rs_send[k - 1] = (part[there * 2 + p.core] + sib_recv[there].astype(F32)).astype(BF)
        copy = to_lane(rs_send.at[k - 1], rs_recv.at[k - 1], send.at[k], recv.at[k], p.lane(k))
        copy.start()
        copies.append(copy)
    total = part[p.t] + sib_recv[p.chip].astype(F32)
    for k in range(1, 4):
        copies[k - 1].wait_recv()
        total = total + rs_recv[k - 1].astype(F32)
    swap.wait_send()
    for copy in copies:
        copy.wait_send()
    return total


def attention_kernel(
    leaf, gain1, gain2, table, wq_hbm, wk_hbm, wv_hbm, wo_hbm, kv_hbm, ein_hbm, eout_hbm,
    res_out, mlp_out, ein_swap, eout_swap,
    wq, wk, wv, wo, kv, xg, qs, qr, bs, br, part, sib_send, sib_recv, rs_send, rs_recv,
    load_sem, swap_send, swap_recv, g1_send, g1_recv, g2_send, g2_recv,
    q_send, q_recv, b_send, b_recv, r_send, r_recv,
):
    p = Place()
    groups = p.groups
    lanes, shard_rows, width = xg.shape
    rows = lanes * shard_rows
    heads = wq.shape[1] // HEAD_DIM
    slot_rows = qs.shape[1]
    leaf_len = slot_rows // 2
    keys = kv.shape[1]
    scale = HEAD_DIM**-0.5

    loads = []
    for j, (src, dst) in enumerate(
        ((wq_hbm, wq), (wk_hbm, wk), (wv_hbm, wv), (wo_hbm, wo), (kv_hbm, kv))
    ):
        copy = pltpu.make_async_copy(src, dst, load_sem.at[j])
        copy.start()
        loads.append(copy)
    announce(p)
    residual = leaf[...].astype(F32)
    xg[p.t] = rms_rows(residual, gain1[...])
    await_all(p)
    other = 1 - p.core
    swaps = [
        to_lane(ein_hbm.at[other], ein_swap, swap_send.at[0], swap_recv.at[0], p.sib),
        to_lane(eout_hbm.at[other], eout_swap, swap_send.at[1], swap_recv.at[1], p.sib),
    ]
    gather_rows(p, xg, (g1_send, g1_recv))
    for copy in swaps:
        copy.start()

    cols = jnp.transpose(table[...], (1, 0))
    lane = iota((rows, HEAD_DIM), 1)
    half = HEAD_DIM // 2
    frequency = jnp.exp(
        (-2.0 / HEAD_DIM * jnp.log(ROPE_BASE)) * lax.rem(lane, half).astype(F32)
    )
    angles = cols[:, 9:10] * frequency
    cosine = jnp.cos(angles)
    sine = jnp.where(lane < half, -1.0, 1.0) * jnp.sin(angles)

    def rotated(values):
        pieces = []
        for h in range(heads):
            one = values[:, h * HEAD_DIM : (h + 1) * HEAD_DIM]
            pieces.append(one * cosine + pltpu.roll(one, half, 1) * sine)
        return jnp.concatenate(pieces, axis=1).astype(BF)

    x = xg[...].reshape(rows, width)
    loads[0].wait()
    queries = rotated(nn_dot(x, wq[...]))

    stacked = []
    places = []
    slot_index = iota((groups * slot_rows, rows), 0).astype(F32)
    for level in range(3):
        start = cols[:, 3 + level : 4 + level]
        count = cols[:, 6 + level : 7 + level]
        start_hi = jnp.floor(start * (1.0 / 32.0))
        count_hi = jnp.floor(count * (1.0 / 32.0))
        meta = jnp.where(
            lane == 0,
            start_hi,
            jnp.where(
                lane == 1,
                start - 32.0 * start_hi,
                jnp.where(lane == 2, count_hi, jnp.where(lane == 3, count - 32.0 * count_hi, 0.0)),
            ),
        )
        stacked.append(jnp.concatenate([queries, meta.astype(BF)], axis=1))
        places.append((slot_index == table[level : level + 1, :]).astype(F32).astype(BF))
    packed = nn_dot(jnp.concatenate(places, axis=1), jnp.concatenate(stacked, axis=0))
    qs[...] = packed.astype(BF).reshape(qs.shape)

    def q_copy(k):
        return to_group(qs.at[k], qr.at[k], q_send.at[k], q_recv.at[k], p.ahead(k))

    def b_copy(k):
        return to_group(bs.at[k], br.at[k], b_send.at[k], b_recv.at[k], p.behind(k))

    def start_q(k, carry):
        q_copy(k).start()
        return carry

    lax.fori_loop(1, groups, start_q, 0)
    qr[0] = qs[0]

    loads[1].wait()
    loads[2].wait()
    key_rows = rotated(nn_dot(x, wk[...]))
    leaf_values = nn_dot(x, wv[...]).astype(BF)
    row_id = iota((rows, rows), 0)
    col_id = iota((rows, rows), 1)
    causal = (row_id // leaf_len == col_id // leaf_len) & (col_id <= row_id)
    outs = [[] for _ in range(heads)]
    logs = [[] for _ in range(heads)]
    for h in range(heads):
        span = slice(h * HEAD_DIM, (h + 1) * HEAD_DIM)
        scores = jnp.where(causal, nt_dot(queries[:, span], key_rows[:, span]) * scale, NEG)
        top = jnp.max(scores, axis=1, keepdims=True)
        weights = jnp.exp(scores - top)
        total = jnp.sum(weights, axis=1, keepdims=True)
        outs[h].append(nn_dot(weights.astype(BF), leaf_values[:, span]) / total)
        logs[h].append(top + jnp.log(total))

    loads[4].wait()
    per_chunk = 8
    chunk_rows = per_chunk * slot_rows
    key_id = iota((chunk_rows, keys), 1).astype(F32)
    chunk_lane = iota((chunk_rows, HEAD_DIM), 1)

    def owner_chunk(c, carry):
        def arrived(k, inner):
            q_copy(k).wait_recv()
            return inner

        lax.fori_loop(jnp.maximum(c * per_chunk, 1), (c + 1) * per_chunk, arrived, 0)
        block = qr[pl.ds(c * per_chunk, per_chunk)].reshape(chunk_rows, qs.shape[2])
        meta = block[:, heads * HEAD_DIM :].astype(F32)
        first = meta[:, 0:1] * 32.0 + meta[:, 1:2]
        last = first + meta[:, 2:3] * 32.0 + meta[:, 3:4]
        visible = (key_id >= first) & (key_id < last)
        pieces = []
        tail = jnp.zeros((chunk_rows, HEAD_DIM), F32)
        for h in range(heads):
            span = slice(h * HEAD_DIM, (h + 1) * HEAD_DIM)
            scores = jnp.where(visible, nt_dot(block[:, span], kv[0, :, span]) * scale, NEG)
            top = jnp.max(scores, axis=1, keepdims=True)
            weights = jnp.exp(scores - top)
            total = jnp.sum(weights, axis=1, keepdims=True)
            pieces.append((nn_dot(weights.astype(BF), kv[1, :, span]) / total).astype(BF))
            log_part = top + jnp.log(total)
            log_hi = log_part.astype(BF).astype(F32)
            tail = jnp.where(
                chunk_lane == 2 * h,
                log_hi,
                jnp.where(chunk_lane == 2 * h + 1, log_part - log_hi, tail),
            )
        pieces.append(tail.astype(BF))
        bs[pl.ds(c * per_chunk, per_chunk)] = jnp.concatenate(pieces, axis=1).reshape(
            per_chunk, slot_rows, qs.shape[2]
        )

        def give_back(k, inner):
            b_copy(k).start()
            return inner

        lax.fori_loop(jnp.maximum(c * per_chunk, 1), (c + 1) * per_chunk, give_back, 0)
        return carry

    lax.fori_loop(0, groups // per_chunk, owner_chunk, 0)
    br[0] = bs[0]

    def returned(k, carry):
        b_copy(k).wait_recv()
        return carry

    lax.fori_loop(1, groups, returned, 0)
    back_all = br[...].reshape(groups * slot_rows, qs.shape[2])
    slot_lane = iota((rows, groups * slot_rows), 1).astype(F32)
    for level in range(3):
        pick = (slot_lane == cols[:, level : level + 1]).astype(F32).astype(BF)
        back = nn_dot(pick, back_all)
        for h in range(heads):
            base = heads * HEAD_DIM + 2 * h
            outs[h].append(back[:, h * HEAD_DIM : (h + 1) * HEAD_DIM])
            logs[h].append(back[:, base : base + 1] + back[:, base + 1 : base + 2])
    merged = []
    for h in range(heads):
        top = jnp.maximum(jnp.maximum(logs[h][0], logs[h][1]), jnp.maximum(logs[h][2], logs[h][3]))
        scales = [jnp.exp(one - top) for one in logs[h]]
        weighted = scales[0] * outs[h][0]
        for j in range(1, 4):
            weighted = weighted + scales[j] * outs[h][j]
        merged.append(weighted / (scales[0] + scales[1] + scales[2] + scales[3]))
    attended = jnp.concatenate(merged, axis=1).astype(BF)

    loads[3].wait()
    part[...] = nn_dot(attended, wo[...]).reshape(part.shape)
    total = scatter_sum(p, part, sib_send, sib_recv, rs_send, rs_recv, (r_send, r_recv))
    residual_mid = residual + total
    res_out[...] = residual_mid
    mlp_out[p.t] = rms_rows(residual_mid, gain2[...])
    gather_rows(p, mlp_out, (g2_send, g2_recv))

    def sent(k, carry):
        q_copy(k).wait_send()
        b_copy(k).wait_send()
        return carry

    lax.fori_loop(1, groups, sent, 0)
    for copy in swaps:
        copy.wait()


def moe_kernel(
    mlp, res, table, ein_hbm, eout_hbm, ein_swap, eout_swap, shin_hbm, shout_hbm,
    out,
    win, wout, shin, shout, sb, xb, yb, zb, part, sib_send, sib_recv, rs_send, rs_recv, fs, fr,
    load_sem, d_send, d_recv, y_send, y_recv, r_send, r_recv, f_send, f_recv,
):
    p = Place()
    groups = p.groups
    lanes, shard_rows, width = mlp.shape
    rows = lanes * shard_rows
    cap = sb.shape[1]
    units = shin.shape[1]
    per_chunk = 8
    chunk_rows = per_chunk * cap
    chunks = groups // per_chunk
    requests = out.shape[0]
    leaf_len = rows // requests

    loads = []
    for j, (src, dst) in enumerate(
        (
            (shin_hbm, shin),
            (shout_hbm, shout),
            (ein_hbm.at[p.core], win.at[:, pl.ds(0, units)]),
            (ein_swap, win.at[:, pl.ds(units, units)]),
            (eout_hbm.at[p.core], wout.at[pl.ds(0, units)]),
            (eout_swap, wout.at[pl.ds(units, units)]),
        )
    ):
        copy = pltpu.make_async_copy(src, dst, load_sem.at[j])
        copy.start()
        loads.append(copy)
    announce(p)

    row_id = iota((rows, rows), 0)
    col_id = iota((rows, rows), 1)
    turn = col_id == lax.rem(row_id, requests) * leaf_len + row_id // requests
    x = nn_dot(turn.astype(F32).astype(BF), mlp[...].reshape(rows, width)).astype(BF)

    top_count = 6
    experts = 2 * groups
    expert_id = iota((experts, rows), 0).astype(F32)
    named = [(expert_id == table[k : k + 1, :]).astype(F32) for k in range(top_count)]
    chosen = named[0]
    for k in range(1, top_count):
        chosen = chosen + named[k]
    earlier = (row_id < col_id).astype(F32).astype(BF)
    before = nn_dot(chosen.astype(BF), earlier)
    slot_rows = []
    for k in range(top_count):
        ids = table[k : k + 1, :]
        slot = jnp.sum(named[k] * before, axis=0, keepdims=True)
        group = jnp.floor(ids * 0.5)
        parity = ids - 2.0 * group
        offset = group - p.me.astype(F32)
        offset = jnp.where(offset < 0, offset + groups, offset)
        place = jnp.where(parity == p.core.astype(F32), offset * cap + slot, -1.0)
        slot_rows.append(place)

    def d_copy(k):
        return to_group(sb.at[k], xb.at[k], d_send.at[k], d_recv.at[k], p.ahead(k))

    def y_copy(k):
        return to_group(yb.at[k], zb.at[k], y_send.at[k], y_recv.at[k], p.behind(k))

    chunk_index = iota((chunk_rows, rows), 0).astype(F32)
    await_all(p)

    def pack(c, carry):
        where = chunk_index + (c * chunk_rows).astype(F32)
        pick = (where == slot_rows[0]).astype(F32)
        for k in range(1, top_count):
            pick = pick + (where == slot_rows[k]).astype(F32)
        sb[pl.ds(c * per_chunk, per_chunk)] = (
            nn_dot(pick.astype(BF), x).astype(BF).reshape(per_chunk, cap, width)
        )

        def start(k, inner):
            d_copy(k).start()
            return inner

        lax.fori_loop(jnp.maximum(c * per_chunk, 1), (c + 1) * per_chunk, start, 0)
        return carry

    lax.fori_loop(0, chunks, pack, 0)
    xb[0] = sb[0]

    loads[0].wait()
    loads[1].wait()
    gate = nt_dot(x, shin[0])
    up = nt_dot(x, shin[1])
    hidden = (gate / (1.0 + jnp.exp(-gate)) * up).astype(BF)
    shared = nn_dot(hidden, shout[...])
    own_row = iota((rows, shard_rows), 0)
    own_col = iota((rows, shard_rows), 1)
    mine = (
        lax.rem(own_row, requests) == (shard_rows // leaf_len) * p.t + own_col // leaf_len
    ) & (own_row // requests == lax.rem(own_col, leaf_len))
    shared = shared + jnp.dot(
        mine.astype(F32), res[...], precision=lax.Precision.HIGHEST, preferred_element_type=F32
    )
    part[...] = shared.reshape(part.shape)

    filler = jnp.zeros((rows - 16, rows), F32)
    cols = jnp.transpose(jnp.concatenate([table[...], filler], axis=0), (1, 0))
    slot_cols = jnp.transpose(
        jnp.concatenate(slot_rows + [jnp.zeros((rows - top_count, rows), F32)], axis=0), (1, 0)
    )
    for j in range(2, 6):
        loads[j].wait()

    def compute(c, carry):
        def arrived(k, inner):
            d_copy(k).wait_recv()
            return inner

        lax.fori_loop(jnp.maximum(c * per_chunk, 1), (c + 1) * per_chunk, arrived, 0)
        block = xb[pl.ds(c * per_chunk, per_chunk)].reshape(chunk_rows, width)
        gate_part = nt_dot(block, win[0])
        up_part = nt_dot(block, win[1])
        acted = (gate_part / (1.0 + jnp.exp(-gate_part)) * up_part).astype(BF)
        yb[pl.ds(c * per_chunk, per_chunk)] = (
            nn_dot(acted, wout[...]).astype(BF).reshape(per_chunk, cap, width)
        )

        def start(k, inner):
            y_copy(k).start()
            return inner

        lax.fori_loop(jnp.maximum(c * per_chunk, 1), (c + 1) * per_chunk, start, 0)
        return carry

    lax.fori_loop(0, chunks, compute, 0)
    zb[0] = yb[0]

    slot_lane = iota((rows, chunk_rows), 1).astype(F32)

    def combine(c, carry):
        def arrived(k, inner):
            y_copy(k).wait_recv()
            return inner

        lax.fori_loop(jnp.maximum(c * per_chunk, 1), (c + 1) * per_chunk, arrived, 0)
        where = slot_lane + (c * chunk_rows).astype(F32)
        gates = jnp.zeros((rows, chunk_rows), F32)
        for k in range(top_count):
            gates = gates + jnp.where(
                where == slot_cols[:, k : k + 1], cols[:, 6 + k : 7 + k], 0.0
            )
        high = gates.astype(BF)
        low = (gates - high.astype(F32)).astype(BF)
        block = zb[pl.ds(c * per_chunk, per_chunk)].reshape(chunk_rows, width)
        part[...] += (nn_dot(high, block) + nn_dot(low, block)).reshape(part.shape)
        return carry

    lax.fori_loop(0, chunks, combine, 0)
    total = scatter_sum(p, part, sib_send, sib_recv, rs_send, rs_recv, (r_send, r_recv))
    mixed = total.astype(BF)

    group_row = iota((groups, requests), 0).astype(F32)
    goes = group_row == table[12:13, 0:requests]
    tags = jnp.sum(jnp.where(goes, table[13:14, 0:requests], 0.0), axis=1, keepdims=True)
    outgoing = nn_dot(goes.astype(F32).astype(BF), mixed)
    tagged = jnp.concatenate([outgoing, jnp.broadcast_to(tags, (groups, 128))], axis=1)
    for k in range(groups):
        fs[k] = tagged[k : k + 1]

    def f_copy(k):
        return to_group(fs.at[k], fr.at[k], f_send.at[k], f_recv.at[k], p.ahead(k))

    def f_start(k, carry):
        f_copy(k).start()
        return carry

    lax.fori_loop(1, groups, f_start, 0)
    fr[0] = fs[0]

    def f_wait(k, carry):
        f_copy(k).wait_recv()
        return carry

    lax.fori_loop(1, groups, f_wait, 0)
    landed = jnp.concatenate([fr[k] for k in range(groups)], axis=0)
    place_lane = iota((groups, requests), 1).astype(F32) + 1.0
    settle = (landed[:, width : width + 1] == place_lane).astype(F32).astype(BF)
    out[...] = lax.dot_general(
        settle,
        landed[:, :width].astype(BF),
        (((0,), (0,)), ((), ())),
        preferred_element_type=F32,
    ).astype(BF)

    def sent(k, carry):
        d_copy(k).wait_send()
        y_copy(k).wait_send()
        f_copy(k).wait_send()
        return carry

    lax.fori_loop(1, groups, sent, 0)


def prefix_table(prefix_owner, prefix_start, prefix_len, leaf_len):
    groups = lax.axis_size("dp")
    owner = jnp.transpose(prefix_owner).reshape(-1)
    order = jnp.arange(owner.shape[0])
    twin = (owner[:, None] == owner[None, :]) & (order[None, :] < order[:, None])
    second = jnp.sum(twin.astype(jnp.int32), axis=1)
    offset = lax.rem(owner - lax.axis_index("dp") + groups, groups)
    slot = ((offset * 2 + second) * leaf_len).reshape(3, -1)
    step = jnp.arange(leaf_len, dtype=jnp.int32)

    def spread(values):
        return jnp.repeat(values, leaf_len, axis=1)

    stepping = jnp.tile(step, prefix_owner.shape[0])[None, :]
    lens = jnp.transpose(prefix_len)
    table = jnp.concatenate(
        [
            spread(slot) + stepping,
            spread(jnp.transpose(prefix_start)),
            spread(lens),
            spread(jnp.sum(lens, axis=0, keepdims=True)) + stepping,
        ],
        axis=0,
    )
    return jnp.pad(table, ((0, 6), (0, 0))).astype(F32)


def route_table(expert_ids, gate_weights, request_of):
    groups = lax.axis_size("dp")
    requests, leaf_len, top_count = expert_ids.shape
    rows = requests * leaf_len
    ids = jnp.transpose(expert_ids, (2, 1, 0)).reshape(top_count, rows).astype(F32)
    gates = jnp.transpose(gate_weights, (2, 1, 0)).reshape(top_count, rows)
    offset = lax.rem(request_of // requests - lax.axis_index("dp") + groups, groups)
    place = lax.rem(request_of, requests) + 1
    moves = jnp.pad(jnp.stack([offset, place]), ((0, 2), (0, rows - requests))).astype(F32)
    return jnp.concatenate([ids, gates, moves], axis=0)


def on_device(
    leaf_tokens,
    attn_gain,
    w_query,
    w_key,
    w_value,
    w_out,
    prefix_kv,
    prefix_owner,
    prefix_start,
    prefix_len,
    mlp_gain,
    shared_in,
    shared_out,
    expert_in,
    expert_out,
    expert_ids,
    gate_weights,
    request_of,
):
    groups = lax.axis_size("dp")
    lanes = lax.axis_size("tensor")
    shard_requests, leaf_len, width = leaf_tokens.shape
    requests = prefix_owner.shape[0]
    shard_rows = shard_requests * leaf_len
    local_width = w_query.shape[1]
    units = shared_out.shape[0]
    slot_rows = 2 * leaf_len
    payload = local_width + 128
    cap = 16
    vmem = pl.BlockSpec(memory_space=pltpu.VMEM)
    hbm = pl.BlockSpec(memory_space=pl.ANY)
    dma = pltpu.SemaphoreType.DMA
    ein = jnp.transpose(expert_in, (0, 2, 3, 1))
    table = prefix_table(prefix_owner, prefix_start, prefix_len, leaf_len)
    exchange = pltpu.VMEM((groups, slot_rows, payload), BF)
    block = pltpu.VMEM((4, shard_rows, width), BF)
    part = pltpu.VMEM((lanes, shard_rows, width), F32)
    residual_mid, mlp_rows, ein_swap, eout_swap = pl.pallas_call(
        attention_kernel,
        out_shape=(
            jax.ShapeDtypeStruct((shard_rows, width), F32),
            jax.ShapeDtypeStruct((lanes, shard_rows, width), BF),
            jax.ShapeDtypeStruct(ein.shape[1:], BF),
            jax.ShapeDtypeStruct(expert_out.shape[1:], BF),
        ),
        in_specs=[vmem] * 4 + [hbm] * 7,
        out_specs=(vmem, vmem, hbm, hbm),
        scratch_shapes=[
            pltpu.VMEM(w_query.shape, BF),
            pltpu.VMEM(w_query.shape, BF),
            pltpu.VMEM(w_query.shape, BF),
            pltpu.VMEM(w_out.shape, BF),
            pltpu.VMEM(prefix_kv.shape, BF),
            pltpu.VMEM((lanes, shard_rows, width), BF),
            exchange,
            exchange,
            exchange,
            exchange,
            part,
            block,
            block,
            block,
            block,
            dma((5,)),
            dma((2,)),
            dma((2,)),
            dma((7,)),
            dma((7,)),
            dma((7,)),
            dma((7,)),
            dma((groups,)),
            dma((groups,)),
            dma((groups,)),
            dma((groups,)),
            dma((4,)),
            dma((4,)),
        ],
        compiler_params=pltpu.CompilerParams(
            collective_id=0, has_side_effects=True, vmem_limit_bytes=48 << 20
        ),
        name="attention",
    )(
        leaf_tokens.reshape(shard_rows, width),
        attn_gain.reshape(1, width),
        mlp_gain.reshape(1, width),
        table,
        w_query,
        w_key,
        w_value,
        w_out,
        prefix_kv,
        ein,
        expert_out,
    )
    routes = route_table(expert_ids, gate_weights, request_of)
    rows_in = pltpu.VMEM((groups, cap, width), BF)
    final = pltpu.VMEM((groups, 1, width + 128), F32)
    mixed = pl.pallas_call(
        moe_kernel,
        out_shape=jax.ShapeDtypeStruct((requests, width), BF),
        in_specs=[vmem] * 3 + [hbm] * 6,
        out_specs=vmem,
        scratch_shapes=[
            pltpu.VMEM((2, 2 * units, width), BF),
            pltpu.VMEM((2 * units, width), BF),
            pltpu.VMEM((2, units, width), BF),
            pltpu.VMEM((units, width), BF),
            rows_in,
            rows_in,
            rows_in,
            rows_in,
            part,
            block,
            block,
            block,
            block,
            final,
            final,
            dma((6,)),
            dma((groups,)),
            dma((groups,)),
            dma((groups,)),
            dma((groups,)),
            dma((4,)),
            dma((4,)),
            dma((groups,)),
            dma((groups,)),
        ],
        compiler_params=pltpu.CompilerParams(
            collective_id=1, has_side_effects=True, vmem_limit_bytes=48 << 20
        ),
        name="experts",
    )(
        mlp_rows,
        residual_mid,
        routes,
        ein,
        expert_out,
        ein_swap,
        eout_swap,
        jnp.transpose(shared_in, (1, 2, 0)),
        shared_out,
    )
    return mixed.reshape(requests, 1, width)


def solution(mesh):
    in_specs = (
        P(("dp", "tensor"), None, None),
        P(),
        P(None, "tensor"),
        P(None, "tensor"),
        P(None, "tensor"),
        P("tensor", None),
        P(None, "dp", "tensor"),
        P("dp", None),
        P("dp", None),
        P("dp", None),
        P(),
        P(None, None, "tensor"),
        P("tensor", None),
        P("dp", None, None, "tensor"),
        P("dp", "tensor", None),
        P("dp", None, None),
        P("dp", None, None),
        P("dp"),
    )
    out_specs = P("dp", "tensor", None)
    return jax.shard_map(
        on_device, mesh=mesh, in_specs=in_specs, out_specs=out_specs, check_vma=False
    )
```

```python
import jax
import jax.numpy as jnp
from jax import lax
from jax.experimental import pallas as pl
from jax.experimental.pallas import tpu as pltpu
from jax.sharding import PartitionSpec as P

HEAD_DIM = 128
EPS = 1e-06
ROPE_BASE = 10000.0
CAP = 16
MESH = pl.DeviceIdType.MESH
BF = jnp.bfloat16
F32 = jnp.float32
NEG = -1e30


def nt_dot(a, b):
    return lax.dot_general(a, b, (((1,), (1,)), ((), ())), preferred_element_type=F32)


def nn_dot(a, b):
    return jnp.dot(a, b, preferred_element_type=F32)


def exact_dot(a, b):
    return jnp.dot(a, b, precision=lax.Precision.HIGHEST, preferred_element_type=F32)


def onehot(mask):
    return mask.astype(F32).astype(BF)


def rms_rows(values, gain):
    mean_square = jnp.mean(values * values, axis=-1, keepdims=True)
    return (values * lax.rsqrt(mean_square + EPS) * gain).astype(BF)


def iota(shape, dim):
    return lax.broadcasted_iota(jnp.int32, shape, dim)


class Place:
    def __init__(self):
        self.groups = lax.axis_size("dp")
        self.me = lax.axis_index("dp")
        self.t = lax.axis_index("tensor")
        self.chip = self.t // 2
        self.core = lax.rem(self.t, 2)
        self.sib = self.chip * 2 + (1 - self.core)
        self.half = lax.rem(self.me, 2)
        self.spot = self.me // 2
        self.spots = self.groups // 2
        self.mirror = self.spot * 2 + (1 - self.half)

    def ahead(self, k):
        return lax.rem(self.me + k, self.groups)

    def behind(self, k):
        return lax.rem(self.me + self.groups - k, self.groups)

    def spot_ahead(self, k):
        return lax.rem(self.spot + k, self.spots) * 2 + self.half

    def spot_behind(self, k):
        return lax.rem(self.spot + self.spots - k, self.spots) * 2 + self.half

    def lane(self, k):
        return lax.rem(self.chip + k, 4) * 2 + self.core


def to_group(src, dst, send, recv, group):
    return pltpu.make_async_remote_copy(
        src, dst, send, recv, device_id={"dp": group}, device_id_type=MESH
    )


def to_lane(src, dst, send, recv, lane):
    return pltpu.make_async_remote_copy(
        src, dst, send, recv, device_id={"tensor": lane}, device_id_type=MESH
    )


def to_both(src, dst, send, recv, group, lane):
    return pltpu.make_async_remote_copy(
        src, dst, send, recv, device_id={"dp": group, "tensor": lane}, device_id_type=MESH
    )


def announce(p):
    barrier = pltpu.get_barrier_semaphore()

    def signal(k, carry):
        pl.semaphore_signal(barrier, inc=1, device_id={"dp": p.ahead(k)}, device_id_type=MESH)
        return carry

    pl.semaphore_signal(barrier, inc=1, device_id={"tensor": p.sib}, device_id_type=MESH)
    for k in range(1, 4):
        pl.semaphore_signal(barrier, inc=1, device_id={"tensor": p.lane(k)}, device_id_type=MESH)
        pl.semaphore_signal(
            barrier,
            inc=1,
            device_id={"dp": p.mirror, "tensor": p.lane(k)},
            device_id_type=MESH,
        )
    lax.fori_loop(1, p.groups, signal, 0)


def await_all(p):
    pl.semaphore_wait(pltpu.get_barrier_semaphore(), p.groups - 1 + 7)


def gather_rows(p, buf, sems, between=None):
    send, recv = sems
    direct = []
    for k in range(1, 4):
        copy = to_lane(buf.at[p.t], buf.at[p.t], send.at[k], recv.at[k], p.lane(k))
        copy.start()
        direct.append(copy)
    passed = [to_lane(buf.at[p.t], buf.at[p.t], send.at[0], recv.at[0], p.sib)]
    passed[0].start()
    if between is not None:
        between()
    for k in range(1, 4):
        direct[k - 1].wait_recv()
        source = p.lane(4 - k)
        copy = to_lane(buf.at[source], buf.at[source], send.at[3 + k], recv.at[3 + k], p.sib)
        copy.start()
        passed.append(copy)
    for copy in direct:
        copy.wait_send()
    for copy in passed:
        copy.wait()


def gather_column(p, buf, sems, between=None):
    send, recv = sems
    direct = []
    for k in range(1, 4):
        direct.append(
            to_lane(buf.at[0, p.t], buf.at[0, p.t], send.at[k], recv.at[k], p.lane(k))
        )
        direct[-1].start()
    for k in range(4):
        direct.append(
            to_both(
                buf.at[0, p.t], buf.at[1, p.t], send.at[4 + k], recv.at[4 + k], p.mirror, p.lane(k)
            )
        )
        direct[-1].start()
    passed = [to_lane(buf.at[0, p.t], buf.at[0, p.t], send.at[0], recv.at[0], p.sib)]
    passed[0].start()
    if between is not None:
        between()
    for j in range(7):
        origin, k = (0, j + 1) if j < 3 else (1, j - 3)
        direct[j].wait_recv()
        block = buf.at[origin, p.lane(4 - k)]
        copy = to_lane(block, block, send.at[8 + j], recv.at[8 + j], p.sib)
        copy.start()
        passed.append(copy)
    for copy in direct:
        copy.wait_send()
    for copy in passed:
        copy.wait()


def scatter_sum(p, part, sib_send, sib_recv, rs_send, rs_recv, sems):
    send, recv = sems
    for c in range(4):
        sib_send[c] = part[:, c * 2 + (1 - p.core)].astype(BF)
    swap = to_lane(sib_send, sib_recv, send.at[0], recv.at[0], p.sib)
    swap.start()
    swap.wait_recv()
    copies = []
    for k in range(1, 4):
        there = lax.rem(p.chip + k, 4)
        rs_send[k - 1] = (part[:, there * 2 + p.core] + sib_recv[there].astype(F32)).astype(BF)
        copy = to_lane(rs_send.at[k - 1], rs_recv.at[k - 1], send.at[k], recv.at[k], p.lane(k))
        copy.start()
        copies.append(copy)
    total = part[:, p.t] + sib_recv[p.chip].astype(F32)
    for k in range(1, 4):
        copies[k - 1].wait_recv()
        total = total + rs_recv[k - 1].astype(F32)
    swap.wait_send()
    for copy in copies:
        copy.wait_send()
    return total


def each(first, last, action):
    def step(k, carry):
        action(k)
        return carry

    lax.fori_loop(first, last, step, 0)


def layer_kernel(
    leaf_hbm, gain1_hbm, gain2_hbm, owner_hbm, start_hbm, count_hbm, wq_hbm, wk_hbm, wv_hbm,
    wo_hbm, kv_hbm, ids_hbm, gates_hbm, moves_hbm, shin_hbm, shout_hbm, ein_hbm, eout_hbm,
    out,
    leaf, gain1, gain2, owner, start, count, wq, wk, wv, wo, kv, ids, gates, moves, shin, shout,
    win, wout, xg, qs, qr, bs, br, part1, sib_send1, sib_recv1, rs_send1, rs_recv1,
    rows2, sb, xb, yb, zb, part2, sib_send2, sib_recv2, rs_send2, rs_recv2,
    cross_send, cross_recv, fs, fr,
    load_sem, swap_send, swap_recv, g1_send, g1_recv, g2_send, g2_recv,
    q_send, q_recv, b_send, b_recv, r1_send, r1_recv,
    d_send, d_recv, y_send, y_recv, r2_send, r2_recv, f_send, f_recv,
):
    p = Place()
    groups = p.groups
    lanes, shard_rows, width = xg.shape
    rows = lanes * shard_rows
    heads = wq.shape[1] // HEAD_DIM
    slot_rows = qs.shape[1]
    leaf_len = slot_rows // 2
    keys = kv.shape[1]
    units = shin.shape[1]
    requests = out.shape[0]
    top_count = ids.shape[1]
    scale = HEAD_DIM**-0.5
    other = 1 - p.core

    loads = {}
    for j, (name, src, dst) in enumerate(
        (
            ("leaf", leaf_hbm, leaf),
            ("gain1", gain1_hbm, gain1),
            ("owner", owner_hbm, owner),
            ("start", start_hbm, start),
            ("count", count_hbm, count),
            ("wq", wq_hbm, wq),
            ("wk", wk_hbm, wk),
            ("wv", wv_hbm, wv),
            ("kv", kv_hbm, kv),
            ("wo", wo_hbm, wo),
            ("gain2", gain2_hbm, gain2),
            ("ids", ids_hbm, ids.at[0]),
            ("gates", gates_hbm, gates.at[0]),
            ("moves", moves_hbm, moves),
            ("shin", shin_hbm, shin),
            ("shout", shout_hbm, shout),
            ("ein", ein_hbm.at[p.core], win.at[:, pl.ds(0, units)]),
            ("eout", eout_hbm.at[p.core], wout.at[pl.ds(0, units)]),
        )
    ):
        loads[name] = pltpu.make_async_copy(src, dst, load_sem.at[j])
        loads[name].start()
    announce(p)
    loads["leaf"].wait()
    loads["gain1"].wait()
    residual = leaf[...].astype(F32)
    xg[p.t] = rms_rows(residual, gain1[...])
    await_all(p)
    swaps = [
        to_lane(
            ein_hbm.at[other], win.at[:, pl.ds(units, units)], swap_send.at[0], swap_recv.at[0], p.sib
        ),
        to_lane(
            eout_hbm.at[other], wout.at[pl.ds(units, units)], swap_send.at[1], swap_recv.at[1], p.sib
        ),
        to_group(ids_hbm, ids.at[1], swap_send.at[2], swap_recv.at[2], p.mirror),
        to_group(gates_hbm, gates.at[1], swap_send.at[3], swap_recv.at[3], p.mirror),
    ]

    lane = iota((rows, HEAD_DIM), 1)
    lane_row = iota((1, rows), 1)
    row_id = iota((rows, rows), 0)
    col_id = iota((rows, rows), 1)
    half = HEAD_DIM // 2
    made = {}

    def tables():
        for name in ("owner", "start", "count"):
            loads[name].wait()
        spread = (iota((requests, rows), 1) // leaf_len == iota((requests, rows), 0)).astype(F32)
        owners = exact_dot(owner[...].astype(F32), spread)
        starts = exact_dot(start[...].astype(F32), spread)
        counts = exact_dot(count[...].astype(F32), spread)
        step = lax.rem(lane_row, leaf_len).astype(F32)
        position = jnp.sum(counts, axis=0, keepdims=True) + step
        first_cols = jnp.transpose(
            jnp.concatenate(
                [owners, starts, counts, position, jnp.zeros((6, rows), F32)], axis=0
            ),
            (1, 0),
        )
        slots = []
        for level in range(3):
            mine = owners[level : level + 1, :]
            second = jnp.zeros((1, rows), F32)
            for above in range(level):
                same = (first_cols[:, above : above + 1] == mine).astype(F32)
                second = jnp.maximum(second, jnp.max(same, axis=0, keepdims=True))
            offset = mine - p.me.astype(F32)
            offset = jnp.where(offset < 0, offset + groups, offset)
            slots.append((offset * 2.0 + second) * leaf_len + step)
        made["slots"] = slots
        made["slot_cols"] = jnp.transpose(
            jnp.concatenate(slots + [jnp.zeros((5, rows), F32)], axis=0), (1, 0)
        )
        frequency = jnp.exp(
            (-2.0 / HEAD_DIM * jnp.log(ROPE_BASE)) * lax.rem(lane, half).astype(F32)
        )
        angles = first_cols[:, 9:10] * frequency
        made["cosine"] = jnp.cos(angles)
        made["sine"] = jnp.where(lane < half, -1.0, 1.0) * jnp.sin(angles)
        made["cols"] = first_cols
        slot_index = iota((groups * slot_rows, rows), 0).astype(F32)
        made["places"] = jnp.concatenate([onehot(slot_index == one) for one in slots], axis=1)
        metas = []
        for level in range(3):
            begin = first_cols[:, 3 + level : 4 + level]
            length = first_cols[:, 6 + level : 7 + level]
            begin_hi = jnp.floor(begin * (1.0 / 32.0))
            length_hi = jnp.floor(length * (1.0 / 32.0))
            meta = jnp.where(lane == 3, length - 32.0 * length_hi, 0.0)
            meta = jnp.where(lane == 2, length_hi, meta)
            meta = jnp.where(lane == 1, begin - 32.0 * begin_hi, meta)
            metas.append(jnp.where(lane == 0, begin_hi, meta).astype(BF))
        made["metas"] = metas

    gather_rows(p, xg, (g1_send, g1_recv), tables)
    for copy in swaps:
        copy.start()
    cosine, sine = made["cosine"], made["sine"]

    def rotated(values):
        pieces = []
        for h in range(heads):
            one = values[:, h * HEAD_DIM : (h + 1) * HEAD_DIM]
            pieces.append(one * cosine + pltpu.roll(one, half, 1) * sine)
        return jnp.concatenate(pieces, axis=1).astype(BF)

    x = xg[...].reshape(rows, width)
    loads["wq"].wait()
    queries = rotated(nn_dot(x, wq[...]))
    stacked = jnp.concatenate(
        [jnp.concatenate([queries, meta], axis=1) for meta in made["metas"]], axis=0
    )
    qs[...] = nn_dot(made["places"], stacked).astype(BF).reshape(qs.shape)

    def q_copy(k):
        return to_group(qs.at[k], qr.at[k], q_send.at[k], q_recv.at[k], p.ahead(k))

    def b_copy(k):
        return to_group(bs.at[k], br.at[k], b_send.at[k], b_recv.at[k], p.behind(k))

    each(1, groups, lambda k: q_copy(k).start())
    qr[0] = qs[0]

    loads["wk"].wait()
    loads["wv"].wait()
    key_rows = rotated(nn_dot(x, wk[...]))
    leaf_values = nn_dot(x, wv[...]).astype(BF)
    causal = (row_id // leaf_len == col_id // leaf_len) & (col_id <= row_id)
    outs = [[] for _ in range(heads)]
    logs = [[] for _ in range(heads)]
    for h in range(heads):
        span = slice(h * HEAD_DIM, (h + 1) * HEAD_DIM)
        scores = jnp.where(causal, nt_dot(queries[:, span], key_rows[:, span]) * scale, NEG)
        top = jnp.max(scores, axis=1, keepdims=True)
        weights = jnp.exp(scores - top)
        total = jnp.sum(weights, axis=1, keepdims=True)
        outs[h].append(nn_dot(weights.astype(BF), leaf_values[:, span]) / total)
        logs[h].append(top + jnp.log(total))

    loads["kv"].wait()
    per_chunk = 8
    chunk_rows = per_chunk * slot_rows
    key_id = iota((chunk_rows, keys), 1).astype(F32)
    chunk_lane = iota((chunk_rows, HEAD_DIM), 1)

    def owner_chunk(c):
        first_k, last_k = jnp.maximum(c * per_chunk, 1), (c + 1) * per_chunk
        each(first_k, last_k, lambda k: q_copy(k).wait_recv())
        block = qr[pl.ds(c * per_chunk, per_chunk)].reshape(chunk_rows, qs.shape[2])
        meta = block[:, heads * HEAD_DIM :].astype(F32)
        first = meta[:, 0:1] * 32.0 + meta[:, 1:2]
        last = first + meta[:, 2:3] * 32.0 + meta[:, 3:4]
        visible = (key_id >= first) & (key_id < last)
        pieces = []
        tail = jnp.zeros((chunk_rows, HEAD_DIM), F32)
        for h in range(heads):
            span = slice(h * HEAD_DIM, (h + 1) * HEAD_DIM)
            scores = jnp.where(visible, nt_dot(block[:, span], kv[0, :, span]) * scale, NEG)
            top = jnp.max(scores, axis=1, keepdims=True)
            weights = jnp.exp(scores - top)
            total = jnp.sum(weights, axis=1, keepdims=True)
            pieces.append((nn_dot(weights.astype(BF), kv[1, :, span]) / total).astype(BF))
            log_part = top + jnp.log(total)
            log_hi = log_part.astype(BF).astype(F32)
            tail = jnp.where(chunk_lane == 2 * h, log_hi, tail)
            tail = jnp.where(chunk_lane == 2 * h + 1, log_part - log_hi, tail)
        pieces.append(tail.astype(BF))
        bs[pl.ds(c * per_chunk, per_chunk)] = jnp.concatenate(pieces, axis=1).reshape(
            per_chunk, slot_rows, qs.shape[2]
        )
        each(first_k, last_k, lambda k: b_copy(k).start())

    each(0, groups // per_chunk, owner_chunk)
    br[0] = bs[0]
    slot_lane = iota((rows, groups * slot_rows), 1).astype(F32)
    picks = [
        onehot(slot_lane == made["slot_cols"][:, level : level + 1]) for level in range(3)
    ]
    each(1, groups, lambda k: b_copy(k).wait_recv())
    back_all = br[...].reshape(groups * slot_rows, qs.shape[2])
    for level in range(3):
        back = nn_dot(picks[level], back_all)
        for h in range(heads):
            base = heads * HEAD_DIM + 2 * h
            outs[h].append(back[:, h * HEAD_DIM : (h + 1) * HEAD_DIM])
            logs[h].append(back[:, base : base + 1] + back[:, base + 1 : base + 2])
    merged = []
    for h in range(heads):
        top = jnp.maximum(jnp.maximum(logs[h][0], logs[h][1]), jnp.maximum(logs[h][2], logs[h][3]))
        scales = [jnp.exp(one - top) for one in logs[h]]
        weighted = scales[0] * outs[h][0]
        for j in range(1, 4):
            weighted = weighted + scales[j] * outs[h][j]
        merged.append(weighted / (scales[0] + scales[1] + scales[2] + scales[3]))
    attended = jnp.concatenate(merged, axis=1).astype(BF)

    loads["wo"].wait()
    part1[...] = nn_dot(attended, wo[...]).reshape(part1.shape)
    total = scatter_sum(p, part1, sib_send1, sib_recv1, rs_send1, rs_recv1, (r1_send, r1_recv))
    residual_mid = residual + total[0]
    loads["gain2"].wait()
    rows2[0, p.t] = rms_rows(residual_mid, gain2[...])

    tokens = 2 * rows
    wide_row = iota((tokens, tokens), 0)
    wide_col = iota((tokens, tokens), 1)
    routes = {}

    def routing():
        loads["ids"].wait()
        loads["gates"].wait()
        swaps[2].wait()
        swaps[3].wait()
        tile = onehot(lax.rem(iota((requests, rows), 1), requests) == iota((requests, rows), 0))
        spots = top_count * leaf_len
        own = (
            lax.rem(iota((spots, rows), 0), leaf_len) == iota((spots, rows), 1) // requests
        ).astype(F32)

        def line(values):
            wide = nn_dot(values.astype(BF), tile) * own
            return jnp.sum(wide.reshape(top_count, leaf_len, rows), axis=1)

        id_lines, gate_lines = [], []
        for origin in range(2):
            id_lines.append(line(ids[origin].reshape(spots, requests).astype(F32)))
            gate = gates[origin].reshape(spots, requests)
            gate_hi = gate.astype(BF).astype(F32)
            gate_lines.append(line(gate_hi) + line(gate - gate_hi))
        id_line = jnp.concatenate(id_lines, axis=1)
        gate_line = jnp.concatenate(gate_lines, axis=1)
        expert_id = iota((2 * groups, tokens), 0).astype(F32)
        named = [(expert_id == id_line[k : k + 1, :]).astype(F32) for k in range(top_count)]
        chosen = named[0]
        for k in range(1, top_count):
            chosen = chosen + named[k]
        earlier = onehot((wide_row < wide_col) & (wide_row // rows == wide_col // rows))
        before = nn_dot(chosen.astype(BF), earlier)
        origin_row = (iota((1, tokens), 1) // rows).astype(F32)
        slots = []
        for k in range(top_count):
            one = id_line[k : k + 1, :]
            slot = jnp.sum(named[k] * before, axis=0, keepdims=True)
            group = jnp.floor(one * 0.5)
            spot = jnp.floor(one * 0.25)
            here = (one - 2.0 * group == p.core.astype(F32)) & (
                group - 2.0 * spot == p.half.astype(F32)
            )
            offset = spot - p.spot.astype(F32)
            offset = jnp.where(offset < 0, offset + p.spots, offset)
            slots.append(jnp.where(here, (offset * 2.0 + origin_row) * CAP + slot, -1.0))
        routes["slots"] = slots
        routes["cols"] = jnp.transpose(
            jnp.concatenate(slots + [gate_line, jnp.zeros((4, tokens), F32)], axis=0), (1, 0)
        )

    gather_column(p, rows2, (g2_send, g2_recv), routing)
    turn = onehot(
        wide_col
        == wide_row // rows * rows
        + lax.rem(wide_row, requests) * leaf_len
        + lax.rem(wide_row, rows) // requests
    )
    x = nn_dot(turn, rows2[...].reshape(tokens, width)).astype(BF)

    cap = sb.shape[1]
    per_chunk2 = 4
    chunk2 = per_chunk2 * cap

    def d_copy(k):
        return to_group(sb.at[k], xb.at[k], d_send.at[k], d_recv.at[k], p.spot_ahead(k))

    def y_copy(k):
        return to_group(yb.at[k], zb.at[k], y_send.at[k], y_recv.at[k], p.spot_behind(k))

    chunk_index = iota((chunk2, tokens), 0).astype(F32)

    def pack(c):
        where = chunk_index + (c * chunk2).astype(F32)
        pick = (where == routes["slots"][0]).astype(F32)
        for k in range(1, top_count):
            pick = pick + (where == routes["slots"][k]).astype(F32)
        sb[pl.ds(c * per_chunk2, per_chunk2)] = (
            nn_dot(pick.astype(BF), x).astype(BF).reshape(per_chunk2, cap, width)
        )
        each(
            jnp.maximum(c * per_chunk2, 1), (c + 1) * per_chunk2, lambda k: d_copy(k).start()
        )

    each(0, p.spots // per_chunk2, pack)
    xb[0] = sb[0]

    loads["shin"].wait()
    loads["shout"].wait()
    x_own = x[:rows]
    gate = nt_dot(x_own, shin[0])
    up = nt_dot(x_own, shin[1])
    hidden = (gate / (1.0 + jnp.exp(-gate)) * up).astype(BF)
    shared = nn_dot(hidden, shout[...])
    own_row = iota((rows, shard_rows), 0)
    own_col = iota((rows, shard_rows), 1)
    mine = (
        lax.rem(own_row, requests) == (shard_rows // leaf_len) * p.t + own_col // leaf_len
    ) & (own_row // requests == lax.rem(own_col, leaf_len))
    shared = shared + exact_dot(mine.astype(F32), residual_mid)
    part2[0] = shared.reshape(part2.shape[1:])
    part2[1] = jnp.zeros(part2.shape[1:], F32)

    loads["ein"].wait()
    loads["eout"].wait()
    swaps[0].wait()
    swaps[1].wait()

    def compute(c):
        first_k, last_k = jnp.maximum(c * per_chunk2, 1), (c + 1) * per_chunk2
        each(first_k, last_k, lambda k: d_copy(k).wait_recv())
        block = xb[pl.ds(c * per_chunk2, per_chunk2)].reshape(chunk2, width)
        gate_part = nt_dot(block, win[0])
        up_part = nt_dot(block, win[1])
        acted = (gate_part / (1.0 + jnp.exp(-gate_part)) * up_part).astype(BF)
        yb[pl.ds(c * per_chunk2, per_chunk2)] = (
            nn_dot(acted, wout[...]).astype(BF).reshape(per_chunk2, cap, width)
        )
        each(first_k, last_k, lambda k: y_copy(k).start())

    each(0, p.spots // per_chunk2, compute)
    zb[0] = yb[0]
    token_lane = iota((tokens, chunk2), 1).astype(F32)

    def combine(c):
        first_k, last_k = jnp.maximum(c * per_chunk2, 1), (c + 1) * per_chunk2
        each(first_k, last_k, lambda k: y_copy(k).wait_recv())
        where = token_lane + (c * chunk2).astype(F32)
        weights = jnp.zeros((tokens, chunk2), F32)
        for k in range(top_count):
            weights = weights + jnp.where(
                where == routes["cols"][:, k : k + 1],
                routes["cols"][:, top_count + k : top_count + k + 1],
                0.0,
            )
        high = weights.astype(BF)
        low = (weights - high.astype(F32)).astype(BF)
        block = zb[pl.ds(c * per_chunk2, per_chunk2)].reshape(chunk2, width)
        part2[...] += (nn_dot(high, block) + nn_dot(low, block)).reshape(part2.shape)

    each(0, p.spots // per_chunk2, combine)
    total = scatter_sum(p, part2, sib_send2, sib_recv2, rs_send2, rs_recv2, (r2_send, r2_recv))
    cross_send[...] = total[1].astype(BF)
    cross = to_group(cross_send, cross_recv, f_send.at[0], f_recv.at[0], p.mirror)
    cross.start()

    loads["moves"].wait()
    target = moves[...]
    aim = lax.rem(target // requests - p.me + groups, groups)
    spot_tag = lax.rem(target, requests) + 1
    goes = iota((groups, requests), 0) == aim
    tags = jnp.sum(jnp.where(goes, spot_tag.astype(F32), 0.0), axis=1, keepdims=True)
    cross.wait_recv()
    mixed = (total[0] + cross_recv[...].astype(F32)).astype(BF)
    outgoing = nn_dot(onehot(goes), mixed)
    tagged = jnp.concatenate([outgoing, jnp.broadcast_to(tags, (groups, 128))], axis=1)
    for k in range(groups):
        fs[k] = tagged[k : k + 1]

    def f_copy(k):
        return to_group(fs.at[k], fr.at[k], f_send.at[k], f_recv.at[k], p.ahead(k))

    each(1, groups, lambda k: f_copy(k).start())
    fr[0] = fs[0]
    each(1, groups, lambda k: f_copy(k).wait_recv())
    landed = jnp.concatenate([fr[k] for k in range(groups)], axis=0)
    place_lane = iota((groups, requests), 1).astype(F32) + 1.0
    settle = onehot(landed[:, width : width + 1] == place_lane)
    out[...] = lax.dot_general(
        settle,
        landed[:, :width].astype(BF),
        (((0,), (0,)), ((), ())),
        preferred_element_type=F32,
    ).astype(BF)

    cross.wait_send()

    def sent(k):
        q_copy(k).wait_send()
        b_copy(k).wait_send()
        f_copy(k).wait_send()

    def sent2(k):
        d_copy(k).wait_send()
        y_copy(k).wait_send()

    each(1, groups, sent)
    each(1, p.spots, sent2)


def on_device(
    leaf_tokens,
    attn_gain,
    w_query,
    w_key,
    w_value,
    w_out,
    prefix_kv,
    prefix_owner,
    prefix_start,
    prefix_len,
    mlp_gain,
    shared_in,
    shared_out,
    expert_in,
    expert_out,
    expert_ids,
    gate_weights,
    request_of,
):
    groups = lax.axis_size("dp")
    lanes = lax.axis_size("tensor")
    shard_requests, leaf_len, width = leaf_tokens.shape
    requests = prefix_owner.shape[0]
    shard_rows = shard_requests * leaf_len
    local_width = w_query.shape[1]
    units = shared_out.shape[0]
    top_count = expert_ids.shape[2]
    slot_rows = 2 * leaf_len
    payload = local_width + 128
    hbm = pl.BlockSpec(memory_space=pltpu.HBM)
    dma = pltpu.SemaphoreType.DMA
    vm = pltpu.VMEM
    exchange = vm((groups, slot_rows, payload), BF)
    table = vm((3, requests), jnp.int32)
    weight = vm(w_query.shape, BF)
    block1 = vm((4, 1, shard_rows, width), BF)
    block2 = vm((4, 2, shard_rows, width), BF)
    rows_in = vm((groups // 2, 2 * CAP, width), BF)
    final = vm((groups, 1, width + 128), F32)
    column = (2, top_count, leaf_len, requests)
    mixed = pl.pallas_call(
        layer_kernel,
        out_shape=jax.ShapeDtypeStruct((requests, width), BF),
        in_specs=[hbm] * 18,
        out_specs=pl.BlockSpec(memory_space=pltpu.VMEM),
        scratch_shapes=[
            vm((shard_rows, width), BF),
            vm((1, width), F32),
            vm((1, width), F32),
            table,
            table,
            table,
            weight,
            weight,
            weight,
            vm(w_out.shape, BF),
            vm(prefix_kv.shape, BF),
            vm(column, jnp.int32),
            vm(column, F32),
            vm((1, requests), jnp.int32),
            vm((2, units, width), BF),
            vm((units, width), BF),
            vm((2, 2 * units, width), BF),
            vm((2 * units, width), BF),
            vm((lanes, shard_rows, width), BF),
            exchange,
            exchange,
            exchange,
            exchange,
            vm((1, lanes, shard_rows, width), F32),
            block1,
            block1,
            block1,
            block1,
            vm((2, lanes, shard_rows, width), BF),
            rows_in,
            rows_in,
            rows_in,
            rows_in,
            vm((2, lanes, shard_rows, width), F32),
            block2,
            block2,
            block2,
            block2,
            vm((shard_rows, width), BF),
            vm((shard_rows, width), BF),
            final,
            final,
            dma((18,)),
            dma((4,)),
            dma((4,)),
            dma((7,)),
            dma((7,)),
            dma((15,)),
            dma((15,)),
            dma((groups,)),
            dma((groups,)),
            dma((groups,)),
            dma((groups,)),
            dma((4,)),
            dma((4,)),
            dma((groups // 2,)),
            dma((groups // 2,)),
            dma((groups // 2,)),
            dma((groups // 2,)),
            dma((4,)),
            dma((4,)),
            dma((groups,)),
            dma((groups,)),
        ],
        compiler_params=pltpu.CompilerParams(
            collective_id=0, has_side_effects=True, vmem_limit_bytes=56 << 20
        ),
        name="layer",
    )(
        leaf_tokens.reshape(shard_rows, width),
        attn_gain.reshape(1, width),
        mlp_gain.reshape(1, width),
        jnp.transpose(prefix_owner),
        jnp.transpose(prefix_start),
        jnp.transpose(prefix_len),
        w_query,
        w_key,
        w_value,
        w_out,
        prefix_kv,
        jnp.transpose(expert_ids, (2, 1, 0)),
        jnp.transpose(gate_weights, (2, 1, 0)),
        request_of.reshape(1, requests),
        jnp.transpose(shared_in, (1, 2, 0)),
        shared_out,
        jnp.transpose(expert_in, (0, 2, 3, 1)),
        expert_out,
    )
    return mixed.reshape(requests, 1, width)


def solution(mesh):
    in_specs = (
        P(("dp", "tensor"), None, None),
        P(),
        P(None, "tensor"),
        P(None, "tensor"),
        P(None, "tensor"),
        P("tensor", None),
        P(None, "dp", "tensor"),
        P("dp", None),
        P("dp", None),
        P("dp", None),
        P(),
        P(None, None, "tensor"),
        P("tensor", None),
        P("dp", None, None, "tensor"),
        P("dp", "tensor", None),
        P("dp", None, None),
        P("dp", None, None),
        P("dp"),
    )
    out_specs = P("dp", "tensor", None)
    return jax.shard_map(
        on_device, mesh=mesh, in_specs=in_specs, out_specs=out_specs, check_vma=False
    )
```

```python
import jax
import jax.numpy as jnp
from jax import lax
from jax.experimental import pallas as pl
from jax.experimental.pallas import tpu as pltpu
from jax.sharding import PartitionSpec as P

HEAD_DIM = 128
EPS = 1e-06
ROPE_BASE = 10000.0
CAP = 16
PARTS = 2
MESH = pl.DeviceIdType.MESH
BF = jnp.bfloat16
F32 = jnp.float32
NEG = -1e30


def nt_dot(a, b):
    return lax.dot_general(a, b, (((1,), (1,)), ((), ())), preferred_element_type=F32)


def nn_dot(a, b):
    return jnp.dot(a, b, preferred_element_type=F32)


def exact_dot(a, b):
    return jnp.dot(a, b, precision=lax.Precision.HIGHEST, preferred_element_type=F32)


def onehot(mask):
    return mask.astype(F32).astype(BF)


def rms_rows(values, gain):
    mean_square = jnp.mean(values * values, axis=-1, keepdims=True)
    return (values * lax.rsqrt(mean_square + EPS) * gain).astype(BF)


def iota(shape, dim):
    return lax.broadcasted_iota(jnp.int32, shape, dim)


class Place:
    def __init__(self):
        self.groups = lax.axis_size("dp")
        self.me = lax.axis_index("dp")
        self.t = lax.axis_index("tensor")
        self.chip = self.t // 2
        self.core = lax.rem(self.t, 2)
        self.sib = self.chip * 2 + (1 - self.core)
        self.half = lax.rem(self.me, 2)
        self.spot = self.me // 2
        self.spots = self.groups // 2
        self.mirror = self.spot * 2 + (1 - self.half)

    def ahead(self, k):
        return lax.rem(self.me + k, self.groups)

    def behind(self, k):
        return lax.rem(self.me + self.groups - k, self.groups)

    def spot_ahead(self, k):
        return lax.rem(self.spot + k, self.spots) * 2 + self.half

    def spot_behind(self, k):
        return lax.rem(self.spot + self.spots - k, self.spots) * 2 + self.half

    def lane(self, k):
        return lax.rem(self.chip + k, 4) * 2 + self.core


def to_group(src, dst, send, recv, group):
    return pltpu.make_async_remote_copy(
        src, dst, send, recv, device_id={"dp": group}, device_id_type=MESH
    )


def to_lane(src, dst, send, recv, lane):
    return pltpu.make_async_remote_copy(
        src, dst, send, recv, device_id={"tensor": lane}, device_id_type=MESH
    )


def to_both(src, dst, send, recv, group, lane):
    return pltpu.make_async_remote_copy(
        src, dst, send, recv, device_id={"dp": group, "tensor": lane}, device_id_type=MESH
    )


def announce(p):
    barrier = pltpu.get_barrier_semaphore()

    def signal(k, carry):
        pl.semaphore_signal(barrier, inc=1, device_id={"dp": p.ahead(k)}, device_id_type=MESH)
        return carry

    pl.semaphore_signal(barrier, inc=1, device_id={"tensor": p.sib}, device_id_type=MESH)
    for k in range(1, 4):
        pl.semaphore_signal(barrier, inc=1, device_id={"tensor": p.lane(k)}, device_id_type=MESH)
        pl.semaphore_signal(
            barrier,
            inc=1,
            device_id={"dp": p.mirror, "tensor": p.lane(k)},
            device_id_type=MESH,
        )
    lax.fori_loop(1, p.groups, signal, 0)


def await_all(p):
    pl.semaphore_wait(pltpu.get_barrier_semaphore(), p.groups - 1 + 7)


def gather_rows(p, buf, sems, between=None):
    send, recv = sems
    direct = []
    for k in range(1, 4):
        copy = to_lane(buf.at[p.t], buf.at[p.t], send.at[k], recv.at[k], p.lane(k))
        copy.start()
        direct.append(copy)
    passed = [to_lane(buf.at[p.t], buf.at[p.t], send.at[0], recv.at[0], p.sib)]
    passed[0].start()
    if between is not None:
        between()
    for k in range(1, 4):
        direct[k - 1].wait_recv()
        source = p.lane(4 - k)
        copy = to_lane(buf.at[source], buf.at[source], send.at[3 + k], recv.at[3 + k], p.sib)
        copy.start()
        passed.append(copy)
    for copy in direct:
        copy.wait_send()
    for copy in passed:
        copy.wait()


class ColumnGather:
    def __init__(self, p, buf, sems, s):
        self.p, self.buf = p, buf.at[s]
        send, recv = sems
        self.send, self.recv = send.at[s], recv.at[s]
        own, there = self.buf.at[0, p.t], self.buf.at[1, p.t]
        self.direct = [
            to_lane(own, own, self.send.at[k], self.recv.at[k], p.lane(k)) for k in range(1, 4)
        ] + [
            to_both(own, there, self.send.at[4 + k], self.recv.at[4 + k], p.mirror, p.lane(k))
            for k in range(4)
        ]
        self.passed = [to_lane(own, own, self.send.at[0], self.recv.at[0], p.sib)]

    def start(self):
        for copy in self.direct + self.passed:
            copy.start()

    def finish(self):
        p = self.p
        for j in range(7):
            origin, k = (0, j + 1) if j < 3 else (1, j - 3)
            self.direct[j].wait_recv()
            block = self.buf.at[origin, p.lane(4 - k)]
            copy = to_lane(block, block, self.send.at[8 + j], self.recv.at[8 + j], p.sib)
            copy.start()
            self.passed.append(copy)
        for copy in self.passed:
            copy.wait_recv()

    def drain(self):
        for copy in self.direct + self.passed:
            copy.wait_send()


class ScatterSum:
    def __init__(self, p, part, sib_send, sib_recv, rs_send, rs_recv, sems):
        self.p, self.part = p, part
        self.sib_send, self.sib_recv = sib_send, sib_recv
        self.rs_send, self.rs_recv = rs_send, rs_recv
        send, recv = sems
        self.swap = to_lane(sib_send, sib_recv, send.at[0], recv.at[0], p.sib)
        self.copies = [
            to_lane(rs_send.at[k - 1], rs_recv.at[k - 1], send.at[k], recv.at[k], p.lane(k))
            for k in range(1, 4)
        ]

    def start(self):
        p = self.p
        for c in range(4):
            self.sib_send[c] = self.part[:, c * 2 + (1 - p.core)].astype(BF)
        self.swap.start()
        self.swap.wait_recv()
        for k in range(1, 4):
            there = lax.rem(p.chip + k, 4)
            self.rs_send[k - 1] = (
                self.part[:, there * 2 + p.core] + self.sib_recv[there].astype(F32)
            ).astype(BF)
            self.copies[k - 1].start()

    def finish(self):
        p = self.p
        total = self.part[:, p.t] + self.sib_recv[p.chip].astype(F32)
        for k in range(1, 4):
            self.copies[k - 1].wait_recv()
            total = total + self.rs_recv[k - 1].astype(F32)
        self.swap.wait_send()
        for copy in self.copies:
            copy.wait_send()
        return total


def each(first, last, action):
    def step(k, carry):
        action(k)
        return carry

    lax.fori_loop(first, last, step, 0)


def layer_kernel(
    leaf_hbm, gain1_hbm, gain2_hbm, owner_hbm, start_hbm, count_hbm, wq_hbm, wk_hbm, wv_hbm,
    wo_hbm, kv_hbm, ids_hbm, gates_hbm, moves_hbm, shin_hbm, shout_hbm, ein_hbm, eout_hbm,
    out,
    leaf, gain1, gain2, owner, start, count, wq, wk, wv, wo, kv, ids, gates, moves, shin, shout,
    win, wout, xg, ms, mr, qs, qr, bs, br, part1, sib_send1, sib_recv1, rs_send1, rs_recv1,
    rows2, sb, xb, hid, yb, zb, gate_hi, gate_lo, part2, sib_send2, sib_recv2, rs_send2, rs_recv2,
    fs, fr,
    load_sem, swap_send, swap_recv, g1_send, g1_recv, g2_send, g2_recv,
    m_send, m_recv, q_send, q_recv, b_send, b_recv, r1_send, r1_recv,
    d_send, d_recv, y_send, y_recv, r2_send, r2_recv, f_send, f_recv,
):
    p = Place()
    groups = p.groups
    lanes, shard_rows, width = xg.shape
    rows = lanes * shard_rows
    heads = wq.shape[1] // HEAD_DIM
    slot_rows = qs.shape[1]
    leaf_len = slot_rows // 2
    keys = kv.shape[1]
    units = shin.shape[1]
    requests = out.shape[0]
    top_count = ids.shape[1]
    scale = HEAD_DIM**-0.5
    other = 1 - p.core

    loads = {}
    for j, (name, src, dst) in enumerate(
        (
            ("leaf", leaf_hbm, leaf),
            ("gain1", gain1_hbm, gain1),
            ("owner", owner_hbm, owner),
            ("start", start_hbm, start),
            ("count", count_hbm, count),
            ("wq", wq_hbm, wq),
            ("wk", wk_hbm, wk),
            ("wv", wv_hbm, wv),
            ("kv", kv_hbm, kv),
            ("wo", wo_hbm, wo),
            ("gain2", gain2_hbm, gain2),
            ("ids", ids_hbm, ids.at[0]),
            ("gates", gates_hbm, gates.at[0]),
            ("moves", moves_hbm, moves.at[0]),
            ("shin", shin_hbm, shin),
            ("shout", shout_hbm, shout),
            ("ein", ein_hbm.at[p.core], win.at[:, pl.ds(0, units)]),
            ("eout", eout_hbm.at[p.core], wout.at[pl.ds(0, units)]),
        )
    ):
        loads[name] = pltpu.make_async_copy(src, dst, load_sem.at[j])
        loads[name].start()
    announce(p)
    loads["leaf"].wait()
    loads["gain1"].wait()
    residual = leaf[...].astype(F32)
    xg[p.t] = rms_rows(residual, gain1[...])
    swaps = [
        to_lane(
            ein_hbm.at[other], win.at[:, pl.ds(units, units)], swap_send.at[0], swap_recv.at[0], p.sib
        ),
        to_lane(
            eout_hbm.at[other], wout.at[pl.ds(units, units)], swap_send.at[1], swap_recv.at[1], p.sib
        ),
        to_group(ids_hbm, ids.at[1], swap_send.at[2], swap_recv.at[2], p.mirror),
        to_group(gates_hbm, gates.at[1], swap_send.at[3], swap_recv.at[3], p.mirror),
        to_group(moves_hbm, moves.at[1], swap_send.at[4], swap_recv.at[4], p.mirror),
    ]

    lane = iota((rows, HEAD_DIM), 1)
    lane_row = iota((1, rows), 1)
    row_id = iota((rows, rows), 0)
    col_id = iota((rows, rows), 1)
    half = HEAD_DIM // 2
    made = {}

    def tables():
        for name in ("owner", "start", "count"):
            loads[name].wait()
        spread = (iota((requests, rows), 1) // leaf_len == iota((requests, rows), 0)).astype(F32)
        owners = exact_dot(owner[...].astype(F32), spread)
        starts = exact_dot(start[...].astype(F32), spread)
        counts = exact_dot(count[...].astype(F32), spread)
        step = lax.rem(lane_row, leaf_len).astype(F32)
        position = jnp.sum(counts, axis=0, keepdims=True) + step
        first_cols = jnp.transpose(
            jnp.concatenate(
                [owners, starts, counts, position, jnp.zeros((6, rows), F32)], axis=0
            ),
            (1, 0),
        )
        slots = []
        for level in range(3):
            mine = owners[level : level + 1, :]
            second = jnp.zeros((1, rows), F32)
            for above in range(level):
                same = (first_cols[:, above : above + 1] == mine).astype(F32)
                second = jnp.maximum(second, jnp.max(same, axis=0, keepdims=True))
            offset = mine - p.me.astype(F32)
            offset = jnp.where(offset < 0, offset + groups, offset)
            slots.append((offset * 2.0 + second) * leaf_len + step)
        made["slots"] = slots
        made["slot_cols"] = jnp.transpose(
            jnp.concatenate(slots + [jnp.zeros((5, rows), F32)], axis=0), (1, 0)
        )
        frequency = jnp.exp(
            (-2.0 / HEAD_DIM * jnp.log(ROPE_BASE)) * lax.rem(lane, half).astype(F32)
        )
        angles = first_cols[:, 9:10] * frequency
        made["cosine"] = jnp.cos(angles)
        made["sine"] = jnp.where(lane < half, -1.0, 1.0) * jnp.sin(angles)
        made["cols"] = first_cols
        slot_index = iota((groups * slot_rows, rows), 0).astype(F32)
        made["places"] = jnp.concatenate([onehot(slot_index == one) for one in slots], axis=1)
        metas = []
        for level in range(3):
            begin = first_cols[:, 3 + level : 4 + level]
            length = first_cols[:, 6 + level : 7 + level]
            begin_hi = jnp.floor(begin * (1.0 / 32.0))
            length_hi = jnp.floor(length * (1.0 / 32.0))
            meta = jnp.where(lane == 3, length - 32.0 * length_hi, 0.0)
            meta = jnp.where(lane == 2, length_hi, meta)
            meta = jnp.where(lane == 1, begin - 32.0 * begin_hi, meta)
            metas.append(jnp.where(lane == 0, begin_hi, meta).astype(BF))
        ms[...] = nn_dot(made["places"], jnp.concatenate(metas, axis=0)).astype(BF).reshape(ms.shape)

    def m_copy(k):
        return to_group(ms.at[k], mr.at[k], m_send.at[k], m_recv.at[k], p.ahead(k))

    tables()
    await_all(p)

    def ahead_of_queries():
        each(1, groups, lambda k: m_copy(k).start())
        mr[0] = ms[0]

    gather_rows(p, xg, (g1_send, g1_recv), ahead_of_queries)
    for copy in swaps:
        copy.start()
    cosine, sine = made["cosine"], made["sine"]

    def rotated(values):
        pieces = []
        for h in range(heads):
            one = values[:, h * HEAD_DIM : (h + 1) * HEAD_DIM]
            pieces.append(one * cosine + pltpu.roll(one, half, 1) * sine)
        return jnp.concatenate(pieces, axis=1).astype(BF)

    x = xg[...].reshape(rows, width)
    loads["wq"].wait()
    queries = rotated(nn_dot(x, wq[...]))
    stacked = jnp.concatenate([queries] * 3, axis=0)
    qs[...] = nn_dot(made["places"], stacked).astype(BF).reshape(qs.shape)

    def q_copy(k):
        return to_group(qs.at[k], qr.at[k], q_send.at[k], q_recv.at[k], p.ahead(k))

    def b_copy(k):
        return to_group(bs.at[k], br.at[k], b_send.at[k], b_recv.at[k], p.behind(k))

    each(1, groups, lambda k: q_copy(k).start())
    qr[0] = qs[0]

    loads["wk"].wait()
    loads["wv"].wait()
    key_rows = rotated(nn_dot(x, wk[...]))
    leaf_values = nn_dot(x, wv[...]).astype(BF)
    causal = (row_id // leaf_len == col_id // leaf_len) & (col_id <= row_id)
    outs = [[] for _ in range(heads)]
    logs = [[] for _ in range(heads)]
    for h in range(heads):
        span = slice(h * HEAD_DIM, (h + 1) * HEAD_DIM)
        scores = jnp.where(causal, nt_dot(queries[:, span], key_rows[:, span]) * scale, NEG)
        top = jnp.max(scores, axis=1, keepdims=True)
        weights = jnp.exp(scores - top)
        total = jnp.sum(weights, axis=1, keepdims=True)
        outs[h].append(nn_dot(weights.astype(BF), leaf_values[:, span]) / total)
        logs[h].append(top + jnp.log(total))

    loads["kv"].wait()
    per_chunk = 8
    chunk_rows = per_chunk * slot_rows
    key_id = iota((chunk_rows, keys), 1).astype(F32)
    chunk_lane = iota((chunk_rows, HEAD_DIM), 1)

    def owner_chunk(c):
        first_k, last_k = jnp.maximum(c * per_chunk, 1), (c + 1) * per_chunk
        each(first_k, last_k, lambda k: m_copy(k).wait_recv())
        each(first_k, last_k, lambda k: q_copy(k).wait_recv())
        block = qr[pl.ds(c * per_chunk, per_chunk)].reshape(chunk_rows, qs.shape[2])
        meta = mr[pl.ds(c * per_chunk, per_chunk)].reshape(chunk_rows, HEAD_DIM).astype(F32)
        first = meta[:, 0:1] * 32.0 + meta[:, 1:2]
        last = first + meta[:, 2:3] * 32.0 + meta[:, 3:4]
        visible = (key_id >= first) & (key_id < last)
        pieces = []
        tail = jnp.zeros((chunk_rows, HEAD_DIM), F32)
        for h in range(heads):
            span = slice(h * HEAD_DIM, (h + 1) * HEAD_DIM)
            scores = jnp.where(visible, nt_dot(block[:, span], kv[0, :, span]) * scale, NEG)
            top = jnp.max(scores, axis=1, keepdims=True)
            weights = jnp.exp(scores - top)
            total = jnp.sum(weights, axis=1, keepdims=True)
            pieces.append((nn_dot(weights.astype(BF), kv[1, :, span]) / total).astype(BF))
            log_part = top + jnp.log(total)
            log_hi = log_part.astype(BF).astype(F32)
            tail = jnp.where(chunk_lane == 2 * h, log_hi, tail)
            tail = jnp.where(chunk_lane == 2 * h + 1, log_part - log_hi, tail)
        pieces.append(tail.astype(BF))
        bs[pl.ds(c * per_chunk, per_chunk)] = jnp.concatenate(pieces, axis=1).reshape(
            per_chunk, slot_rows, bs.shape[2]
        )
        each(first_k, last_k, lambda k: b_copy(k).start())

    each(0, groups // per_chunk, owner_chunk)
    br[0] = bs[0]
    slot_lane = iota((rows, groups * slot_rows), 1).astype(F32)
    picks = [
        onehot(slot_lane == made["slot_cols"][:, level : level + 1]) for level in range(3)
    ]
    each(1, groups, lambda k: b_copy(k).wait_recv())
    back_all = br[...].reshape(groups * slot_rows, br.shape[2])
    for level in range(3):
        back = nn_dot(picks[level], back_all)
        for h in range(heads):
            base = heads * HEAD_DIM + 2 * h
            outs[h].append(back[:, h * HEAD_DIM : (h + 1) * HEAD_DIM])
            logs[h].append(back[:, base : base + 1] + back[:, base + 1 : base + 2])
    merged = []
    for h in range(heads):
        top = jnp.maximum(jnp.maximum(logs[h][0], logs[h][1]), jnp.maximum(logs[h][2], logs[h][3]))
        scales = [jnp.exp(one - top) for one in logs[h]]
        weighted = scales[0] * outs[h][0]
        for j in range(1, 4):
            weighted = weighted + scales[j] * outs[h][j]
        merged.append(weighted / (scales[0] + scales[1] + scales[2] + scales[3]))
    attended = jnp.concatenate(merged, axis=1).astype(BF)

    loads["wo"].wait()
    part1[...] = nn_dot(attended, wo[...]).reshape(part1.shape)
    summed = ScatterSum(
        p, part1, sib_send1, sib_recv1, rs_send1, rs_recv1, (r1_send, r1_recv)
    )
    summed.start()
    residual_mid = residual + summed.finish()[0]
    loads["gain2"].wait()
    normed = rms_rows(residual_mid, gain2[...])
    span = width // PARTS
    gathers = [ColumnGather(p, rows2, (g2_send, g2_recv), s) for s in range(PARTS)]
    for s in range(PARTS):
        rows2[s, 0, p.t] = normed[:, s * span : (s + 1) * span]
        gathers[s].start()

    tokens = 2 * rows
    wide_row = iota((tokens, tokens), 0)
    wide_col = iota((tokens, tokens), 1)
    routes = {}

    def routing():
        loads["ids"].wait()
        loads["gates"].wait()
        swaps[2].wait()
        swaps[3].wait()
        tile = onehot(lax.rem(iota((requests, rows), 1), requests) == iota((requests, rows), 0))
        spots = top_count * leaf_len
        own = (
            lax.rem(iota((spots, rows), 0), leaf_len) == iota((spots, rows), 1) // requests
        ).astype(F32)

        def line(values):
            wide = nn_dot(values.astype(BF), tile) * own
            return jnp.sum(wide.reshape(top_count, leaf_len, rows), axis=1)

        id_lines, gate_lines = [], []
        for origin in range(2):
            id_lines.append(line(ids[origin].reshape(spots, requests).astype(F32)))
            gate = gates[origin].reshape(spots, requests)
            gate_hi = gate.astype(BF).astype(F32)
            gate_lines.append(line(gate_hi) + line(gate - gate_hi))
        id_line = jnp.concatenate(id_lines, axis=1)
        gate_line = jnp.concatenate(gate_lines, axis=1)
        expert_id = iota((2 * groups, tokens), 0).astype(F32)
        named = [(expert_id == id_line[k : k + 1, :]).astype(F32) for k in range(top_count)]
        chosen = named[0]
        for k in range(1, top_count):
            chosen = chosen + named[k]
        earlier = onehot((wide_row < wide_col) & (wide_row // rows == wide_col // rows))
        before = nn_dot(chosen.astype(BF), earlier)
        origin_row = (iota((1, tokens), 1) // rows).astype(F32)
        slots = []
        for k in range(top_count):
            one = id_line[k : k + 1, :]
            slot = jnp.sum(named[k] * before, axis=0, keepdims=True)
            group = jnp.floor(one * 0.5)
            spot = jnp.floor(one * 0.25)
            here = (one - 2.0 * group == p.core.astype(F32)) & (
                group - 2.0 * spot == p.half.astype(F32)
            )
            offset = spot - p.spot.astype(F32)
            offset = jnp.where(offset < 0, offset + p.spots, offset)
            slots.append(jnp.where(here, (offset * 2.0 + origin_row) * CAP + slot, -1.0))
        routes["slots"] = slots
        routes["cols"] = jnp.transpose(
            jnp.concatenate(slots + [gate_line, jnp.zeros((4, tokens), F32)], axis=0), (1, 0)
        )

    routing()
    turn = onehot(
        wide_col
        == wide_row // rows * rows
        + lax.rem(wide_row, requests) * leaf_len
        + lax.rem(wide_row, rows) // requests
    )
    cap = sb.shape[2]
    per_chunk2 = 4
    chunk2 = per_chunk2 * cap
    chunks2 = p.spots // per_chunk2

    def d_copy(s, k):
        return to_group(
            sb.at[s, k], xb.at[s, k], d_send.at[s, k], d_recv.at[s, k], p.spot_ahead(k)
        )

    def y_copy(s, k):
        return to_group(
            yb.at[s, k], zb.at[s, k], y_send.at[s, k], y_recv.at[s, k], p.spot_behind(k)
        )

    chunk_index = iota((chunk2, tokens), 0)
    picks = []
    for c in range(chunks2):
        where = (chunk_index + c * chunk2).astype(F32)
        pick = (where == routes["slots"][0]).astype(F32)
        for k in range(1, top_count):
            pick = pick + (where == routes["slots"][k]).astype(F32)
        picks.append(pick.astype(BF))
    x_own = []
    for s in range(PARTS):
        gathers[s].finish()
        x = nn_dot(turn, rows2[s].reshape(tokens, span)).astype(BF)
        x_own.append(x[:rows])
        for c in range(chunks2):
            sb[s, c * per_chunk2 : (c + 1) * per_chunk2] = (
                nn_dot(picks[c], x).astype(BF).reshape(per_chunk2, cap, span)
            )
            each(max(c * per_chunk2, 1), (c + 1) * per_chunk2, lambda k: d_copy(s, k).start())
        xb[s, 0] = sb[s, 0]

    loads["shin"].wait()
    loads["shout"].wait()
    def by_parts(pieces, weights):
        total = nt_dot(pieces[0], weights[:, :span])
        for s in range(1, PARTS):
            total = total + nt_dot(pieces[s], weights[:, s * span : (s + 1) * span])
        return total

    gate = by_parts(x_own, shin.at[0])
    up = by_parts(x_own, shin.at[1])
    hidden = (gate / (1.0 + jnp.exp(-gate)) * up).astype(BF)
    shared = nn_dot(hidden, shout[...])
    own_row = iota((rows, shard_rows), 0)
    own_col = iota((rows, shard_rows), 1)
    mine = (
        lax.rem(own_row, requests) == (shard_rows // leaf_len) * p.t + own_col // leaf_len
    ) & (own_row // requests == lax.rem(own_col, leaf_len))
    shared = shared + exact_dot(mine.astype(F32), residual_mid)
    for s in range(PARTS):
        part2[s, 0] = shared[:, s * span : (s + 1) * span].reshape(part2.shape[2:])
        part2[s, 1] = jnp.zeros(part2.shape[2:], F32)
    all_slots = tokens * 2
    token_lane = iota((tokens, all_slots), 1).astype(F32)
    weights = jnp.zeros((tokens, all_slots), F32)
    for k in range(top_count):
        weights = weights + jnp.where(
            token_lane == routes["cols"][:, k : k + 1],
            routes["cols"][:, top_count + k : top_count + k + 1],
            0.0,
        )
    high = weights.astype(BF)
    gate_hi[...] = high
    gate_lo[...] = (weights - high.astype(F32)).astype(BF)

    loads["ein"].wait()
    loads["eout"].wait()
    swaps[0].wait()
    swaps[1].wait()

    def compute(c):
        first_k, last_k = jnp.maximum(c * per_chunk2, 1), (c + 1) * per_chunk2
        blocks = []
        for s in range(PARTS):
            each(first_k, last_k, lambda k: d_copy(s, k).wait_recv())
            blocks.append(xb[s, pl.ds(c * per_chunk2, per_chunk2)].reshape(chunk2, span))
        gate_part = by_parts(blocks, win.at[0])
        up_part = by_parts(blocks, win.at[1])
        acted = (gate_part / (1.0 + jnp.exp(-gate_part)) * up_part).astype(BF)
        hid[c] = acted
        yb[0, pl.ds(c * per_chunk2, per_chunk2)] = (
            nn_dot(acted, wout[:, :span]).astype(BF).reshape(per_chunk2, cap, span)
        )
        each(first_k, last_k, lambda k: y_copy(0, k).start())

    each(0, chunks2, compute)
    zb[0, 0] = yb[0, 0]
    for s in range(1, PARTS):

        def later(c):
            yb[s, pl.ds(c * per_chunk2, per_chunk2)] = (
                nn_dot(hid[c], wout[:, s * span : (s + 1) * span])
                .astype(BF)
                .reshape(per_chunk2, cap, span)
            )
            each(
                jnp.maximum(c * per_chunk2, 1),
                (c + 1) * per_chunk2,
                lambda k: y_copy(s, k).start(),
            )

        each(0, chunks2, later)
        zb[s, 0] = yb[s, 0]

    sums = []
    for s in range(PARTS):
        for c in range(chunks2):
            each(
                max(c * per_chunk2, 1), (c + 1) * per_chunk2, lambda k: y_copy(s, k).wait_recv()
            )
            block = zb[s, c * per_chunk2 : (c + 1) * per_chunk2].reshape(chunk2, span)
            cut = slice(c * chunk2, (c + 1) * chunk2)
            part2[s] += (
                nn_dot(gate_hi[:, cut], block) + nn_dot(gate_lo[:, cut], block)
            ).reshape(part2.shape[1:])
        sums.append(
            ScatterSum(
                p,
                part2.at[s],
                sib_send2.at[s],
                sib_recv2.at[s],
                rs_send2.at[s],
                rs_recv2.at[s],
                (r2_send.at[s], r2_recv.at[s]),
            )
        )
        sums[s].start()

    loads["moves"].wait()
    swaps[4].wait()
    target = jnp.concatenate([moves[0], moves[1]], axis=1)
    aim = lax.rem(target // requests - p.me + groups, groups)
    spot_tag = (lax.rem(target, requests) + 1).astype(F32)
    pairs = (2 * groups, 2 * requests)
    goes = (iota(pairs, 0) // 2 == aim) & (lax.rem(iota(pairs, 0), 2) == iota(pairs, 1) // requests)
    tags = jnp.sum(jnp.where(goes, spot_tag, 0.0), axis=1, keepdims=True)
    goes = onehot(goes)
    pieces = []
    for s in range(PARTS):
        mixed = sums[s].finish().astype(BF).reshape(2 * requests, span)
        pieces.append(nn_dot(goes, mixed))
    tagged = jnp.concatenate(pieces + [jnp.broadcast_to(tags, (2 * groups, 128))], axis=1)
    for k in range(groups):
        fs[k] = tagged[2 * k : 2 * k + 2].astype(BF)

    def f_copy(k):
        return to_group(fs.at[k], fr.at[k], f_send.at[k], f_recv.at[k], p.ahead(k))

    each(1, groups, lambda k: f_copy(k).start())
    fr[0] = fs[0]
    each(1, groups, lambda k: f_copy(k).wait_recv())
    landed = jnp.concatenate([fr[k].astype(F32) for k in range(groups)], axis=0)
    place_lane = iota((2 * groups, requests), 1).astype(F32) + 1.0
    settle = onehot(landed[:, width : width + 1] == place_lane)
    out[...] = lax.dot_general(
        settle,
        landed[:, :width].astype(BF),
        (((0,), (0,)), ((), ())),
        preferred_element_type=F32,
    ).astype(BF)

    for gather in gathers:
        gather.drain()

    def sent(k):
        m_copy(k).wait_send()
        q_copy(k).wait_send()
        b_copy(k).wait_send()
        f_copy(k).wait_send()

    def sent2(k):
        for s in range(PARTS):
            d_copy(s, k).wait_send()
            y_copy(s, k).wait_send()

    each(1, groups, sent)
    each(1, p.spots, sent2)


def on_device(
    leaf_tokens,
    attn_gain,
    w_query,
    w_key,
    w_value,
    w_out,
    prefix_kv,
    prefix_owner,
    prefix_start,
    prefix_len,
    mlp_gain,
    shared_in,
    shared_out,
    expert_in,
    expert_out,
    expert_ids,
    gate_weights,
    request_of,
):
    groups = lax.axis_size("dp")
    lanes = lax.axis_size("tensor")
    shard_requests, leaf_len, width = leaf_tokens.shape
    requests = prefix_owner.shape[0]
    shard_rows = shard_requests * leaf_len
    local_width = w_query.shape[1]
    units = shared_out.shape[0]
    top_count = expert_ids.shape[2]
    slot_rows = 2 * leaf_len
    payload = local_width + 128
    hbm = pl.BlockSpec(memory_space=pltpu.HBM)
    dma = pltpu.SemaphoreType.DMA
    vm = pltpu.VMEM
    meta = vm((groups, slot_rows, 128), BF)
    exchange = vm((groups, slot_rows, local_width), BF)
    answer = vm((groups, slot_rows, payload), BF)
    table = vm((3, requests), jnp.int32)
    weight = vm(w_query.shape, BF)
    block1 = vm((4, 1, shard_rows, width), BF)
    span = width // PARTS
    tokens = 2 * lanes * shard_rows
    block2 = vm((PARTS, 4, 2, shard_rows, span), BF)
    rows_in = vm((PARTS, groups // 2, 2 * CAP, span), BF)
    gate_table = vm((tokens, groups // 2 * 2 * CAP), BF)
    final = vm((groups, 2, width + 128), BF)
    column = (2, top_count, leaf_len, requests)
    mixed = pl.pallas_call(
        layer_kernel,
        out_shape=jax.ShapeDtypeStruct((requests, width), BF),
        in_specs=[hbm] * 18,
        out_specs=pl.BlockSpec(memory_space=pltpu.VMEM),
        scratch_shapes=[
            vm((shard_rows, width), BF),
            vm((1, width), F32),
            vm((1, width), F32),
            table,
            table,
            table,
            weight,
            weight,
            weight,
            vm(w_out.shape, BF),
            vm(prefix_kv.shape, BF),
            vm(column, jnp.int32),
            vm(column, F32),
            vm((2, 1, requests), jnp.int32),
            vm((2, units, width), BF),
            vm((units, width), BF),
            vm((2, 2 * units, width), BF),
            vm((2 * units, width), BF),
            vm((lanes, shard_rows, width), BF),
            meta,
            meta,
            exchange,
            exchange,
            answer,
            answer,
            vm((1, lanes, shard_rows, width), F32),
            block1,
            block1,
            block1,
            block1,
            vm((PARTS, 2, lanes, shard_rows, span), BF),
            rows_in,
            rows_in,
            vm((4, groups // 8 * 2 * CAP, 2 * units), BF),
            rows_in,
            rows_in,
            gate_table,
            gate_table,
            vm((PARTS, 2, lanes, shard_rows, span), F32),
            block2,
            block2,
            block2,
            block2,
            final,
            final,
            dma((18,)),
            dma((5,)),
            dma((5,)),
            dma((7,)),
            dma((7,)),
            dma((PARTS, 15)),
            dma((PARTS, 15)),
            dma((groups,)),
            dma((groups,)),
            dma((groups,)),
            dma((groups,)),
            dma((groups,)),
            dma((groups,)),
            dma((4,)),
            dma((4,)),
            dma((PARTS, groups // 2)),
            dma((PARTS, groups // 2)),
            dma((PARTS, groups // 2)),
            dma((PARTS, groups // 2)),
            dma((PARTS, 4)),
            dma((PARTS, 4)),
            dma((groups,)),
            dma((groups,)),
        ],
        compiler_params=pltpu.CompilerParams(
            collective_id=0, has_side_effects=True, vmem_limit_bytes=56 << 20
        ),
        name="layer",
    )(
        leaf_tokens.reshape(shard_rows, width),
        attn_gain.reshape(1, width),
        mlp_gain.reshape(1, width),
        jnp.transpose(prefix_owner),
        jnp.transpose(prefix_start),
        jnp.transpose(prefix_len),
        w_query,
        w_key,
        w_value,
        w_out,
        prefix_kv,
        jnp.transpose(expert_ids, (2, 1, 0)),
        jnp.transpose(gate_weights, (2, 1, 0)),
        request_of.reshape(1, requests),
        jnp.transpose(shared_in, (1, 2, 0)),
        shared_out,
        jnp.transpose(expert_in, (0, 2, 3, 1)),
        expert_out,
    )
    return mixed.reshape(requests, 1, width)


def solution(mesh):
    in_specs = (
        P(("dp", "tensor"), None, None),
        P(),
        P(None, "tensor"),
        P(None, "tensor"),
        P(None, "tensor"),
        P("tensor", None),
        P(None, "dp", "tensor"),
        P("dp", None),
        P("dp", None),
        P("dp", None),
        P(),
        P(None, None, "tensor"),
        P("tensor", None),
        P("dp", None, None, "tensor"),
        P("dp", "tensor", None),
        P("dp", None, None),
        P("dp", None, None),
        P("dp"),
    )
    out_specs = P("dp", "tensor", None)
    return jax.shard_map(
        on_device, mesh=mesh, in_specs=in_specs, out_specs=out_specs, check_vma=False
    )
```

```python
import jax
import jax.numpy as jnp
from jax import lax
from jax.experimental import pallas as pl
from jax.experimental.pallas import tpu as pltpu
from jax.sharding import PartitionSpec as P

HEAD_DIM = 128
EPS = 1e-06
ROPE_BASE = 10000.0
CAP = 16
PARTS = 4
FINAL = ((0, 1, 2), (3,))
MESH = pl.DeviceIdType.MESH
BF = jnp.bfloat16
F32 = jnp.float32
NEG = -1e30


def nt_dot(a, b):
    return lax.dot_general(a, b, (((1,), (1,)), ((), ())), preferred_element_type=F32)


def nn_dot(a, b):
    return jnp.dot(a, b, preferred_element_type=F32)


def exact_dot(a, b):
    return jnp.dot(a, b, precision=lax.Precision.HIGHEST, preferred_element_type=F32)


def onehot(mask):
    return mask.astype(F32).astype(BF)


def rms_rows(values, gain):
    mean_square = jnp.mean(values * values, axis=-1, keepdims=True)
    return (values * lax.rsqrt(mean_square + EPS) * gain).astype(BF)


def iota(shape, dim):
    return lax.broadcasted_iota(jnp.int32, shape, dim)


class Place:
    def __init__(self):
        self.groups = lax.axis_size("dp")
        self.me = lax.axis_index("dp")
        self.t = lax.axis_index("tensor")
        self.chip = self.t // 2
        self.core = lax.rem(self.t, 2)
        self.sib = self.chip * 2 + (1 - self.core)
        self.half = lax.rem(self.me, 2)
        self.spot = self.me // 2
        self.spots = self.groups // 2
        self.mirror = self.spot * 2 + (1 - self.half)

    def ahead(self, k):
        return lax.rem(self.me + k, self.groups)

    def behind(self, k):
        return lax.rem(self.me + self.groups - k, self.groups)

    def spot_ahead(self, k):
        return lax.rem(self.spot + k, self.spots) * 2 + self.half

    def spot_behind(self, k):
        return lax.rem(self.spot + self.spots - k, self.spots) * 2 + self.half

    def lane(self, k):
        return lax.rem(self.chip + k, 4) * 2 + self.core


def to_group(src, dst, send, recv, group):
    return pltpu.make_async_remote_copy(
        src, dst, send, recv, device_id={"dp": group}, device_id_type=MESH
    )


def to_lane(src, dst, send, recv, lane):
    return pltpu.make_async_remote_copy(
        src, dst, send, recv, device_id={"tensor": lane}, device_id_type=MESH
    )


def to_both(src, dst, send, recv, group, lane):
    return pltpu.make_async_remote_copy(
        src, dst, send, recv, device_id={"dp": group, "tensor": lane}, device_id_type=MESH
    )


def announce(p):
    barrier = pltpu.get_barrier_semaphore()

    def signal(k, carry):
        pl.semaphore_signal(barrier, inc=1, device_id={"dp": p.ahead(k)}, device_id_type=MESH)
        return carry

    pl.semaphore_signal(barrier, inc=1, device_id={"tensor": p.sib}, device_id_type=MESH)
    for k in range(1, 4):
        pl.semaphore_signal(barrier, inc=1, device_id={"tensor": p.lane(k)}, device_id_type=MESH)
        pl.semaphore_signal(
            barrier,
            inc=1,
            device_id={"dp": p.mirror, "tensor": p.lane(k)},
            device_id_type=MESH,
        )
    lax.fori_loop(1, p.groups, signal, 0)


def await_all(p):
    pl.semaphore_wait(pltpu.get_barrier_semaphore(), p.groups - 1 + 7)


def gather_rows(p, buf, sems, between=None):
    send, recv = sems
    direct = []
    for k in range(1, 4):
        copy = to_lane(buf.at[p.t], buf.at[p.t], send.at[k], recv.at[k], p.lane(k))
        copy.start()
        direct.append(copy)
    passed = [to_lane(buf.at[p.t], buf.at[p.t], send.at[0], recv.at[0], p.sib)]
    passed[0].start()
    if between is not None:
        between()
    for k in range(1, 4):
        direct[k - 1].wait_recv()
        source = p.lane(4 - k)
        copy = to_lane(buf.at[source], buf.at[source], send.at[3 + k], recv.at[3 + k], p.sib)
        copy.start()
        passed.append(copy)
    for copy in direct:
        copy.wait_send()
    for copy in passed:
        copy.wait()


class ColumnGather:
    def __init__(self, p, buf, sems, s):
        self.p, self.buf = p, buf.at[s]
        send, recv = sems
        self.send, self.recv = send.at[s], recv.at[s]
        own, there = self.buf.at[0, p.t], self.buf.at[1, p.t]
        self.direct = [
            to_lane(own, own, self.send.at[k], self.recv.at[k], p.lane(k)) for k in range(1, 4)
        ] + [
            to_both(own, there, self.send.at[4 + k], self.recv.at[4 + k], p.mirror, p.lane(k))
            for k in range(4)
        ]
        self.passed = [to_lane(own, own, self.send.at[0], self.recv.at[0], p.sib)]

    def start(self):
        for copy in self.direct + self.passed:
            copy.start()

    def finish(self):
        p = self.p
        for j in range(7):
            origin, k = (0, j + 1) if j < 3 else (1, j - 3)
            self.direct[j].wait_recv()
            block = self.buf.at[origin, p.lane(4 - k)]
            copy = to_lane(block, block, self.send.at[8 + j], self.recv.at[8 + j], p.sib)
            copy.start()
            self.passed.append(copy)
        for copy in self.passed:
            copy.wait_recv()

    def drain(self):
        for copy in self.direct + self.passed:
            copy.wait_send()


class ScatterSum:
    def __init__(self, p, part, sib_send, sib_recv, rs_send, rs_recv, sems):
        self.p, self.part = p, part
        self.sib_send, self.sib_recv = sib_send, sib_recv
        self.rs_send, self.rs_recv = rs_send, rs_recv
        send, recv = sems
        self.swap = to_lane(sib_send, sib_recv, send.at[0], recv.at[0], p.sib)
        self.copies = [
            to_lane(rs_send.at[k - 1], rs_recv.at[k - 1], send.at[k], recv.at[k], p.lane(k))
            for k in range(1, 4)
        ]

    def start(self):
        p = self.p
        for c in range(4):
            self.sib_send[c] = self.part[:, c * 2 + (1 - p.core)].astype(BF)
        self.swap.start()
        self.swap.wait_recv()
        for k in range(1, 4):
            there = lax.rem(p.chip + k, 4)
            self.rs_send[k - 1] = (
                self.part[:, there * 2 + p.core] + self.sib_recv[there].astype(F32)
            ).astype(BF)
            self.copies[k - 1].start()

    def finish(self):
        p = self.p
        total = self.part[:, p.t] + self.sib_recv[p.chip].astype(F32)
        for k in range(1, 4):
            self.copies[k - 1].wait_recv()
            total = total + self.rs_recv[k - 1].astype(F32)
        self.swap.wait_send()
        for copy in self.copies:
            copy.wait_send()
        return total


def each(first, last, action):
    def step(k, carry):
        action(k)
        return carry

    lax.fori_loop(first, last, step, 0)


def layer_kernel(
    leaf_hbm, gain1_hbm, gain2_hbm, owner_hbm, start_hbm, count_hbm, wq_hbm, wk_hbm, wv_hbm,
    wo_hbm, kv_hbm, ids_hbm, gates_hbm, moves_hbm, shin_hbm, shout_hbm, ein_hbm, eout_hbm,
    out,
    leaf, gain1, gain2, owner, start, count, wq, wk, wv, wo, kv, ids, gates, moves, shin, shout,
    win, wout, xg, qs, qr, bs, br, part1, sib_send1, sib_recv1, rs_send1, rs_recv1,
    rows2, sb, xb, hid, yb, zb, gate_hi, gate_lo, part2, sib_send2, sib_recv2, rs_send2, rs_recv2,
    fs0, fs1, fr0, fr1,
    load_sem, swap_send, swap_recv, g1_send, g1_recv, g2_send, g2_recv,
    q_send, q_recv, b_send, b_recv, r1_send, r1_recv,
    d_send, d_recv, y_send, y_recv, r2_send, r2_recv, f_send, f_recv,
):
    p = Place()
    fs, fr = (fs0, fs1), (fr0, fr1)
    groups = p.groups
    lanes, shard_rows, width = xg.shape
    rows = lanes * shard_rows
    heads = wq.shape[1] // HEAD_DIM
    slot_rows = qs.shape[1]
    leaf_len = slot_rows // 2
    keys = kv.shape[1]
    units = shin.shape[1]
    requests = out.shape[0]
    top_count = ids.shape[1]
    scale = HEAD_DIM**-0.5
    other = 1 - p.core

    loads = {}
    for j, (name, src, dst) in enumerate(
        (
            ("leaf", leaf_hbm, leaf),
            ("gain1", gain1_hbm, gain1),
            ("owner", owner_hbm, owner),
            ("start", start_hbm, start),
            ("count", count_hbm, count),
            ("wq", wq_hbm, wq),
            ("wk", wk_hbm, wk),
            ("wv", wv_hbm, wv),
            ("kv", kv_hbm, kv),
            ("wo", wo_hbm, wo),
            ("gain2", gain2_hbm, gain2),
            ("ids", ids_hbm, ids.at[0]),
            ("gates", gates_hbm, gates.at[0]),
            ("moves", moves_hbm, moves.at[0]),
            ("shin", shin_hbm, shin),
            ("shout", shout_hbm, shout),
            ("ein", ein_hbm.at[p.core], win.at[:, pl.ds(0, units)]),
            ("eout", eout_hbm.at[p.core], wout.at[pl.ds(0, units)]),
        )
    ):
        loads[name] = pltpu.make_async_copy(src, dst, load_sem.at[j])
        loads[name].start()
    announce(p)
    loads["leaf"].wait()
    loads["gain1"].wait()
    residual = leaf[...].astype(F32)
    xg[p.t] = rms_rows(residual, gain1[...])
    swaps = [
        to_lane(
            ein_hbm.at[other], win.at[:, pl.ds(units, units)], swap_send.at[0], swap_recv.at[0], p.sib
        ),
        to_lane(
            eout_hbm.at[other], wout.at[pl.ds(units, units)], swap_send.at[1], swap_recv.at[1], p.sib
        ),
        to_group(ids_hbm, ids.at[1], swap_send.at[2], swap_recv.at[2], p.mirror),
        to_group(gates_hbm, gates.at[1], swap_send.at[3], swap_recv.at[3], p.mirror),
        to_group(moves_hbm, moves.at[1], swap_send.at[4], swap_recv.at[4], p.mirror),
    ]

    lane = iota((rows, HEAD_DIM), 1)
    lane_row = iota((1, rows), 1)
    row_id = iota((rows, rows), 0)
    col_id = iota((rows, rows), 1)
    half = HEAD_DIM // 2
    made = {}

    def tables():
        for name in ("owner", "start", "count"):
            loads[name].wait()
        spread = (iota((requests, rows), 1) // leaf_len == iota((requests, rows), 0)).astype(F32)
        owners = exact_dot(owner[...].astype(F32), spread)
        starts = exact_dot(start[...].astype(F32), spread)
        counts = exact_dot(count[...].astype(F32), spread)
        step = lax.rem(lane_row, leaf_len).astype(F32)
        position = jnp.sum(counts, axis=0, keepdims=True) + step
        first_cols = jnp.transpose(
            jnp.concatenate(
                [owners, starts, counts, position, jnp.zeros((6, rows), F32)], axis=0
            ),
            (1, 0),
        )
        slots = []
        for level in range(3):
            mine = owners[level : level + 1, :]
            second = jnp.zeros((1, rows), F32)
            for above in range(level):
                same = (first_cols[:, above : above + 1] == mine).astype(F32)
                second = jnp.maximum(second, jnp.max(same, axis=0, keepdims=True))
            offset = mine - p.me.astype(F32)
            offset = jnp.where(offset < 0, offset + groups, offset)
            slots.append((offset * 2.0 + second) * leaf_len + step)
        made["slots"] = slots
        made["slot_cols"] = jnp.transpose(
            jnp.concatenate(slots + [jnp.zeros((5, rows), F32)], axis=0), (1, 0)
        )
        frequency = jnp.exp(
            (-2.0 / HEAD_DIM * jnp.log(ROPE_BASE)) * lax.rem(lane, half).astype(F32)
        )
        angles = first_cols[:, 9:10] * frequency
        made["cosine"] = jnp.cos(angles)
        made["sine"] = jnp.where(lane < half, -1.0, 1.0) * jnp.sin(angles)
        made["cols"] = first_cols
        slot_index = iota((groups * slot_rows, rows), 0).astype(F32)
        made["places"] = jnp.concatenate([onehot(slot_index == one) for one in slots], axis=1)
        metas = []
        for level in range(3):
            begin = first_cols[:, 3 + level : 4 + level]
            length = first_cols[:, 6 + level : 7 + level]
            begin_hi = jnp.floor(begin * (1.0 / 32.0))
            length_hi = jnp.floor(length * (1.0 / 32.0))
            meta = jnp.where(lane == 3, length - 32.0 * length_hi, 0.0)
            meta = jnp.where(lane == 2, length_hi, meta)
            meta = jnp.where(lane == 1, begin - 32.0 * begin_hi, meta)
            metas.append(jnp.where(lane == 0, begin_hi, meta).astype(BF))
        made["metas"] = metas

    tables()
    await_all(p)
    gather_rows(p, xg, (g1_send, g1_recv))
    for copy in swaps:
        copy.start()
    cosine, sine = made["cosine"], made["sine"]

    def rotated(values):
        pieces = []
        for h in range(heads):
            one = values[:, h * HEAD_DIM : (h + 1) * HEAD_DIM]
            pieces.append(one * cosine + pltpu.roll(one, half, 1) * sine)
        return jnp.concatenate(pieces, axis=1).astype(BF)

    x = xg[...].reshape(rows, width)
    loads["wq"].wait()
    queries = rotated(nn_dot(x, wq[...]))
    stacked = jnp.concatenate(
        [jnp.concatenate([queries, meta], axis=1) for meta in made["metas"]], axis=0
    )
    qs[...] = nn_dot(made["places"], stacked).astype(BF).reshape(qs.shape)

    def q_copy(k):
        return to_group(qs.at[k], qr.at[k], q_send.at[k], q_recv.at[k], p.ahead(k))

    def b_copy(k):
        return to_group(bs.at[k], br.at[k], b_send.at[k], b_recv.at[k], p.behind(k))

    each(1, groups, lambda k: q_copy(k).start())
    qr[0] = qs[0]

    loads["wk"].wait()
    loads["wv"].wait()
    key_rows = rotated(nn_dot(x, wk[...]))
    leaf_values = nn_dot(x, wv[...]).astype(BF)
    causal = (row_id // leaf_len == col_id // leaf_len) & (col_id <= row_id)
    outs = [[] for _ in range(heads)]
    logs = [[] for _ in range(heads)]
    for h in range(heads):
        span = slice(h * HEAD_DIM, (h + 1) * HEAD_DIM)
        scores = jnp.where(causal, nt_dot(queries[:, span], key_rows[:, span]) * scale, NEG)
        top = jnp.max(scores, axis=1, keepdims=True)
        weights = jnp.exp(scores - top)
        total = jnp.sum(weights, axis=1, keepdims=True)
        outs[h].append(nn_dot(weights.astype(BF), leaf_values[:, span]) / total)
        logs[h].append(top + jnp.log(total))

    loads["kv"].wait()
    per_chunk = 8
    chunk_rows = per_chunk * slot_rows
    key_id = iota((chunk_rows, keys), 1).astype(F32)
    chunk_lane = iota((chunk_rows, HEAD_DIM), 1)

    def owner_chunk(c):
        first_k, last_k = jnp.maximum(c * per_chunk, 1), (c + 1) * per_chunk
        each(first_k, last_k, lambda k: q_copy(k).wait_recv())
        block = qr[pl.ds(c * per_chunk, per_chunk)].reshape(chunk_rows, qs.shape[2])
        meta = block[:, heads * HEAD_DIM :].astype(F32)
        first = meta[:, 0:1] * 32.0 + meta[:, 1:2]
        last = first + meta[:, 2:3] * 32.0 + meta[:, 3:4]
        visible = (key_id >= first) & (key_id < last)
        pieces = []
        tail = jnp.zeros((chunk_rows, HEAD_DIM), F32)
        for h in range(heads):
            span = slice(h * HEAD_DIM, (h + 1) * HEAD_DIM)
            scores = jnp.where(visible, nt_dot(block[:, span], kv[0, :, span]) * scale, NEG)
            top = jnp.max(scores, axis=1, keepdims=True)
            weights = jnp.exp(scores - top)
            total = jnp.sum(weights, axis=1, keepdims=True)
            pieces.append((nn_dot(weights.astype(BF), kv[1, :, span]) / total).astype(BF))
            log_part = top + jnp.log(total)
            log_hi = log_part.astype(BF).astype(F32)
            tail = jnp.where(chunk_lane == 2 * h, log_hi, tail)
            tail = jnp.where(chunk_lane == 2 * h + 1, log_part - log_hi, tail)
        pieces.append(tail.astype(BF))
        bs[pl.ds(c * per_chunk, per_chunk)] = jnp.concatenate(pieces, axis=1).reshape(
            per_chunk, slot_rows, bs.shape[2]
        )
        each(first_k, last_k, lambda k: b_copy(k).start())

    each(0, groups // per_chunk, owner_chunk)
    br[0] = bs[0]
    slot_lane = iota((rows, groups * slot_rows), 1).astype(F32)
    picks = [
        onehot(slot_lane == made["slot_cols"][:, level : level + 1]) for level in range(3)
    ]
    tokens = 2 * rows
    wide_row = iota((tokens, tokens), 0)
    wide_col = iota((tokens, tokens), 1)
    routes = {}

    def routing():
        loads["ids"].wait()
        loads["gates"].wait()
        swaps[2].wait()
        swaps[3].wait()
        tile = onehot(lax.rem(iota((requests, rows), 1), requests) == iota((requests, rows), 0))
        spots = top_count * leaf_len
        own = (
            lax.rem(iota((spots, rows), 0), leaf_len) == iota((spots, rows), 1) // requests
        ).astype(F32)

        def line(values):
            wide = nn_dot(values.astype(BF), tile) * own
            return jnp.sum(wide.reshape(top_count, leaf_len, rows), axis=1)

        id_lines, gate_lines = [], []
        for origin in range(2):
            id_lines.append(line(ids[origin].reshape(spots, requests).astype(F32)))
            gate = gates[origin].reshape(spots, requests)
            gate_hi = gate.astype(BF).astype(F32)
            gate_lines.append(line(gate_hi) + line(gate - gate_hi))
        id_line = jnp.concatenate(id_lines, axis=1)
        gate_line = jnp.concatenate(gate_lines, axis=1)
        expert_id = iota((2 * groups, tokens), 0).astype(F32)
        named = [(expert_id == id_line[k : k + 1, :]).astype(F32) for k in range(top_count)]
        chosen = named[0]
        for k in range(1, top_count):
            chosen = chosen + named[k]
        earlier = onehot((wide_row < wide_col) & (wide_row // rows == wide_col // rows))
        before = nn_dot(chosen.astype(BF), earlier)
        origin_row = (iota((1, tokens), 1) // rows).astype(F32)
        slots = []
        for k in range(top_count):
            one = id_line[k : k + 1, :]
            slot = jnp.sum(named[k] * before, axis=0, keepdims=True)
            group = jnp.floor(one * 0.5)
            spot = jnp.floor(one * 0.25)
            here = (one - 2.0 * group == p.core.astype(F32)) & (
                group - 2.0 * spot == p.half.astype(F32)
            )
            offset = spot - p.spot.astype(F32)
            offset = jnp.where(offset < 0, offset + p.spots, offset)
            slots.append(jnp.where(here, (offset * 2.0 + origin_row) * CAP + slot, -1.0))
        routes["slots"] = slots
        routes["cols"] = jnp.transpose(
            jnp.concatenate(slots + [gate_line, jnp.zeros((4, tokens), F32)], axis=0), (1, 0)
        )

    routing()
    turn = onehot(
        wide_col
        == wide_row // rows * rows
        + lax.rem(wide_row, requests) * leaf_len
        + lax.rem(wide_row, rows) // requests
    )
    cap = sb.shape[2]
    per_chunk2 = 4
    chunk2 = per_chunk2 * cap
    chunks2 = p.spots // per_chunk2

    chunk_index = iota((chunk2, tokens), 0)
    row_picks = []
    for c in range(chunks2):
        where = (chunk_index + c * chunk2).astype(F32)
        pick = (where == routes["slots"][0]).astype(F32)
        for k in range(1, top_count):
            pick = pick + (where == routes["slots"][k]).astype(F32)
        row_picks.append(pick.astype(BF))
    each(1, groups, lambda k: b_copy(k).wait_recv())
    back_all = br[...].reshape(groups * slot_rows, br.shape[2])
    for level in range(3):
        back = nn_dot(picks[level], back_all)
        for h in range(heads):
            base = heads * HEAD_DIM + 2 * h
            outs[h].append(back[:, h * HEAD_DIM : (h + 1) * HEAD_DIM])
            logs[h].append(back[:, base : base + 1] + back[:, base + 1 : base + 2])
    merged = []
    for h in range(heads):
        top = jnp.maximum(jnp.maximum(logs[h][0], logs[h][1]), jnp.maximum(logs[h][2], logs[h][3]))
        scales = [jnp.exp(one - top) for one in logs[h]]
        weighted = scales[0] * outs[h][0]
        for j in range(1, 4):
            weighted = weighted + scales[j] * outs[h][j]
        merged.append(weighted / (scales[0] + scales[1] + scales[2] + scales[3]))
    attended = jnp.concatenate(merged, axis=1).astype(BF)

    loads["wo"].wait()
    part1[...] = nn_dot(attended, wo[...]).reshape(part1.shape)
    summed = ScatterSum(
        p, part1, sib_send1, sib_recv1, rs_send1, rs_recv1, (r1_send, r1_recv)
    )
    summed.start()
    residual_mid = residual + summed.finish()[0]
    loads["gain2"].wait()
    normed = rms_rows(residual_mid, gain2[...])
    span = width // PARTS
    gathers = [ColumnGather(p, rows2, (g2_send, g2_recv), s) for s in range(PARTS)]
    for s in range(PARTS):
        rows2[s, 0, p.t] = normed[:, s * span : (s + 1) * span]
        gathers[s].start()

    def d_copy(s, k):
        return to_group(
            sb.at[s, k], xb.at[s, k], d_send.at[s, k], d_recv.at[s, k], p.spot_ahead(k)
        )

    def y_copy(s, k):
        return to_group(
            yb.at[s, k], zb.at[s, k], y_send.at[s, k], y_recv.at[s, k], p.spot_behind(k)
        )

    x_own = []
    for s in range(PARTS):
        gathers[s].finish()
        x = nn_dot(turn, rows2[s].reshape(tokens, span)).astype(BF)
        x_own.append(x[:rows])
        for c in range(chunks2):
            sb[s, c * per_chunk2 : (c + 1) * per_chunk2] = (
                nn_dot(row_picks[c], x).astype(BF).reshape(per_chunk2, cap, span)
            )
            each(max(c * per_chunk2, 1), (c + 1) * per_chunk2, lambda k: d_copy(s, k).start())
        xb[s, 0] = sb[s, 0]

    loads["shin"].wait()
    loads["shout"].wait()
    def by_parts(pieces, weights):
        total = nt_dot(pieces[0], weights[:, :span])
        for s in range(1, PARTS):
            total = total + nt_dot(pieces[s], weights[:, s * span : (s + 1) * span])
        return total

    gate = by_parts(x_own, shin.at[0])
    up = by_parts(x_own, shin.at[1])
    hidden = (gate / (1.0 + jnp.exp(-gate)) * up).astype(BF)
    shared = nn_dot(hidden, shout[...])
    own_row = iota((rows, shard_rows), 0)
    own_col = iota((rows, shard_rows), 1)
    mine = (
        lax.rem(own_row, requests) == (shard_rows // leaf_len) * p.t + own_col // leaf_len
    ) & (own_row // requests == lax.rem(own_col, leaf_len))
    shared = shared + exact_dot(mine.astype(F32), residual_mid)
    for s in range(PARTS):
        part2[s, 0] = shared[:, s * span : (s + 1) * span].reshape(part2.shape[2:])
        part2[s, 1] = jnp.zeros(part2.shape[2:], F32)
    all_slots = tokens * 2
    token_lane = iota((tokens, all_slots), 1).astype(F32)
    weights = jnp.zeros((tokens, all_slots), F32)
    for k in range(top_count):
        weights = weights + jnp.where(
            token_lane == routes["cols"][:, k : k + 1],
            routes["cols"][:, top_count + k : top_count + k + 1],
            0.0,
        )
    high = weights.astype(BF)
    gate_hi[...] = high
    gate_lo[...] = (weights - high.astype(F32)).astype(BF)

    loads["ein"].wait()
    loads["eout"].wait()
    swaps[0].wait()
    swaps[1].wait()

    def compute(c):
        first_k, last_k = jnp.maximum(c * per_chunk2, 1), (c + 1) * per_chunk2
        blocks = []
        for s in range(PARTS):
            each(first_k, last_k, lambda k: d_copy(s, k).wait_recv())
            blocks.append(xb[s, pl.ds(c * per_chunk2, per_chunk2)].reshape(chunk2, span))
        gate_part = by_parts(blocks, win.at[0])
        up_part = by_parts(blocks, win.at[1])
        acted = (gate_part / (1.0 + jnp.exp(-gate_part)) * up_part).astype(BF)
        hid[c] = acted
        yb[0, pl.ds(c * per_chunk2, per_chunk2)] = (
            nn_dot(acted, wout[:, :span]).astype(BF).reshape(per_chunk2, cap, span)
        )
        each(first_k, last_k, lambda k: y_copy(0, k).start())

    def sent(k):
        q_copy(k).wait_send()
        b_copy(k).wait_send()

    for gather in gathers:
        gather.drain()
    each(1, groups, sent)
    each(0, chunks2, compute)
    zb[0, 0] = yb[0, 0]
    for s in range(1, PARTS):

        def later(c):
            yb[s, pl.ds(c * per_chunk2, per_chunk2)] = (
                nn_dot(hid[c], wout[:, s * span : (s + 1) * span])
                .astype(BF)
                .reshape(per_chunk2, cap, span)
            )
            each(
                jnp.maximum(c * per_chunk2, 1),
                (c + 1) * per_chunk2,
                lambda k: y_copy(s, k).start(),
            )

        each(0, chunks2, later)
        zb[s, 0] = yb[s, 0]

    loads["moves"].wait()
    swaps[4].wait()
    target = jnp.concatenate([moves[0], moves[1]], axis=1)
    aim = lax.rem(target // requests - p.me + groups, groups)
    spot_tag = (lax.rem(target, requests) + 1).astype(F32)
    pairs = (2 * groups, 2 * requests)
    goes = (iota(pairs, 0) // 2 == aim) & (lax.rem(iota(pairs, 0), 2) == iota(pairs, 1) // requests)
    tags = jnp.sum(jnp.where(goes, spot_tag, 0.0), axis=1, keepdims=True)
    tags = jnp.broadcast_to(tags, (2 * groups, 128))
    goes = onehot(goes)

    def f_copy(j, k):
        return to_group(
            fs[j].at[k], fr[j].at[k], f_send.at[j, k], f_recv.at[j, k], p.ahead(k)
        )

    sums = []
    for j, members in enumerate(FINAL):
        for s in members:
            for c in range(chunks2):
                each(
                    max(c * per_chunk2, 1),
                    (c + 1) * per_chunk2,
                    lambda k: y_copy(s, k).wait_recv(),
                )
                block = zb[s, c * per_chunk2 : (c + 1) * per_chunk2].reshape(chunk2, span)
                cut = slice(c * chunk2, (c + 1) * chunk2)
                part2[s] += (
                    nn_dot(gate_hi[:, cut], block) + nn_dot(gate_lo[:, cut], block)
                ).reshape(part2.shape[1:])
            sums.append(
                ScatterSum(
                    p,
                    part2.at[s],
                    sib_send2.at[s],
                    sib_recv2.at[s],
                    rs_send2.at[s],
                    rs_recv2.at[s],
                    (r2_send.at[s], r2_recv.at[s]),
                )
            )
            sums[s].start()
        pieces = []
        for s in members:
            mixed = sums[s].finish().astype(BF).reshape(2 * requests, span)
            pieces.append(nn_dot(goes, mixed))
        if j == 0:
            pieces.append(tags)
        outgoing = jnp.concatenate(pieces, axis=1)
        for k in range(groups):
            fs[j][k] = outgoing[2 * k : 2 * k + 2].astype(BF)
        each(1, groups, lambda k: f_copy(j, k).start())
        fr[j][0] = fs[j][0]

    def sent2(k):
        for s in range(PARTS):
            d_copy(s, k).wait_send()
            y_copy(s, k).wait_send()

    each(1, p.spots, sent2)
    settle = None
    base = 0
    for j, members in enumerate(FINAL):
        each(1, groups, lambda k: f_copy(j, k).wait_recv())
        landed = jnp.concatenate([fr[j][k].astype(F32) for k in range(groups)], axis=0)
        wide = len(members) * span
        if j == 0:
            place_lane = iota((2 * groups, requests), 1).astype(F32) + 1.0
            settle = onehot(landed[:, wide : wide + 1] == place_lane)
        out[:, base : base + wide] = lax.dot_general(
            settle,
            landed[:, :wide].astype(BF),
            (((0,), (0,)), ((), ())),
            preferred_element_type=F32,
        ).astype(BF)
        base += wide
    for j in range(len(FINAL)):
        each(1, groups, lambda k: f_copy(j, k).wait_send())


def on_device(
    leaf_tokens,
    attn_gain,
    w_query,
    w_key,
    w_value,
    w_out,
    prefix_kv,
    prefix_owner,
    prefix_start,
    prefix_len,
    mlp_gain,
    shared_in,
    shared_out,
    expert_in,
    expert_out,
    expert_ids,
    gate_weights,
    request_of,
):
    groups = lax.axis_size("dp")
    lanes = lax.axis_size("tensor")
    shard_requests, leaf_len, width = leaf_tokens.shape
    requests = prefix_owner.shape[0]
    shard_rows = shard_requests * leaf_len
    local_width = w_query.shape[1]
    units = shared_out.shape[0]
    top_count = expert_ids.shape[2]
    slot_rows = 2 * leaf_len
    payload = local_width + 128
    hbm = pl.BlockSpec(memory_space=pltpu.HBM)
    dma = pltpu.SemaphoreType.DMA
    vm = pltpu.VMEM
    exchange = vm((groups, slot_rows, payload), BF)
    table = vm((3, requests), jnp.int32)
    weight = vm(w_query.shape, BF)
    block1 = vm((4, 1, shard_rows, width), BF)
    span = width // PARTS
    tokens = 2 * lanes * shard_rows
    block2 = vm((PARTS, 4, 2, shard_rows, span), BF)
    rows_in = vm((PARTS, groups // 2, 2 * CAP, span), BF)
    gate_table = vm((tokens, groups // 2 * 2 * CAP), BF)
    final0 = vm((groups, 2, len(FINAL[0]) * span + 128), BF)
    final1 = vm((groups, 2, len(FINAL[1]) * span), BF)
    column = (2, top_count, leaf_len, requests)
    mixed = pl.pallas_call(
        layer_kernel,
        out_shape=jax.ShapeDtypeStruct((requests, width), BF),
        in_specs=[hbm] * 18,
        out_specs=pl.BlockSpec(memory_space=pltpu.VMEM),
        scratch_shapes=[
            vm((shard_rows, width), BF),
            vm((1, width), F32),
            vm((1, width), F32),
            table,
            table,
            table,
            weight,
            weight,
            weight,
            vm(w_out.shape, BF),
            vm(prefix_kv.shape, BF),
            vm(column, jnp.int32),
            vm(column, F32),
            vm((2, 1, requests), jnp.int32),
            vm((2, units, width), BF),
            vm((units, width), BF),
            vm((2, 2 * units, width), BF),
            vm((2 * units, width), BF),
            vm((lanes, shard_rows, width), BF),
            exchange,
            exchange,
            exchange,
            exchange,
            vm((1, lanes, shard_rows, width), F32),
            block1,
            block1,
            block1,
            block1,
            vm((PARTS, 2, lanes, shard_rows, span), BF),
            rows_in,
            rows_in,
            vm((4, groups // 8 * 2 * CAP, 2 * units), BF),
            rows_in,
            rows_in,
            gate_table,
            gate_table,
            vm((PARTS, 2, lanes, shard_rows, span), F32),
            block2,
            block2,
            block2,
            block2,
            final0,
            final1,
            final0,
            final1,
            dma((18,)),
            dma((5,)),
            dma((5,)),
            dma((7,)),
            dma((7,)),
            dma((PARTS, 15)),
            dma((PARTS, 15)),
            dma((groups,)),
            dma((groups,)),
            dma((groups,)),
            dma((groups,)),
            dma((4,)),
            dma((4,)),
            dma((PARTS, groups // 2)),
            dma((PARTS, groups // 2)),
            dma((PARTS, groups // 2)),
            dma((PARTS, groups // 2)),
            dma((PARTS, 4)),
            dma((PARTS, 4)),
            dma((2, groups)),
            dma((2, groups)),
        ],
        compiler_params=pltpu.CompilerParams(
            collective_id=0, has_side_effects=True, vmem_limit_bytes=56 << 20
        ),
        name="layer",
    )(
        leaf_tokens.reshape(shard_rows, width),
        attn_gain.reshape(1, width),
        mlp_gain.reshape(1, width),
        jnp.transpose(prefix_owner),
        jnp.transpose(prefix_start),
        jnp.transpose(prefix_len),
        w_query,
        w_key,
        w_value,
        w_out,
        prefix_kv,
        jnp.transpose(expert_ids, (2, 1, 0)),
        jnp.transpose(gate_weights, (2, 1, 0)),
        request_of.reshape(1, requests),
        jnp.transpose(shared_in, (1, 2, 0)),
        shared_out,
        jnp.transpose(expert_in, (0, 2, 3, 1)),
        expert_out,
    )
    return mixed.reshape(requests, 1, width)


def solution(mesh):
    in_specs = (
        P(("dp", "tensor"), None, None),
        P(),
        P(None, "tensor"),
        P(None, "tensor"),
        P(None, "tensor"),
        P("tensor", None),
        P(None, "dp", "tensor"),
        P("dp", None),
        P("dp", None),
        P("dp", None),
        P(),
        P(None, None, "tensor"),
        P("tensor", None),
        P("dp", None, None, "tensor"),
        P("dp", "tensor", None),
        P("dp", None, None),
        P("dp", None, None),
        P("dp"),
    )
    out_specs = P("dp", "tensor", None)
    return jax.shard_map(
        on_device, mesh=mesh, in_specs=in_specs, out_specs=out_specs, check_vma=False
    )
```

```python
import jax
import jax.numpy as jnp
from jax import lax
from jax.experimental import pallas as pl
from jax.experimental.pallas import tpu as pltpu
from jax.sharding import PartitionSpec as P

HEAD_DIM = 128
EPS = 1e-06
ROPE_BASE = 10000.0
CAP = 16
PARTS = 4
FINAL = ((0, 1, 2), (3,))
CHUNK = 4
OWNERS = 16
MESH = pl.DeviceIdType.MESH
BF = jnp.bfloat16
F32 = jnp.float32
NEG = -1e30


def nt_dot(a, b):
    return lax.dot_general(a, b, (((1,), (1,)), ((), ())), preferred_element_type=F32)


def nn_dot(a, b):
    return jnp.dot(a, b, preferred_element_type=F32)


def exact_dot(a, b):
    return jnp.dot(a, b, precision=lax.Precision.HIGHEST, preferred_element_type=F32)


def onehot(mask):
    return mask.astype(F32).astype(BF)


def rms_rows(values, gain):
    mean_square = jnp.mean(values * values, axis=-1, keepdims=True)
    return (values * lax.rsqrt(mean_square + EPS) * gain).astype(BF)


def iota(shape, dim):
    return lax.broadcasted_iota(jnp.int32, shape, dim)


class Place:
    def __init__(self):
        self.groups = lax.axis_size("dp")
        self.me = lax.axis_index("dp")
        self.t = lax.axis_index("tensor")
        self.chip = self.t // 2
        self.core = lax.rem(self.t, 2)
        self.sib = self.chip * 2 + (1 - self.core)
        self.half = lax.rem(self.me, 2)
        self.spot = self.me // 2
        self.spots = self.groups // 2
        self.mirror = self.spot * 2 + (1 - self.half)

    def ahead(self, k):
        return lax.rem(self.me + k, self.groups)

    def behind(self, k):
        return lax.rem(self.me + self.groups - k, self.groups)

    def spot_ahead(self, k):
        return lax.rem(self.spot + k, self.spots) * 2 + self.half

    def spot_behind(self, k):
        return lax.rem(self.spot + self.spots - k, self.spots) * 2 + self.half

    def lane(self, k):
        return lax.rem(self.chip + k, 4) * 2 + self.core


def to_group(src, dst, send, recv, group):
    return pltpu.make_async_remote_copy(
        src, dst, send, recv, device_id={"dp": group}, device_id_type=MESH
    )


def to_lane(src, dst, send, recv, lane):
    return pltpu.make_async_remote_copy(
        src, dst, send, recv, device_id={"tensor": lane}, device_id_type=MESH
    )


def to_both(src, dst, send, recv, group, lane):
    return pltpu.make_async_remote_copy(
        src, dst, send, recv, device_id={"dp": group, "tensor": lane}, device_id_type=MESH
    )


def announce(p):
    barrier = pltpu.get_barrier_semaphore()

    def signal(k, carry):
        pl.semaphore_signal(barrier, inc=1, device_id={"dp": p.ahead(k)}, device_id_type=MESH)
        return carry

    pl.semaphore_signal(barrier, inc=1, device_id={"tensor": p.sib}, device_id_type=MESH)
    for k in range(1, 4):
        pl.semaphore_signal(barrier, inc=1, device_id={"tensor": p.lane(k)}, device_id_type=MESH)
        pl.semaphore_signal(
            barrier,
            inc=1,
            device_id={"dp": p.mirror, "tensor": p.lane(k)},
            device_id_type=MESH,
        )
    lax.fori_loop(1, p.groups, signal, 0)


def await_all(p):
    pl.semaphore_wait(pltpu.get_barrier_semaphore(), p.groups - 1 + 7)


def gather_rows(p, buf, sems, between=None):
    send, recv = sems
    direct = []
    for k in range(1, 4):
        copy = to_lane(buf.at[p.t], buf.at[p.t], send.at[k], recv.at[k], p.lane(k))
        copy.start()
        direct.append(copy)
    passed = [to_lane(buf.at[p.t], buf.at[p.t], send.at[0], recv.at[0], p.sib)]
    passed[0].start()
    if between is not None:
        between()
    for k in range(1, 4):
        direct[k - 1].wait_recv()
        source = p.lane(4 - k)
        copy = to_lane(buf.at[source], buf.at[source], send.at[3 + k], recv.at[3 + k], p.sib)
        copy.start()
        passed.append(copy)
    for copy in direct:
        copy.wait_send()
    for copy in passed:
        copy.wait()


class ColumnGather:
    def __init__(self, p, buf, sems, s):
        self.p, self.buf = p, buf.at[s]
        send, recv = sems
        self.send, self.recv = send.at[s], recv.at[s]
        own, there = self.buf.at[0, p.t], self.buf.at[1, p.t]
        self.direct = [
            to_lane(own, own, self.send.at[k], self.recv.at[k], p.lane(k)) for k in range(1, 4)
        ] + [
            to_both(own, there, self.send.at[4 + k], self.recv.at[4 + k], p.mirror, p.lane(k))
            for k in range(4)
        ]
        self.passed = [to_lane(own, own, self.send.at[0], self.recv.at[0], p.sib)]

    def start(self):
        for copy in self.direct + self.passed:
            copy.start()

    def finish(self):
        p = self.p
        for j in range(7):
            origin, k = (0, j + 1) if j < 3 else (1, j - 3)
            self.direct[j].wait_recv()
            block = self.buf.at[origin, p.lane(4 - k)]
            copy = to_lane(block, block, self.send.at[8 + j], self.recv.at[8 + j], p.sib)
            copy.start()
            self.passed.append(copy)
        for copy in self.passed:
            copy.wait_recv()

    def drain(self):
        for copy in self.direct + self.passed:
            copy.wait_send()


class ScatterSum:
    def __init__(self, p, part, sib_send, sib_recv, rs_send, rs_recv, sems):
        self.p, self.part = p, part
        self.sib_send, self.sib_recv = sib_send, sib_recv
        self.rs_send, self.rs_recv = rs_send, rs_recv
        send, recv = sems
        self.swap = to_lane(sib_send, sib_recv, send.at[0], recv.at[0], p.sib)
        self.copies = [
            to_lane(rs_send.at[k - 1], rs_recv.at[k - 1], send.at[k], recv.at[k], p.lane(k))
            for k in range(1, 4)
        ]

    def start(self):
        p = self.p
        for c in range(4):
            self.sib_send[c] = self.part[:, c * 2 + (1 - p.core)].astype(BF)
        self.swap.start()
        self.swap.wait_recv()
        for k in range(1, 4):
            there = lax.rem(p.chip + k, 4)
            self.rs_send[k - 1] = (
                self.part[:, there * 2 + p.core] + self.sib_recv[there].astype(F32)
            ).astype(BF)
            self.copies[k - 1].start()

    def finish(self):
        p = self.p
        total = self.part[:, p.t] + self.sib_recv[p.chip].astype(F32)
        for k in range(1, 4):
            self.copies[k - 1].wait_recv()
            total = total + self.rs_recv[k - 1].astype(F32)
        self.swap.wait_send()
        for copy in self.copies:
            copy.wait_send()
        return total


def each(first, last, action):
    def step(k, carry):
        action(k)
        return carry

    lax.fori_loop(first, last, step, 0)


def layer_kernel(
    leaf_hbm, gain1_hbm, gain2_hbm, owner_hbm, start_hbm, count_hbm, wq_hbm, wk_hbm, wv_hbm,
    wo_hbm, kv_hbm, ids_hbm, gates_hbm, moves_hbm, shin_hbm, shout_hbm, ein_hbm, eout_hbm,
    out,
    leaf, gain1, gain2, owner, start, count, wq, wk, wv, wo, kv, ids, gates, moves, shin, shout,
    win, wout, xg, qs, qr, bs, br, part1, sib_send1, sib_recv1, rs_send1, rs_recv1,
    rows2, sb, xb, hid, gate_sum, up_sum, yb, zb, gate_hi, gate_lo, part2, sib_send2, sib_recv2, rs_send2, rs_recv2,
    fs0, fs1, fr0, fr1,
    load_sem, swap_send, swap_recv, g1_send, g1_recv, g2_send, g2_recv,
    q_send, q_recv, b_send, b_recv, r1_send, r1_recv,
    d_send, d_recv, y_send, y_recv, r2_send, r2_recv, f_send, f_recv,
):
    p = Place()
    fs, fr = (fs0, fs1), (fr0, fr1)
    groups = p.groups
    lanes, shard_rows, width = xg.shape
    rows = lanes * shard_rows
    heads = wq.shape[1] // HEAD_DIM
    slot_rows = qs.shape[1]
    leaf_len = slot_rows // 2
    keys = kv.shape[1]
    units = shin.shape[1]
    requests = out.shape[0]
    top_count = ids.shape[1]
    scale = HEAD_DIM**-0.5
    other = 1 - p.core

    loads = {}
    for j, (name, src, dst) in enumerate(
        (
            ("leaf", leaf_hbm, leaf),
            ("gain1", gain1_hbm, gain1),
            ("owner", owner_hbm, owner),
            ("start", start_hbm, start),
            ("count", count_hbm, count),
            ("wq", wq_hbm, wq),
            ("wk", wk_hbm, wk),
            ("wv", wv_hbm, wv),
            ("kv", kv_hbm, kv),
            ("wo", wo_hbm, wo),
            ("gain2", gain2_hbm, gain2),
            ("ids", ids_hbm, ids.at[0]),
            ("gates", gates_hbm, gates.at[0]),
            ("moves", moves_hbm, moves.at[0]),
            ("shin", shin_hbm, shin),
            ("shout", shout_hbm, shout),
            ("ein", ein_hbm.at[p.core], win.at[:, pl.ds(0, units)]),
            ("eout", eout_hbm.at[p.core], wout.at[pl.ds(0, units)]),
        )
    ):
        loads[name] = pltpu.make_async_copy(src, dst, load_sem.at[j])
        loads[name].start()
    announce(p)
    loads["leaf"].wait()
    loads["gain1"].wait()
    residual = leaf[...].astype(F32)
    xg[p.t] = rms_rows(residual, gain1[...])
    swaps = [
        to_lane(
            ein_hbm.at[other], win.at[:, pl.ds(units, units)], swap_send.at[0], swap_recv.at[0], p.sib
        ),
        to_lane(
            eout_hbm.at[other], wout.at[pl.ds(units, units)], swap_send.at[1], swap_recv.at[1], p.sib
        ),
        to_group(ids_hbm, ids.at[1], swap_send.at[2], swap_recv.at[2], p.mirror),
        to_group(gates_hbm, gates.at[1], swap_send.at[3], swap_recv.at[3], p.mirror),
        to_group(moves_hbm, moves.at[1], swap_send.at[4], swap_recv.at[4], p.mirror),
    ]

    lane = iota((rows, HEAD_DIM), 1)
    lane_row = iota((1, rows), 1)
    row_id = iota((rows, rows), 0)
    col_id = iota((rows, rows), 1)
    half = HEAD_DIM // 2
    made = {}

    def tables():
        for name in ("owner", "start", "count"):
            loads[name].wait()
        spread = (iota((requests, rows), 1) // leaf_len == iota((requests, rows), 0)).astype(F32)
        owners = exact_dot(owner[...].astype(F32), spread)
        starts = exact_dot(start[...].astype(F32), spread)
        counts = exact_dot(count[...].astype(F32), spread)
        step = lax.rem(lane_row, leaf_len).astype(F32)
        position = jnp.sum(counts, axis=0, keepdims=True) + step
        first_cols = jnp.transpose(
            jnp.concatenate(
                [owners, starts, counts, position, jnp.zeros((6, rows), F32)], axis=0
            ),
            (1, 0),
        )
        slots = []
        for level in range(3):
            mine = owners[level : level + 1, :]
            second = jnp.zeros((1, rows), F32)
            for above in range(level):
                same = (first_cols[:, above : above + 1] == mine).astype(F32)
                second = jnp.maximum(second, jnp.max(same, axis=0, keepdims=True))
            offset = mine - p.me.astype(F32)
            offset = jnp.where(offset < 0, offset + groups, offset)
            slots.append((offset * 2.0 + second) * leaf_len + step)
        made["slots"] = slots
        made["slot_cols"] = jnp.transpose(
            jnp.concatenate(slots + [jnp.zeros((5, rows), F32)], axis=0), (1, 0)
        )
        frequency = jnp.exp(
            (-2.0 / HEAD_DIM * jnp.log(ROPE_BASE)) * lax.rem(lane, half).astype(F32)
        )
        angles = first_cols[:, 9:10] * frequency
        made["cosine"] = jnp.cos(angles)
        made["sine"] = jnp.where(lane < half, -1.0, 1.0) * jnp.sin(angles)
        made["cols"] = first_cols
        slot_index = iota((groups * slot_rows, rows), 0).astype(F32)
        made["places"] = jnp.concatenate([onehot(slot_index == one) for one in slots], axis=1)
        metas = []
        for level in range(3):
            begin = first_cols[:, 3 + level : 4 + level]
            length = first_cols[:, 6 + level : 7 + level]
            begin_hi = jnp.floor(begin * (1.0 / 32.0))
            length_hi = jnp.floor(length * (1.0 / 32.0))
            meta = jnp.where(lane == 3, length - 32.0 * length_hi, 0.0)
            meta = jnp.where(lane == 2, length_hi, meta)
            meta = jnp.where(lane == 1, begin - 32.0 * begin_hi, meta)
            metas.append(jnp.where(lane == 0, begin_hi, meta).astype(BF))
        made["metas"] = metas

    tables()
    await_all(p)
    gather_rows(p, xg, (g1_send, g1_recv))
    for copy in swaps:
        copy.start()
    cosine, sine = made["cosine"], made["sine"]

    def rotated(values):
        pieces = []
        for h in range(heads):
            one = values[:, h * HEAD_DIM : (h + 1) * HEAD_DIM]
            pieces.append(one * cosine + pltpu.roll(one, half, 1) * sine)
        return jnp.concatenate(pieces, axis=1).astype(BF)

    x = xg[...].reshape(rows, width)
    loads["wq"].wait()
    queries = rotated(nn_dot(x, wq[...]))
    stacked = jnp.concatenate(
        [jnp.concatenate([queries, meta], axis=1) for meta in made["metas"]], axis=0
    )
    qs[...] = nn_dot(made["places"], stacked).astype(BF).reshape(qs.shape)

    def q_copy(k):
        return to_group(qs.at[k], qr.at[k], q_send.at[k], q_recv.at[k], p.ahead(k))

    def b_copy(k):
        return to_group(bs.at[k], br.at[k], b_send.at[k], b_recv.at[k], p.behind(k))

    each(1, groups, lambda k: q_copy(k).start())
    qr[0] = qs[0]

    loads["wk"].wait()
    loads["wv"].wait()
    key_rows = rotated(nn_dot(x, wk[...]))
    leaf_values = nn_dot(x, wv[...]).astype(BF)
    causal = (row_id // leaf_len == col_id // leaf_len) & (col_id <= row_id)
    outs = [[] for _ in range(heads)]
    logs = [[] for _ in range(heads)]
    for h in range(heads):
        span = slice(h * HEAD_DIM, (h + 1) * HEAD_DIM)
        scores = jnp.where(causal, nt_dot(queries[:, span], key_rows[:, span]) * scale, NEG)
        top = jnp.max(scores, axis=1, keepdims=True)
        weights = jnp.exp(scores - top)
        total = jnp.sum(weights, axis=1, keepdims=True)
        outs[h].append(nn_dot(weights.astype(BF), leaf_values[:, span]) / total)
        logs[h].append(top + jnp.log(total))

    loads["kv"].wait()
    per_chunk = OWNERS
    chunk_rows = per_chunk * slot_rows
    key_id = iota((chunk_rows, keys), 1).astype(F32)
    chunk_lane = iota((chunk_rows, HEAD_DIM), 1)

    def owner_chunk(c):
        first_k, last_k = jnp.maximum(c * per_chunk, 1), (c + 1) * per_chunk
        each(first_k, last_k, lambda k: q_copy(k).wait_recv())
        block = qr[pl.ds(c * per_chunk, per_chunk)].reshape(chunk_rows, qs.shape[2])
        meta = block[:, heads * HEAD_DIM :].astype(F32)
        first = meta[:, 0:1] * 32.0 + meta[:, 1:2]
        last = first + meta[:, 2:3] * 32.0 + meta[:, 3:4]
        visible = (key_id >= first) & (key_id < last)
        pieces = []
        tail = jnp.zeros((chunk_rows, HEAD_DIM), F32)
        for h in range(heads):
            span = slice(h * HEAD_DIM, (h + 1) * HEAD_DIM)
            scores = jnp.where(visible, nt_dot(block[:, span], kv[0, :, span]) * scale, NEG)
            top = jnp.max(scores, axis=1, keepdims=True)
            weights = jnp.exp(scores - top)
            total = jnp.sum(weights, axis=1, keepdims=True)
            pieces.append((nn_dot(weights.astype(BF), kv[1, :, span]) / total).astype(BF))
            log_part = top + jnp.log(total)
            log_hi = log_part.astype(BF).astype(F32)
            tail = jnp.where(chunk_lane == 2 * h, log_hi, tail)
            tail = jnp.where(chunk_lane == 2 * h + 1, log_part - log_hi, tail)
        pieces.append(tail.astype(BF))
        bs[pl.ds(c * per_chunk, per_chunk)] = jnp.concatenate(pieces, axis=1).reshape(
            per_chunk, slot_rows, bs.shape[2]
        )
        each(first_k, last_k, lambda k: b_copy(k).start())

    each(0, groups // per_chunk, owner_chunk)
    br[0] = bs[0]
    slot_lane = iota((rows, groups * slot_rows), 1).astype(F32)
    picks = [
        onehot(slot_lane == made["slot_cols"][:, level : level + 1]) for level in range(3)
    ]
    tokens = 2 * rows
    wide_row = iota((tokens, tokens), 0)
    wide_col = iota((tokens, tokens), 1)
    routes = {}

    def routing():
        loads["ids"].wait()
        loads["gates"].wait()
        swaps[2].wait()
        swaps[3].wait()
        tile = onehot(lax.rem(iota((requests, rows), 1), requests) == iota((requests, rows), 0))
        spots = top_count * leaf_len
        own = (
            lax.rem(iota((spots, rows), 0), leaf_len) == iota((spots, rows), 1) // requests
        ).astype(F32)

        def line(values):
            wide = nn_dot(values.astype(BF), tile) * own
            return jnp.sum(wide.reshape(top_count, leaf_len, rows), axis=1)

        id_lines, gate_lines = [], []
        for origin in range(2):
            id_lines.append(line(ids[origin].reshape(spots, requests).astype(F32)))
            gate = gates[origin].reshape(spots, requests)
            gate_hi = gate.astype(BF).astype(F32)
            gate_lines.append(line(gate_hi) + line(gate - gate_hi))
        id_line = jnp.concatenate(id_lines, axis=1)
        gate_line = jnp.concatenate(gate_lines, axis=1)
        expert_id = iota((2 * groups, tokens), 0).astype(F32)
        named = [(expert_id == id_line[k : k + 1, :]).astype(F32) for k in range(top_count)]
        chosen = named[0]
        for k in range(1, top_count):
            chosen = chosen + named[k]
        earlier = onehot((wide_row < wide_col) & (wide_row // rows == wide_col // rows))
        before = nn_dot(chosen.astype(BF), earlier)
        origin_row = (iota((1, tokens), 1) // rows).astype(F32)
        slots = []
        for k in range(top_count):
            one = id_line[k : k + 1, :]
            slot = jnp.sum(named[k] * before, axis=0, keepdims=True)
            group = jnp.floor(one * 0.5)
            spot = jnp.floor(one * 0.25)
            here = (one - 2.0 * group == p.core.astype(F32)) & (
                group - 2.0 * spot == p.half.astype(F32)
            )
            offset = spot - p.spot.astype(F32)
            offset = jnp.where(offset < 0, offset + p.spots, offset)
            slots.append(jnp.where(here, (offset * 2.0 + origin_row) * CAP + slot, -1.0))
        routes["slots"] = slots
        routes["cols"] = jnp.transpose(
            jnp.concatenate(slots + [gate_line, jnp.zeros((4, tokens), F32)], axis=0), (1, 0)
        )

    routing()
    turn = onehot(
        wide_col
        == wide_row // rows * rows
        + lax.rem(wide_row, requests) * leaf_len
        + lax.rem(wide_row, rows) // requests
    )
    cap = sb.shape[2]
    per_chunk2 = CHUNK
    chunk2 = per_chunk2 * cap
    chunks2 = p.spots // per_chunk2

    chunk_index = iota((chunk2, tokens), 0)
    row_picks = []
    for c in range(chunks2):
        where = (chunk_index + c * chunk2).astype(F32)
        pick = (where == routes["slots"][0]).astype(F32)
        for k in range(1, top_count):
            pick = pick + (where == routes["slots"][k]).astype(F32)
        row_picks.append(pick.astype(BF))
    each(1, groups, lambda k: b_copy(k).wait_recv())
    back_all = br[...].reshape(groups * slot_rows, br.shape[2])
    for level in range(3):
        back = nn_dot(picks[level], back_all)
        for h in range(heads):
            base = heads * HEAD_DIM + 2 * h
            outs[h].append(back[:, h * HEAD_DIM : (h + 1) * HEAD_DIM])
            logs[h].append(back[:, base : base + 1] + back[:, base + 1 : base + 2])
    merged = []
    for h in range(heads):
        top = jnp.maximum(jnp.maximum(logs[h][0], logs[h][1]), jnp.maximum(logs[h][2], logs[h][3]))
        scales = [jnp.exp(one - top) for one in logs[h]]
        weighted = scales[0] * outs[h][0]
        for j in range(1, 4):
            weighted = weighted + scales[j] * outs[h][j]
        merged.append(weighted / (scales[0] + scales[1] + scales[2] + scales[3]))
    attended = jnp.concatenate(merged, axis=1).astype(BF)

    loads["wo"].wait()
    part1[...] = nn_dot(attended, wo[...]).reshape(part1.shape)
    summed = ScatterSum(
        p, part1, sib_send1, sib_recv1, rs_send1, rs_recv1, (r1_send, r1_recv)
    )
    summed.start()
    residual_mid = residual + summed.finish()[0]
    loads["gain2"].wait()
    normed = rms_rows(residual_mid, gain2[...])
    span = width // PARTS
    gathers = [ColumnGather(p, rows2, (g2_send, g2_recv), s) for s in range(PARTS)]
    for s in range(PARTS):
        rows2[s, 0, p.t] = normed[:, s * span : (s + 1) * span]
        gathers[s].start()

    def d_copy(s, k):
        return to_group(
            sb.at[s, k], xb.at[s, k], d_send.at[s, k], d_recv.at[s, k], p.spot_ahead(k)
        )

    def y_copy(s, k):
        return to_group(
            yb.at[s, k], zb.at[s, k], y_send.at[s, k], y_recv.at[s, k], p.spot_behind(k)
        )

    x_own = []
    for s in range(PARTS):
        gathers[s].finish()
        x = nn_dot(turn, rows2[s].reshape(tokens, span)).astype(BF)
        x_own.append(x[:rows])
        for c in range(chunks2):
            sb[s, c * per_chunk2 : (c + 1) * per_chunk2] = (
                nn_dot(row_picks[c], x).astype(BF).reshape(per_chunk2, cap, span)
            )
            each(max(c * per_chunk2, 1), (c + 1) * per_chunk2, lambda k: d_copy(s, k).start())
        xb[s, 0] = sb[s, 0]

    loads["shin"].wait()
    loads["shout"].wait()
    def by_parts(pieces, weights):
        total = nt_dot(pieces[0], weights[:, :span])
        for s in range(1, PARTS):
            total = total + nt_dot(pieces[s], weights[:, s * span : (s + 1) * span])
        return total

    gate = by_parts(x_own, shin.at[0])
    up = by_parts(x_own, shin.at[1])
    hidden = (gate / (1.0 + jnp.exp(-gate)) * up).astype(BF)
    shared = nn_dot(hidden, shout[...])
    own_row = iota((rows, shard_rows), 0)
    own_col = iota((rows, shard_rows), 1)
    mine = (
        lax.rem(own_row, requests) == (shard_rows // leaf_len) * p.t + own_col // leaf_len
    ) & (own_row // requests == lax.rem(own_col, leaf_len))
    shared = shared + exact_dot(mine.astype(F32), residual_mid)
    for s in range(PARTS):
        part2[s, 0] = shared[:, s * span : (s + 1) * span].reshape(part2.shape[2:])
        part2[s, 1] = jnp.zeros(part2.shape[2:], F32)
    all_slots = tokens * 2
    token_lane = iota((tokens, all_slots), 1).astype(F32)
    weights = jnp.zeros((tokens, all_slots), F32)
    for k in range(top_count):
        weights = weights + jnp.where(
            token_lane == routes["cols"][:, k : k + 1],
            routes["cols"][:, top_count + k : top_count + k + 1],
            0.0,
        )
    high = weights.astype(BF)
    gate_hi[...] = high
    gate_lo[...] = (weights - high.astype(F32)).astype(BF)

    loads["ein"].wait()
    loads["eout"].wait()
    swaps[0].wait()
    swaps[1].wait()

    def product(s, c, weights):
        block = xb[s, pl.ds(c * per_chunk2, per_chunk2)].reshape(chunk2, span)
        return nt_dot(block, weights[:, s * span : (s + 1) * span])

    def arrived(s, c):
        each(
            jnp.maximum(c * per_chunk2, 1),
            (c + 1) * per_chunk2,
            lambda k: d_copy(s, k).wait_recv(),
        )

    for s in range(PARTS - 1):

        def gather_products(c):
            arrived(s, c)
            gate_part = product(s, c, win.at[0])
            up_part = product(s, c, win.at[1])
            if s:
                gate_part = gate_part + gate_sum[c]
                up_part = up_part + up_sum[c]
            gate_sum[c] = gate_part
            up_sum[c] = up_part

        each(0, chunks2, gather_products)

    def compute(c):
        first_k, last_k = jnp.maximum(c * per_chunk2, 1), (c + 1) * per_chunk2
        arrived(PARTS - 1, c)
        gate_part = gate_sum[c] + product(PARTS - 1, c, win.at[0])
        up_part = up_sum[c] + product(PARTS - 1, c, win.at[1])
        acted = (gate_part / (1.0 + jnp.exp(-gate_part)) * up_part).astype(BF)
        hid[c] = acted
        yb[0, pl.ds(c * per_chunk2, per_chunk2)] = (
            nn_dot(acted, wout[:, :span]).astype(BF).reshape(per_chunk2, cap, span)
        )
        each(first_k, last_k, lambda k: y_copy(0, k).start())

    def sent(k):
        q_copy(k).wait_send()
        b_copy(k).wait_send()

    for gather in gathers:
        gather.drain()
    each(1, groups, sent)
    each(0, chunks2, compute)
    zb[0, 0] = yb[0, 0]
    for s in range(1, PARTS):

        def later(c):
            yb[s, pl.ds(c * per_chunk2, per_chunk2)] = (
                nn_dot(hid[c], wout[:, s * span : (s + 1) * span])
                .astype(BF)
                .reshape(per_chunk2, cap, span)
            )
            each(
                jnp.maximum(c * per_chunk2, 1),
                (c + 1) * per_chunk2,
                lambda k: y_copy(s, k).start(),
            )

        each(0, chunks2, later)
        zb[s, 0] = yb[s, 0]

    loads["moves"].wait()
    swaps[4].wait()
    target = jnp.concatenate([moves[0], moves[1]], axis=1)
    aim = lax.rem(target // requests - p.me + groups, groups)
    spot_tag = (lax.rem(target, requests) + 1).astype(F32)
    pairs = (2 * groups, 2 * requests)
    goes = (iota(pairs, 0) // 2 == aim) & (lax.rem(iota(pairs, 0), 2) == iota(pairs, 1) // requests)
    tags = jnp.sum(jnp.where(goes, spot_tag, 0.0), axis=1, keepdims=True)
    tags = jnp.broadcast_to(tags, (2 * groups, 128))
    goes = onehot(goes)

    def f_copy(j, k):
        return to_group(
            fs[j].at[k], fr[j].at[k], f_send.at[j, k], f_recv.at[j, k], p.ahead(k)
        )

    sums = []
    for j, members in enumerate(FINAL):
        for s in members:
            for c in range(chunks2):
                each(
                    max(c * per_chunk2, 1),
                    (c + 1) * per_chunk2,
                    lambda k: y_copy(s, k).wait_recv(),
                )
                block = zb[s, c * per_chunk2 : (c + 1) * per_chunk2].reshape(chunk2, span)
                cut = slice(c * chunk2, (c + 1) * chunk2)
                part2[s] += (
                    nn_dot(gate_hi[:, cut], block) + nn_dot(gate_lo[:, cut], block)
                ).reshape(part2.shape[1:])
            sums.append(
                ScatterSum(
                    p,
                    part2.at[s],
                    sib_send2.at[s],
                    sib_recv2.at[s],
                    rs_send2.at[s],
                    rs_recv2.at[s],
                    (r2_send.at[s], r2_recv.at[s]),
                )
            )
            sums[s].start()
        pieces = []
        for s in members:
            mixed = sums[s].finish().astype(BF).reshape(2 * requests, span)
            pieces.append(nn_dot(goes, mixed))
        if j == 0:
            pieces.append(tags)
        outgoing = jnp.concatenate(pieces, axis=1)
        for k in range(groups):
            fs[j][k] = outgoing[2 * k : 2 * k + 2].astype(BF)
        each(1, groups, lambda k: f_copy(j, k).start())
        fr[j][0] = fs[j][0]

    def sent2(k):
        for s in range(PARTS):
            d_copy(s, k).wait_send()
            y_copy(s, k).wait_send()

    each(1, p.spots, sent2)
    settle = None
    base = 0
    for j, members in enumerate(FINAL):
        each(1, groups, lambda k: f_copy(j, k).wait_recv())
        landed = jnp.concatenate([fr[j][k].astype(F32) for k in range(groups)], axis=0)
        wide = len(members) * span
        if j == 0:
            place_lane = iota((2 * groups, requests), 1).astype(F32) + 1.0
            settle = onehot(landed[:, wide : wide + 1] == place_lane)
        out[:, base : base + wide] = lax.dot_general(
            settle,
            landed[:, :wide].astype(BF),
            (((0,), (0,)), ((), ())),
            preferred_element_type=F32,
        ).astype(BF)
        base += wide
    for j in range(len(FINAL)):
        each(1, groups, lambda k: f_copy(j, k).wait_send())


def on_device(
    leaf_tokens,
    attn_gain,
    w_query,
    w_key,
    w_value,
    w_out,
    prefix_kv,
    prefix_owner,
    prefix_start,
    prefix_len,
    mlp_gain,
    shared_in,
    shared_out,
    expert_in,
    expert_out,
    expert_ids,
    gate_weights,
    request_of,
):
    groups = lax.axis_size("dp")
    lanes = lax.axis_size("tensor")
    shard_requests, leaf_len, width = leaf_tokens.shape
    requests = prefix_owner.shape[0]
    shard_rows = shard_requests * leaf_len
    local_width = w_query.shape[1]
    units = shared_out.shape[0]
    top_count = expert_ids.shape[2]
    slot_rows = 2 * leaf_len
    payload = local_width + 128
    hbm = pl.BlockSpec(memory_space=pltpu.HBM)
    dma = pltpu.SemaphoreType.DMA
    vm = pltpu.VMEM
    exchange = vm((groups, slot_rows, payload), BF)
    table = vm((3, requests), jnp.int32)
    weight = vm(w_query.shape, BF)
    block1 = vm((4, 1, shard_rows, width), BF)
    span = width // PARTS
    tokens = 2 * lanes * shard_rows
    block2 = vm((PARTS, 4, 2, shard_rows, span), BF)
    rows_in = vm((PARTS, groups // 2, 2 * CAP, span), BF)
    chunked = (groups // 2 // CHUNK, CHUNK * 2 * CAP, 2 * units)
    gate_table = vm((tokens, groups // 2 * 2 * CAP), BF)
    final0 = vm((groups, 2, len(FINAL[0]) * span + 128), BF)
    final1 = vm((groups, 2, len(FINAL[1]) * span), BF)
    column = (2, top_count, leaf_len, requests)
    mixed = pl.pallas_call(
        layer_kernel,
        out_shape=jax.ShapeDtypeStruct((requests, width), BF),
        in_specs=[hbm] * 18,
        out_specs=pl.BlockSpec(memory_space=pltpu.VMEM),
        scratch_shapes=[
            vm((shard_rows, width), BF),
            vm((1, width), F32),
            vm((1, width), F32),
            table,
            table,
            table,
            weight,
            weight,
            weight,
            vm(w_out.shape, BF),
            vm(prefix_kv.shape, BF),
            vm(column, jnp.int32),
            vm(column, F32),
            vm((2, 1, requests), jnp.int32),
            vm((2, units, width), BF),
            vm((units, width), BF),
            vm((2, 2 * units, width), BF),
            vm((2 * units, width), BF),
            vm((lanes, shard_rows, width), BF),
            exchange,
            exchange,
            exchange,
            exchange,
            vm((1, lanes, shard_rows, width), F32),
            block1,
            block1,
            block1,
            block1,
            vm((PARTS, 2, lanes, shard_rows, span), BF),
            rows_in,
            rows_in,
            vm(chunked, BF),
            vm(chunked, F32),
            vm(chunked, F32),
            rows_in,
            rows_in,
            gate_table,
            gate_table,
            vm((PARTS, 2, lanes, shard_rows, span), F32),
            block2,
            block2,
            block2,
            block2,
            final0,
            final1,
            final0,
            final1,
            dma((18,)),
            dma((5,)),
            dma((5,)),
            dma((7,)),
            dma((7,)),
            dma((PARTS, 15)),
            dma((PARTS, 15)),
            dma((groups,)),
            dma((groups,)),
            dma((groups,)),
            dma((groups,)),
            dma((4,)),
            dma((4,)),
            dma((PARTS, groups // 2)),
            dma((PARTS, groups // 2)),
            dma((PARTS, groups // 2)),
            dma((PARTS, groups // 2)),
            dma((PARTS, 4)),
            dma((PARTS, 4)),
            dma((2, groups)),
            dma((2, groups)),
        ],
        compiler_params=pltpu.CompilerParams(
            collective_id=0, has_side_effects=True, vmem_limit_bytes=56 << 20
        ),
        name="layer",
    )(
        leaf_tokens.reshape(shard_rows, width),
        attn_gain.reshape(1, width),
        mlp_gain.reshape(1, width),
        jnp.transpose(prefix_owner),
        jnp.transpose(prefix_start),
        jnp.transpose(prefix_len),
        w_query,
        w_key,
        w_value,
        w_out,
        prefix_kv,
        jnp.transpose(expert_ids, (2, 1, 0)),
        jnp.transpose(gate_weights, (2, 1, 0)),
        request_of.reshape(1, requests),
        jnp.transpose(shared_in, (1, 2, 0)),
        shared_out,
        jnp.transpose(expert_in, (0, 2, 3, 1)),
        expert_out,
    )
    return mixed.reshape(requests, 1, width)


def solution(mesh):
    in_specs = (
        P(("dp", "tensor"), None, None),
        P(),
        P(None, "tensor"),
        P(None, "tensor"),
        P(None, "tensor"),
        P("tensor", None),
        P(None, "dp", "tensor"),
        P("dp", None),
        P("dp", None),
        P("dp", None),
        P(),
        P(None, None, "tensor"),
        P("tensor", None),
        P("dp", None, None, "tensor"),
        P("dp", "tensor", None),
        P("dp", None, None),
        P("dp", None, None),
        P("dp"),
    )
    out_specs = P("dp", "tensor", None)
    return jax.shard_map(
        on_device, mesh=mesh, in_specs=in_specs, out_specs=out_specs, check_vma=False
    )
```

```python
import jax
import jax.numpy as jnp
from jax import lax
from jax.experimental import pallas as pl
from jax.experimental.pallas import tpu as pltpu
from jax.sharding import PartitionSpec as P

HEAD_DIM = 128
EPS = 1e-06
ROPE_BASE = 10000.0
CAP = 16
PARTS = 4
FINAL = ((0, 1, 2), (3,))
CHUNK = 4
OWNERS = 16
MESH = pl.DeviceIdType.MESH
BF = jnp.bfloat16
F32 = jnp.float32
NEG = -1e30


def nt_dot(a, b):
    return lax.dot_general(a, b, (((1,), (1,)), ((), ())), preferred_element_type=F32)


def nn_dot(a, b):
    return jnp.dot(a, b, preferred_element_type=F32)


def exact_dot(a, b):
    return jnp.dot(a, b, precision=lax.Precision.HIGHEST, preferred_element_type=F32)


def onehot(mask):
    return mask.astype(F32).astype(BF)


def rms_rows(values, gain):
    mean_square = jnp.mean(values * values, axis=-1, keepdims=True)
    return (values * lax.rsqrt(mean_square + EPS) * gain).astype(BF)


def iota(shape, dim):
    return lax.broadcasted_iota(jnp.int32, shape, dim)


class Place:
    def __init__(self):
        self.groups = lax.axis_size("dp")
        self.me = lax.axis_index("dp")
        self.t = lax.axis_index("tensor")
        self.chip = self.t // 2
        self.core = lax.rem(self.t, 2)
        self.sib = self.chip * 2 + (1 - self.core)
        self.half = lax.rem(self.me, 2)
        self.spot = self.me // 2
        self.spots = self.groups // 2
        self.mirror = self.spot * 2 + (1 - self.half)

    def ahead(self, k):
        return lax.rem(self.me + k, self.groups)

    def behind(self, k):
        return lax.rem(self.me + self.groups - k, self.groups)

    def spot_ahead(self, k):
        return lax.rem(self.spot + k, self.spots) * 2 + self.half

    def spot_behind(self, k):
        return lax.rem(self.spot + self.spots - k, self.spots) * 2 + self.half

    def lane(self, k):
        return lax.rem(self.chip + k, 4) * 2 + self.core


def to_group(src, dst, send, recv, group):
    return pltpu.make_async_remote_copy(
        src, dst, send, recv, device_id={"dp": group}, device_id_type=MESH
    )


def to_lane(src, dst, send, recv, lane):
    return pltpu.make_async_remote_copy(
        src, dst, send, recv, device_id={"tensor": lane}, device_id_type=MESH
    )


def to_both(src, dst, send, recv, group, lane):
    return pltpu.make_async_remote_copy(
        src, dst, send, recv, device_id={"dp": group, "tensor": lane}, device_id_type=MESH
    )


def announce(p):
    barrier = pltpu.get_barrier_semaphore()

    def signal(k, carry):
        pl.semaphore_signal(barrier, inc=1, device_id={"dp": p.ahead(k)}, device_id_type=MESH)
        return carry

    pl.semaphore_signal(barrier, inc=1, device_id={"tensor": p.sib}, device_id_type=MESH)
    for k in range(1, 4):
        pl.semaphore_signal(barrier, inc=1, device_id={"tensor": p.lane(k)}, device_id_type=MESH)
        pl.semaphore_signal(
            barrier,
            inc=1,
            device_id={"dp": p.mirror, "tensor": p.lane(k)},
            device_id_type=MESH,
        )
    lax.fori_loop(1, p.groups, signal, 0)


def await_all(p):
    pl.semaphore_wait(pltpu.get_barrier_semaphore(), p.groups - 1 + 7)


def gather_rows(p, buf, sems, between=None):
    send, recv = sems
    direct = []
    for k in range(1, 4):
        copy = to_lane(buf.at[p.t], buf.at[p.t], send.at[k], recv.at[k], p.lane(k))
        copy.start()
        direct.append(copy)
    passed = [to_lane(buf.at[p.t], buf.at[p.t], send.at[0], recv.at[0], p.sib)]
    passed[0].start()
    if between is not None:
        between()
    for k in range(1, 4):
        direct[k - 1].wait_recv()
        source = p.lane(4 - k)
        copy = to_lane(buf.at[source], buf.at[source], send.at[3 + k], recv.at[3 + k], p.sib)
        copy.start()
        passed.append(copy)
    for copy in direct:
        copy.wait_send()
    for copy in passed:
        copy.wait()


class ColumnGather:
    def __init__(self, p, buf, sems, s):
        self.p, self.buf = p, buf.at[s]
        send, recv = sems
        self.send, self.recv = send.at[s], recv.at[s]
        own, there = self.buf.at[0, p.t], self.buf.at[1, p.t]
        self.direct = [
            to_lane(own, own, self.send.at[k], self.recv.at[k], p.lane(k)) for k in range(1, 4)
        ] + [
            to_both(own, there, self.send.at[4 + k], self.recv.at[4 + k], p.mirror, p.lane(k))
            for k in range(4)
        ]
        self.passed = [to_lane(own, own, self.send.at[0], self.recv.at[0], p.sib)]

    def start(self):
        for copy in self.direct[3:] + self.direct[:3] + self.passed:
            copy.start()

    def finish(self):
        p = self.p
        for j in range(7):
            origin, k = (0, j + 1) if j < 3 else (1, j - 3)
            self.direct[j].wait_recv()
            block = self.buf.at[origin, p.lane(4 - k)]
            copy = to_lane(block, block, self.send.at[8 + j], self.recv.at[8 + j], p.sib)
            copy.start()
            self.passed.append(copy)
        for copy in self.passed:
            copy.wait_recv()

    def drain(self):
        for copy in self.direct + self.passed:
            copy.wait_send()


class ScatterSum:
    def __init__(self, p, part, sib_send, sib_recv, rs_send, rs_recv, sems):
        self.p, self.part = p, part
        self.sib_send, self.sib_recv = sib_send, sib_recv
        self.rs_send, self.rs_recv = rs_send, rs_recv
        send, recv = sems
        self.swap = to_lane(sib_send, sib_recv, send.at[0], recv.at[0], p.sib)
        self.copies = [
            to_lane(rs_send.at[k - 1], rs_recv.at[k - 1], send.at[k], recv.at[k], p.lane(k))
            for k in range(1, 4)
        ]

    def start(self):
        p = self.p
        for c in range(4):
            self.sib_send[c] = self.part[:, c * 2 + (1 - p.core)].astype(BF)
        self.swap.start()
        self.swap.wait_recv()
        for k in range(1, 4):
            there = lax.rem(p.chip + k, 4)
            self.rs_send[k - 1] = (
                self.part[:, there * 2 + p.core] + self.sib_recv[there].astype(F32)
            ).astype(BF)
            self.copies[k - 1].start()

    def finish(self):
        p = self.p
        total = self.part[:, p.t] + self.sib_recv[p.chip].astype(F32)
        for k in range(1, 4):
            self.copies[k - 1].wait_recv()
            total = total + self.rs_recv[k - 1].astype(F32)
        self.swap.wait_send()
        for copy in self.copies:
            copy.wait_send()
        return total


def each(first, last, action):
    def step(k, carry):
        action(k)
        return carry

    lax.fori_loop(first, last, step, 0)


def layer_kernel(
    leaf_hbm, gain1_hbm, gain2_hbm, owner_hbm, start_hbm, count_hbm, wq_hbm, wk_hbm, wv_hbm,
    wo_hbm, kv_hbm, ids_hbm, gates_hbm, moves_hbm, shin_hbm, shout_hbm, ein_hbm, eout_hbm,
    out,
    leaf, gain1, gain2, owner, start, count, wq, wk, wv, wo, kv, ids, gates, moves, shin, shout,
    win, wout, xg, qs, qr, bs, br, part1, sib_send1, sib_recv1, rs_send1, rs_recv1,
    rows2, sb, xb, hid, gate_sum, up_sum, yb, zb, gate_hi, gate_lo, part2, sib_send2, sib_recv2, rs_send2, rs_recv2,
    fs0, fs1, fr0, fr1,
    load_sem, swap_send, swap_recv, g1_send, g1_recv, g2_send, g2_recv,
    q_send, q_recv, b_send, b_recv, r1_send, r1_recv,
    d_send, d_recv, y_send, y_recv, r2_send, r2_recv, f_send, f_recv,
):
    p = Place()
    fs, fr = (fs0, fs1), (fr0, fr1)
    groups = p.groups
    lanes, shard_rows, width = xg.shape
    rows = lanes * shard_rows
    heads = wq.shape[1] // HEAD_DIM
    slot_rows = qs.shape[1]
    leaf_len = slot_rows // 2
    keys = kv.shape[1]
    units = shin.shape[1]
    requests = out.shape[0]
    top_count = ids.shape[1]
    scale = HEAD_DIM**-0.5
    other = 1 - p.core

    loads = {}
    for j, (name, src, dst) in enumerate(
        (
            ("leaf", leaf_hbm, leaf),
            ("gain1", gain1_hbm, gain1),
            ("owner", owner_hbm, owner),
            ("start", start_hbm, start),
            ("count", count_hbm, count),
            ("wq", wq_hbm, wq),
            ("wk", wk_hbm, wk),
            ("wv", wv_hbm, wv),
            ("kv", kv_hbm, kv),
            ("wo", wo_hbm, wo),
            ("gain2", gain2_hbm, gain2),
            ("ids", ids_hbm, ids.at[0]),
            ("gates", gates_hbm, gates.at[0]),
            ("moves", moves_hbm, moves.at[0]),
            ("shin", shin_hbm, shin),
            ("shout", shout_hbm, shout),
            ("ein", ein_hbm.at[p.core], win.at[:, pl.ds(0, units)]),
            ("eout", eout_hbm.at[p.core], wout.at[pl.ds(0, units)]),
        )
    ):
        loads[name] = pltpu.make_async_copy(src, dst, load_sem.at[j])
        loads[name].start()
    announce(p)
    loads["leaf"].wait()
    loads["gain1"].wait()
    residual = leaf[...].astype(F32)
    xg[p.t] = rms_rows(residual, gain1[...])
    swaps = [
        to_lane(
            ein_hbm.at[other], win.at[:, pl.ds(units, units)], swap_send.at[0], swap_recv.at[0], p.sib
        ),
        to_lane(
            eout_hbm.at[other], wout.at[pl.ds(units, units)], swap_send.at[1], swap_recv.at[1], p.sib
        ),
        to_group(ids_hbm, ids.at[1], swap_send.at[2], swap_recv.at[2], p.mirror),
        to_group(gates_hbm, gates.at[1], swap_send.at[3], swap_recv.at[3], p.mirror),
        to_group(moves_hbm, moves.at[1], swap_send.at[4], swap_recv.at[4], p.mirror),
    ]

    lane = iota((rows, HEAD_DIM), 1)
    lane_row = iota((1, rows), 1)
    row_id = iota((rows, rows), 0)
    col_id = iota((rows, rows), 1)
    half = HEAD_DIM // 2
    made = {}

    def tables():
        for name in ("owner", "start", "count"):
            loads[name].wait()
        spread = (iota((requests, rows), 1) // leaf_len == iota((requests, rows), 0)).astype(F32)
        owners = exact_dot(owner[...].astype(F32), spread)
        starts = exact_dot(start[...].astype(F32), spread)
        counts = exact_dot(count[...].astype(F32), spread)
        step = lax.rem(lane_row, leaf_len).astype(F32)
        position = jnp.sum(counts, axis=0, keepdims=True) + step
        first_cols = jnp.transpose(
            jnp.concatenate(
                [owners, starts, counts, position, jnp.zeros((6, rows), F32)], axis=0
            ),
            (1, 0),
        )
        slots = []
        for level in range(3):
            mine = owners[level : level + 1, :]
            second = jnp.zeros((1, rows), F32)
            for above in range(level):
                same = (first_cols[:, above : above + 1] == mine).astype(F32)
                second = jnp.maximum(second, jnp.max(same, axis=0, keepdims=True))
            offset = mine - p.me.astype(F32)
            offset = jnp.where(offset < 0, offset + groups, offset)
            slots.append((offset * 2.0 + second) * leaf_len + step)
        made["slots"] = slots
        made["slot_cols"] = jnp.transpose(
            jnp.concatenate(slots + [jnp.zeros((5, rows), F32)], axis=0), (1, 0)
        )
        frequency = jnp.exp(
            (-2.0 / HEAD_DIM * jnp.log(ROPE_BASE)) * lax.rem(lane, half).astype(F32)
        )
        angles = first_cols[:, 9:10] * frequency
        made["cosine"] = jnp.cos(angles)
        made["sine"] = jnp.where(lane < half, -1.0, 1.0) * jnp.sin(angles)
        made["cols"] = first_cols
        slot_index = iota((groups * slot_rows, rows), 0).astype(F32)
        made["places"] = jnp.concatenate([onehot(slot_index == one) for one in slots], axis=1)
        metas = []
        for level in range(3):
            begin = first_cols[:, 3 + level : 4 + level]
            length = first_cols[:, 6 + level : 7 + level]
            begin_hi = jnp.floor(begin * (1.0 / 32.0))
            length_hi = jnp.floor(length * (1.0 / 32.0))
            meta = jnp.where(lane == 3, length - 32.0 * length_hi, 0.0)
            meta = jnp.where(lane == 2, length_hi, meta)
            meta = jnp.where(lane == 1, begin - 32.0 * begin_hi, meta)
            metas.append(jnp.where(lane == 0, begin_hi, meta).astype(BF))
        made["metas"] = metas

    tables()
    await_all(p)
    gather_rows(p, xg, (g1_send, g1_recv))
    for copy in swaps:
        copy.start()
    cosine, sine = made["cosine"], made["sine"]

    def rotated(values):
        pieces = []
        for h in range(heads):
            one = values[:, h * HEAD_DIM : (h + 1) * HEAD_DIM]
            pieces.append(one * cosine + pltpu.roll(one, half, 1) * sine)
        return jnp.concatenate(pieces, axis=1).astype(BF)

    x = xg[...].reshape(rows, width)
    loads["wq"].wait()
    queries = rotated(nn_dot(x, wq[...]))
    stacked = jnp.concatenate(
        [jnp.concatenate([queries, meta], axis=1) for meta in made["metas"]], axis=0
    )

    def q_copy(k):
        return to_group(qs.at[k], qr.at[k], q_send.at[k], q_recv.at[k], p.ahead(k))

    def b_copy(k):
        return to_group(bs.at[k], br.at[k], b_send.at[k], b_recv.at[k], p.behind(k))

    some = groups // 2
    for part in range(2):
        begin = part * some
        cut = slice(begin * slot_rows, (begin + some) * slot_rows)
        qs[begin : begin + some] = (
            nn_dot(made["places"][cut], stacked).astype(BF).reshape(some, *qs.shape[1:])
        )
        each(max(begin, 1), begin + some, lambda k: q_copy(k).start())
    qr[0] = qs[0]

    loads["wk"].wait()
    loads["wv"].wait()
    key_rows = rotated(nn_dot(x, wk[...]))
    leaf_values = nn_dot(x, wv[...]).astype(BF)
    causal = (row_id // leaf_len == col_id // leaf_len) & (col_id <= row_id)
    outs = [[] for _ in range(heads)]
    logs = [[] for _ in range(heads)]
    for h in range(heads):
        span = slice(h * HEAD_DIM, (h + 1) * HEAD_DIM)
        scores = jnp.where(causal, nt_dot(queries[:, span], key_rows[:, span]) * scale, NEG)
        top = jnp.max(scores, axis=1, keepdims=True)
        weights = jnp.exp(scores - top)
        total = jnp.sum(weights, axis=1, keepdims=True)
        outs[h].append(nn_dot(weights.astype(BF), leaf_values[:, span]) / total)
        logs[h].append(top + jnp.log(total))

    loads["kv"].wait()
    per_chunk = OWNERS
    chunk_rows = per_chunk * slot_rows
    key_id = iota((chunk_rows, keys), 1).astype(F32)
    chunk_lane = iota((chunk_rows, HEAD_DIM), 1)

    def owner_chunk(c):
        first_k, last_k = jnp.maximum(c * per_chunk, 1), (c + 1) * per_chunk
        each(first_k, last_k, lambda k: q_copy(k).wait_recv())
        block = qr[pl.ds(c * per_chunk, per_chunk)].reshape(chunk_rows, qs.shape[2])
        meta = block[:, heads * HEAD_DIM :].astype(F32)
        first = meta[:, 0:1] * 32.0 + meta[:, 1:2]
        last = first + meta[:, 2:3] * 32.0 + meta[:, 3:4]
        visible = (key_id >= first) & (key_id < last)
        pieces = []
        tail = jnp.zeros((chunk_rows, HEAD_DIM), F32)
        for h in range(heads):
            span = slice(h * HEAD_DIM, (h + 1) * HEAD_DIM)
            scores = jnp.where(visible, nt_dot(block[:, span], kv[0, :, span]) * scale, NEG)
            top = jnp.max(scores, axis=1, keepdims=True)
            weights = jnp.exp(scores - top)
            total = jnp.sum(weights, axis=1, keepdims=True)
            pieces.append((nn_dot(weights.astype(BF), kv[1, :, span]) / total).astype(BF))
            log_part = top + jnp.log(total)
            log_hi = log_part.astype(BF).astype(F32)
            tail = jnp.where(chunk_lane == 2 * h, log_hi, tail)
            tail = jnp.where(chunk_lane == 2 * h + 1, log_part - log_hi, tail)
        pieces.append(tail.astype(BF))
        bs[pl.ds(c * per_chunk, per_chunk)] = jnp.concatenate(pieces, axis=1).reshape(
            per_chunk, slot_rows, bs.shape[2]
        )
        each(first_k, last_k, lambda k: b_copy(k).start())

    each(0, groups // per_chunk, owner_chunk)
    br[0] = bs[0]
    slot_lane = iota((rows, groups * slot_rows), 1).astype(F32)
    picks = [
        onehot(slot_lane == made["slot_cols"][:, level : level + 1]) for level in range(3)
    ]
    tokens = 2 * rows
    wide_row = iota((tokens, tokens), 0)
    wide_col = iota((tokens, tokens), 1)
    routes = {}

    def routing():
        loads["ids"].wait()
        loads["gates"].wait()
        swaps[2].wait()
        swaps[3].wait()
        tile = onehot(lax.rem(iota((requests, rows), 1), requests) == iota((requests, rows), 0))
        spots = top_count * leaf_len
        own = (
            lax.rem(iota((spots, rows), 0), leaf_len) == iota((spots, rows), 1) // requests
        ).astype(F32)

        def line(values):
            wide = nn_dot(values.astype(BF), tile) * own
            return jnp.sum(wide.reshape(top_count, leaf_len, rows), axis=1)

        id_lines, gate_lines = [], []
        for origin in range(2):
            id_lines.append(line(ids[origin].reshape(spots, requests).astype(F32)))
            gate = gates[origin].reshape(spots, requests)
            gate_hi = gate.astype(BF).astype(F32)
            gate_lines.append(line(gate_hi) + line(gate - gate_hi))
        id_line = jnp.concatenate(id_lines, axis=1)
        gate_line = jnp.concatenate(gate_lines, axis=1)
        expert_id = iota((2 * groups, tokens), 0).astype(F32)
        named = [(expert_id == id_line[k : k + 1, :]).astype(F32) for k in range(top_count)]
        chosen = named[0]
        for k in range(1, top_count):
            chosen = chosen + named[k]
        earlier = onehot((wide_row < wide_col) & (wide_row // rows == wide_col // rows))
        before = nn_dot(chosen.astype(BF), earlier)
        origin_row = (iota((1, tokens), 1) // rows).astype(F32)
        slots = []
        for k in range(top_count):
            one = id_line[k : k + 1, :]
            slot = jnp.sum(named[k] * before, axis=0, keepdims=True)
            group = jnp.floor(one * 0.5)
            spot = jnp.floor(one * 0.25)
            here = (one - 2.0 * group == p.core.astype(F32)) & (
                group - 2.0 * spot == p.half.astype(F32)
            )
            offset = spot - p.spot.astype(F32)
            offset = jnp.where(offset < 0, offset + p.spots, offset)
            slots.append(jnp.where(here, (offset * 2.0 + origin_row) * CAP + slot, -1.0))
        routes["slots"] = slots
        routes["cols"] = jnp.transpose(
            jnp.concatenate(slots + [gate_line, jnp.zeros((4, tokens), F32)], axis=0), (1, 0)
        )

    routing()
    turn = onehot(
        wide_col
        == wide_row // rows * rows
        + lax.rem(wide_row, requests) * leaf_len
        + lax.rem(wide_row, rows) // requests
    )
    cap = sb.shape[2]
    per_chunk2 = CHUNK
    chunk2 = per_chunk2 * cap
    chunks2 = p.spots // per_chunk2

    chunk_index = iota((chunk2, tokens), 0)
    row_picks = []
    for c in range(chunks2):
        where = (chunk_index + c * chunk2).astype(F32)
        pick = (where == routes["slots"][0]).astype(F32)
        for k in range(1, top_count):
            pick = pick + (where == routes["slots"][k]).astype(F32)
        row_picks.append(nn_dot(pick.astype(BF), turn).astype(BF))
    each(1, groups, lambda k: b_copy(k).wait_recv())
    back_all = br[...].reshape(groups * slot_rows, br.shape[2])
    for level in range(3):
        back = nn_dot(picks[level], back_all)
        for h in range(heads):
            base = heads * HEAD_DIM + 2 * h
            outs[h].append(back[:, h * HEAD_DIM : (h + 1) * HEAD_DIM])
            logs[h].append(back[:, base : base + 1] + back[:, base + 1 : base + 2])
    merged = []
    for h in range(heads):
        top = jnp.maximum(jnp.maximum(logs[h][0], logs[h][1]), jnp.maximum(logs[h][2], logs[h][3]))
        scales = [jnp.exp(one - top) for one in logs[h]]
        weighted = scales[0] * outs[h][0]
        for j in range(1, 4):
            weighted = weighted + scales[j] * outs[h][j]
        merged.append(weighted / (scales[0] + scales[1] + scales[2] + scales[3]))
    attended = jnp.concatenate(merged, axis=1).astype(BF)

    loads["wo"].wait()
    part1[...] = nn_dot(attended, wo[...]).reshape(part1.shape)
    summed = ScatterSum(
        p, part1, sib_send1, sib_recv1, rs_send1, rs_recv1, (r1_send, r1_recv)
    )
    summed.start()
    residual_mid = residual + summed.finish()[0]
    loads["gain2"].wait()
    normed = rms_rows(residual_mid, gain2[...])
    span = width // PARTS
    gathers = [ColumnGather(p, rows2, (g2_send, g2_recv), s) for s in range(PARTS)]
    for s in range(PARTS):
        rows2[s, 0, p.t] = normed[:, s * span : (s + 1) * span]
        gathers[s].start()

    def d_copy(s, k):
        return to_group(
            sb.at[s, k], xb.at[s, k], d_send.at[s, k], d_recv.at[s, k], p.spot_ahead(k)
        )

    def y_copy(s, k):
        return to_group(
            yb.at[s, k], zb.at[s, k], y_send.at[s, k], y_recv.at[s, k], p.spot_behind(k)
        )

    x_own = []
    for s in range(PARTS):
        gathers[s].finish()
        x = rows2[s].reshape(tokens, span)
        for c in range(chunks2):
            sb[s, c * per_chunk2 : (c + 1) * per_chunk2] = (
                nn_dot(row_picks[c], x).astype(BF).reshape(per_chunk2, cap, span)
            )
            each(max(c * per_chunk2, 1), (c + 1) * per_chunk2, lambda k: d_copy(s, k).start())
        xb[s, 0] = sb[s, 0]
        x_own.append(
            nn_dot(turn[:rows, :rows], rows2[s, 0].reshape(rows, span)).astype(BF)
        )

    loads["shin"].wait()
    loads["shout"].wait()
    def by_parts(pieces, weights):
        total = nt_dot(pieces[0], weights[:, :span])
        for s in range(1, PARTS):
            total = total + nt_dot(pieces[s], weights[:, s * span : (s + 1) * span])
        return total

    gate = by_parts(x_own, shin.at[0])
    up = by_parts(x_own, shin.at[1])
    hidden = (gate / (1.0 + jnp.exp(-gate)) * up).astype(BF)
    shared = nn_dot(hidden, shout[...])
    own_row = iota((rows, shard_rows), 0)
    own_col = iota((rows, shard_rows), 1)
    mine = (
        lax.rem(own_row, requests) == (shard_rows // leaf_len) * p.t + own_col // leaf_len
    ) & (own_row // requests == lax.rem(own_col, leaf_len))
    shared = shared + exact_dot(mine.astype(F32), residual_mid)
    for s in range(PARTS):
        part2[s, 0] = shared[:, s * span : (s + 1) * span].reshape(part2.shape[2:])
        part2[s, 1] = jnp.zeros(part2.shape[2:], F32)
    all_slots = tokens * 2
    token_lane = iota((tokens, all_slots), 1).astype(F32)
    weights = jnp.zeros((tokens, all_slots), F32)
    for k in range(top_count):
        weights = weights + jnp.where(
            token_lane == routes["cols"][:, k : k + 1],
            routes["cols"][:, top_count + k : top_count + k + 1],
            0.0,
        )
    high = weights.astype(BF)
    gate_hi[...] = high
    gate_lo[...] = (weights - high.astype(F32)).astype(BF)

    loads["ein"].wait()
    loads["eout"].wait()
    swaps[0].wait()
    swaps[1].wait()

    def product(s, c, weights):
        block = xb[s, pl.ds(c * per_chunk2, per_chunk2)].reshape(chunk2, span)
        return nt_dot(block, weights[:, s * span : (s + 1) * span])

    def arrived(s, c):
        each(
            jnp.maximum(c * per_chunk2, 1),
            (c + 1) * per_chunk2,
            lambda k: d_copy(s, k).wait_recv(),
        )

    for s in range(PARTS - 1):

        def gather_products(c):
            arrived(s, c)
            gate_part = product(s, c, win.at[0])
            up_part = product(s, c, win.at[1])
            if s:
                gate_part = gate_part + gate_sum[c]
                up_part = up_part + up_sum[c]
            gate_sum[c] = gate_part
            up_sum[c] = up_part

        each(0, chunks2, gather_products)

    def compute(c):
        first_k, last_k = jnp.maximum(c * per_chunk2, 1), (c + 1) * per_chunk2
        arrived(PARTS - 1, c)
        gate_part = gate_sum[c] + product(PARTS - 1, c, win.at[0])
        up_part = up_sum[c] + product(PARTS - 1, c, win.at[1])
        acted = (gate_part / (1.0 + jnp.exp(-gate_part)) * up_part).astype(BF)
        hid[c] = acted
        yb[0, pl.ds(c * per_chunk2, per_chunk2)] = (
            nn_dot(acted, wout[:, :span]).astype(BF).reshape(per_chunk2, cap, span)
        )
        each(first_k, last_k, lambda k: y_copy(0, k).start())

    def sent(k):
        q_copy(k).wait_send()
        b_copy(k).wait_send()

    for gather in gathers:
        gather.drain()
    each(1, groups, sent)
    each(0, chunks2, compute)
    zb[0, 0] = yb[0, 0]
    for s in range(1, PARTS):

        def later(c):
            yb[s, pl.ds(c * per_chunk2, per_chunk2)] = (
                nn_dot(hid[c], wout[:, s * span : (s + 1) * span])
                .astype(BF)
                .reshape(per_chunk2, cap, span)
            )
            each(
                jnp.maximum(c * per_chunk2, 1),
                (c + 1) * per_chunk2,
                lambda k: y_copy(s, k).start(),
            )

        each(0, chunks2, later)
        zb[s, 0] = yb[s, 0]

    loads["moves"].wait()
    swaps[4].wait()
    target = jnp.concatenate([moves[0], moves[1]], axis=1)
    aim = lax.rem(target // requests - p.me + groups, groups)
    spot_tag = (lax.rem(target, requests) + 1).astype(F32)
    pairs = (2 * groups, 2 * requests)
    goes = (iota(pairs, 0) // 2 == aim) & (lax.rem(iota(pairs, 0), 2) == iota(pairs, 1) // requests)
    tags = jnp.sum(jnp.where(goes, spot_tag, 0.0), axis=1, keepdims=True)
    tags = jnp.broadcast_to(tags, (2 * groups, 128))
    goes = onehot(goes)

    def f_copy(j, k):
        return to_group(
            fs[j].at[k], fr[j].at[k], f_send.at[j, k], f_recv.at[j, k], p.ahead(k)
        )

    sums = []
    for j, members in enumerate(FINAL):
        for s in members:
            for c in range(chunks2):
                each(
                    max(c * per_chunk2, 1),
                    (c + 1) * per_chunk2,
                    lambda k: y_copy(s, k).wait_recv(),
                )
                block = zb[s, c * per_chunk2 : (c + 1) * per_chunk2].reshape(chunk2, span)
                cut = slice(c * chunk2, (c + 1) * chunk2)
                part2[s] += (
                    nn_dot(gate_hi[:, cut], block) + nn_dot(gate_lo[:, cut], block)
                ).reshape(part2.shape[1:])
            sums.append(
                ScatterSum(
                    p,
                    part2.at[s],
                    sib_send2.at[s],
                    sib_recv2.at[s],
                    rs_send2.at[s],
                    rs_recv2.at[s],
                    (r2_send.at[s], r2_recv.at[s]),
                )
            )
            sums[s].start()
        pieces = []
        for s in members:
            mixed = sums[s].finish().astype(BF).reshape(2 * requests, span)
            pieces.append(nn_dot(goes, mixed))
        if j == 0:
            pieces.append(tags)
        outgoing = jnp.concatenate(pieces, axis=1)
        for k in range(groups):
            fs[j][k] = outgoing[2 * k : 2 * k + 2].astype(BF)
        each(1, groups, lambda k: f_copy(j, k).start())
        fr[j][0] = fs[j][0]

    def sent2(k):
        for s in range(PARTS):
            d_copy(s, k).wait_send()
            y_copy(s, k).wait_send()

    each(1, p.spots, sent2)
    settle = None
    base = 0
    for j, members in enumerate(FINAL):
        each(1, groups, lambda k: f_copy(j, k).wait_recv())
        landed = jnp.concatenate([fr[j][k].astype(F32) for k in range(groups)], axis=0)
        wide = len(members) * span
        if j == 0:
            place_lane = iota((2 * groups, requests), 1).astype(F32) + 1.0
            settle = onehot(landed[:, wide : wide + 1] == place_lane)
        out[:, base : base + wide] = lax.dot_general(
            settle,
            landed[:, :wide].astype(BF),
            (((0,), (0,)), ((), ())),
            preferred_element_type=F32,
        ).astype(BF)
        base += wide
    for j in range(len(FINAL)):
        each(1, groups, lambda k: f_copy(j, k).wait_send())


def on_device(
    leaf_tokens,
    attn_gain,
    w_query,
    w_key,
    w_value,
    w_out,
    prefix_kv,
    prefix_owner,
    prefix_start,
    prefix_len,
    mlp_gain,
    shared_in,
    shared_out,
    expert_in,
    expert_out,
    expert_ids,
    gate_weights,
    request_of,
):
    groups = lax.axis_size("dp")
    lanes = lax.axis_size("tensor")
    shard_requests, leaf_len, width = leaf_tokens.shape
    requests = prefix_owner.shape[0]
    shard_rows = shard_requests * leaf_len
    local_width = w_query.shape[1]
    units = shared_out.shape[0]
    top_count = expert_ids.shape[2]
    slot_rows = 2 * leaf_len
    payload = local_width + 128
    hbm = pl.BlockSpec(memory_space=pltpu.HBM)
    dma = pltpu.SemaphoreType.DMA
    vm = pltpu.VMEM
    exchange = vm((groups, slot_rows, payload), BF)
    table = vm((3, requests), jnp.int32)
    weight = vm(w_query.shape, BF)
    block1 = vm((4, 1, shard_rows, width), BF)
    span = width // PARTS
    tokens = 2 * lanes * shard_rows
    block2 = vm((PARTS, 4, 2, shard_rows, span), BF)
    rows_in = vm((PARTS, groups // 2, 2 * CAP, span), BF)
    chunked = (groups // 2 // CHUNK, CHUNK * 2 * CAP, 2 * units)
    gate_table = vm((tokens, groups // 2 * 2 * CAP), BF)
    final0 = vm((groups, 2, len(FINAL[0]) * span + 128), BF)
    final1 = vm((groups, 2, len(FINAL[1]) * span), BF)
    column = (2, top_count, leaf_len, requests)
    mixed = pl.pallas_call(
        layer_kernel,
        out_shape=jax.ShapeDtypeStruct((requests, width), BF),
        in_specs=[hbm] * 18,
        out_specs=pl.BlockSpec(memory_space=pltpu.VMEM),
        scratch_shapes=[
            vm((shard_rows, width), BF),
            vm((1, width), F32),
            vm((1, width), F32),
            table,
            table,
            table,
            weight,
            weight,
            weight,
            vm(w_out.shape, BF),
            vm(prefix_kv.shape, BF),
            vm(column, jnp.int32),
            vm(column, F32),
            vm((2, 1, requests), jnp.int32),
            vm((2, units, width), BF),
            vm((units, width), BF),
            vm((2, 2 * units, width), BF),
            vm((2 * units, width), BF),
            vm((lanes, shard_rows, width), BF),
            exchange,
            exchange,
            exchange,
            exchange,
            vm((1, lanes, shard_rows, width), F32),
            block1,
            block1,
            block1,
            block1,
            vm((PARTS, 2, lanes, shard_rows, span), BF),
            rows_in,
            rows_in,
            vm(chunked, BF),
            vm(chunked, F32),
            vm(chunked, F32),
            rows_in,
            rows_in,
            gate_table,
            gate_table,
            vm((PARTS, 2, lanes, shard_rows, span), F32),
            block2,
            block2,
            block2,
            block2,
            final0,
            final1,
            final0,
            final1,
            dma((18,)),
            dma((5,)),
            dma((5,)),
            dma((7,)),
            dma((7,)),
            dma((PARTS, 15)),
            dma((PARTS, 15)),
            dma((groups,)),
            dma((groups,)),
            dma((groups,)),
            dma((groups,)),
            dma((4,)),
            dma((4,)),
            dma((PARTS, groups // 2)),
            dma((PARTS, groups // 2)),
            dma((PARTS, groups // 2)),
            dma((PARTS, groups // 2)),
            dma((PARTS, 4)),
            dma((PARTS, 4)),
            dma((2, groups)),
            dma((2, groups)),
        ],
        compiler_params=pltpu.CompilerParams(
            collective_id=0, has_side_effects=True, vmem_limit_bytes=56 << 20
        ),
        name="layer",
    )(
        leaf_tokens.reshape(shard_rows, width),
        attn_gain.reshape(1, width),
        mlp_gain.reshape(1, width),
        jnp.transpose(prefix_owner),
        jnp.transpose(prefix_start),
        jnp.transpose(prefix_len),
        w_query,
        w_key,
        w_value,
        w_out,
        prefix_kv,
        jnp.transpose(expert_ids, (2, 1, 0)),
        jnp.transpose(gate_weights, (2, 1, 0)),
        request_of.reshape(1, requests),
        jnp.transpose(shared_in, (1, 2, 0)),
        shared_out,
        jnp.transpose(expert_in, (0, 2, 3, 1)),
        expert_out,
    )
    return mixed.reshape(requests, 1, width)


def solution(mesh):
    in_specs = (
        P(("dp", "tensor"), None, None),
        P(),
        P(None, "tensor"),
        P(None, "tensor"),
        P(None, "tensor"),
        P("tensor", None),
        P(None, "dp", "tensor"),
        P("dp", None),
        P("dp", None),
        P("dp", None),
        P(),
        P(None, None, "tensor"),
        P("tensor", None),
        P("dp", None, None, "tensor"),
        P("dp", "tensor", None),
        P("dp", None, None),
        P("dp", None, None),
        P("dp"),
    )
    out_specs = P("dp", "tensor", None)
    return jax.shard_map(
        on_device, mesh=mesh, in_specs=in_specs, out_specs=out_specs, check_vma=False
    )
```
